32 devices in a mesh: dp: 8 (over y, x, core), ctx: 4 (over z).
Axes of the slice: x: 2, y: 2, z: 4, core: 2. Of those that a mesh axis runs over, the one named last changes fastest.
Arguments:
- tokens: bfloat16 [16, 1024, 768], P('dp', 'ctx'), may hold values from -6 to 6
- segments: int32 [16, 1024], P('dp', 'ctx'), may hold values from 0 to 16, as said below
- positions: int32 [16, 1024], P('dp', 'ctx'), may hold values from 0 to 799, as said below
- qkv_weight: bfloat16 [1769472], P(('dp', 'ctx')), may hold values from -0.21875 to 0.21875
- out_weight: bfloat16 [589824], P(('dp', 'ctx')), may hold values from -1.75 to 1.75
- gate_up_weight: bfloat16 [4718592], P(('dp', 'ctx')), may hold values from -0.21875 to 0.21875
- down_weight: bfloat16 [2359296], P(('dp', 'ctx')), may hold values from -0.109375 to 0.109375
- first_gain: bfloat16 [768], P(('dp', 'ctx')), may hold values from 0.099609375 to 1.8984375
- first_bias: bfloat16 [768], P(('dp', 'ctx')), may hold values from -3 to 3
- second_gain: bfloat16 [768], P(('dp', 'ctx')), may hold values from 0.099609375 to 1.8984375
- second_bias: bfloat16 [768], P(('dp', 'ctx')), may hold values from -3 to 3
- output_grad: bfloat16 [16, 1024, 768], P('dp', 'ctx'), may hold values from -6 to 6
Outputs:
- output: bfloat16 [16, 1024, 768], P('dp', 'ctx')
- input_grad: float32 [16, 1024, 768], P('dp', 'ctx')
- qkv_weight_grad: float32 [1769472], P(('dp', 'ctx'))
- out_weight_grad: float32 [589824], P(('dp', 'ctx'))
- gate_up_weight_grad: float32 [4718592], P(('dp', 'ctx'))
- down_weight_grad: float32 [2359296], P(('dp', 'ctx'))
- first_gain_grad: float32 [768], P(('dp', 'ctx'))
- first_bias_grad: float32 [768], P(('dp', 'ctx'))
- second_gain_grad: float32 [768], P(('dp', 'ctx'))
- second_bias_grad: float32 [768], P(('dp', 'ctx'))
The draws below stay inside these ranges and needn't reach their ends.
Inputs may be any that keep to these rules, and one draw needn't show every extreme that they name: `segments`: each sequence is packed with whole documents of 60 to 800 tokens; a document's tokens carry one id, ids count up from 0 along the sequence; every draw holds a document of exactly 800 tokens and a sequence with the most documents. `positions`: each token's place within its document, counting from 0 at the document's first token.
All inputs are finite; a program needn't handle non-finite values.
Results may differ from the reference program's by a relative error of at most 0.015.
Values may be sent and summed in bfloat16 or wider, within the bound.
No kernel may reach another device: no remote copies, remote signals or barrier semaphores. Data moves between devices by JAX's collectives and lax.ppermute only.
A program may use at most 192 MiB of HBM per device.

```python
import math
import jax
import jax.numpy as jnp
from jax import lax

D = 768
HEADS = 12
HEAD_DIM = 64
FF = 3072
SEQ_LEN = 1024
MIN_DOC = 60
MAX_DOC = 800
SEQS = 16


def document_layout(key):
    layout_key = jax.random.fold_in(key, 7)
    length_key, choose_key = jax.random.split(layout_key)
    pieces = SEQ_LEN // MIN_DOC + 2
    lengths = jax.random.randint(length_key, (SEQS, pieces), MIN_DOC, MAX_DOC // 2 + 1)
    chosen = jax.random.randint(choose_key, (), 0, SEQS)
    dense = (chosen + 1) % SEQS
    seq_index = jnp.arange(SEQS)
    lengths = jnp.where((seq_index == dense)[:, None], MIN_DOC, lengths)
    leading = jnp.where(seq_index == chosen, MAX_DOC, lengths[:, 0])
    lengths = lengths.at[:, 0].set(leading)
    ends = jnp.cumsum(lengths, axis=1)
    kept = ends < SEQ_LEN - MIN_DOC
    places = jnp.arange(SEQ_LEN)
    passed = kept[:, None, :] & (ends[:, None, :] <= places[None, :, None])
    segment_ids = jnp.sum(passed.astype(jnp.int32), axis=2)
    starts = jnp.max(jnp.where(passed, ends[:, None, :], 0), axis=2)
    return (segment_ids.astype(jnp.int32), (places[None, :] - starts).astype(jnp.int32))


def draw_segments(key, part):
    return document_layout(key)[0]


def draw_positions(key, part):
    return document_layout(key)[1]


def level_of(stream_key, extent, shards, smallest, top_value):
    loudness, own = 1.0, jax.random.fold_in(stream_key, 6)
    for dim, parts in shards:
        draws = jnp.exp(jax.random.uniform(jax.random.fold_in(own, dim), (parts,), jnp.float32, smallest / len(shards), top_value / len(shards)))
        loudness = loudness * jnp.repeat(draws, extent[dim] // parts).reshape([-1 if axis == dim else 1 for axis in range(len(extent))])
    return loudness


def gaussian(stream_key, extent, deviation, reach, cuts=(), kind=jnp.bfloat16):
    loudness = level_of(stream_key, extent, cuts, -0.22, 0.18) if cuts else 1.0
    values = jax.random.normal(stream_key, extent, jnp.float32) * deviation * loudness
    return jnp.minimum(jnp.maximum(values, -reach), reach).astype(kind)


def setup_inputs(seed: int = 0) -> dict:
    seeds = jax.random.split(jax.random.key(seed), 13)
    tokens = gaussian(seeds[0], (SEQS, SEQ_LEN, D), 1.0, 6.0, ((0, 8), (1, 4)))
    segments = draw_segments(jax.random.fold_in(seeds[12], 71), 0)
    positions = draw_positions(jax.random.fold_in(seeds[12], 71), 0)
    qkv_weight = gaussian(seeds[3], (3 * D * D,), D ** -0.5, 0.21875, ((0, 32),))
    out_weight = gaussian(seeds[4], (D * D,), (D // 64) ** -0.5, 1.75, ((0, 32),))
    gate_up_weight = gaussian(seeds[5], (2 * D * FF,), D ** -0.5, 0.21875, ((0, 32),))
    down_weight = gaussian(seeds[6], (FF * D,), FF ** -0.5, 0.109375, ((0, 32),))
    first_gain = jnp.clip(1.0 + 0.18 * jax.random.normal(seeds[7], (D,), jnp.float32), 0.099609375, 1.8984375).astype(jnp.bfloat16)
    first_bias = gaussian(seeds[8], (D,), 0.5, 3.0, ((0, 32),))
    second_gain = jnp.clip(1.0 + 0.18 * jax.random.normal(seeds[9], (D,), jnp.float32), 0.099609375, 1.8984375).astype(jnp.bfloat16)
    second_bias = gaussian(seeds[10], (D,), 0.5, 3.0, ((0, 32),))
    output_grad = gaussian(seeds[11], (SEQS, SEQ_LEN, D), 1.0, 6.0, ((0, 8), (1, 4)))
    return {"tokens": tokens, "segments": segments, "positions": positions, "qkv_weight": qkv_weight, "out_weight": out_weight, "gate_up_weight": gate_up_weight, "down_weight": down_weight, "first_gain": first_gain, "first_bias": first_bias, "second_gain": second_gain, "second_bias": second_bias, "output_grad": output_grad}


norm_epsilon = 1e-05
rotary_base = 1000.0
masked_score = -1000000000.0

@jax.custom_vjp
def low(v):
    return lax.optimization_barrier(v.astype(jnp.bfloat16)).astype(jnp.float32)

@jax.custom_vjp
def low_back(v):
    return v

def low_keep(v):
    return (low(v), None)

def low_pass(kept, grad):
    return (grad,)

def back_keep(v):
    return (v, None)

def back_low(kept, grad):
    return (low(grad),)
low.defvjp(low_keep, low_pass)
low_back.defvjp(back_keep, back_low)

def matmul_high(left, right):
    return jnp.dot(left, right, precision=lax.Precision.HIGHEST)

def rotary_tables(positions, head_size):
    half_dim = head_size // 2
    counter = jnp.arange(half_dim, dtype=jnp.float32)
    inverse = jnp.exp(counter * (-2.0 * math.log(rotary_base) / head_size))
    angles = positions.astype(jnp.float32)[..., None] * inverse
    return (jnp.cos(angles)[..., None, :], jnp.sin(angles)[..., None, :])

def rotate(values, cosine_table, sine_table):
    half_dim = values.shape[-1] // 2
    first_half = values[..., :half_dim]
    second_half = values[..., half_dim:]
    return jnp.concatenate([first_half * cosine_table - second_half * sine_table, second_half * cosine_table + first_half * sine_table], axis=-1)

def layer_norm(hidden_sum, gain, bias):
    average = lax.optimization_barrier(jnp.mean(hidden_sum, axis=-1, keepdims=True))
    centered = hidden_sum - average
    variance = lax.optimization_barrier(jnp.mean(centered * centered, axis=-1, keepdims=True))
    return centered * lax.rsqrt(variance + norm_epsilon) * gain + bias

def block_forward(params, block_tokens, block_segments, cosine_table, sine_table):
    qkv_mat, out_mat, gate_up_mat, down_mat, gain_one, bias_one, gain_two, bias_two = params
    seq_count, key_count, feature_count = block_tokens.shape
    token_rows = block_tokens.reshape(seq_count * key_count, feature_count)
    projected = low_back(matmul_high(token_rows, qkv_mat)).reshape(seq_count, key_count, 3, HEADS, HEAD_DIM)
    queries = low(rotate(projected[:, :, 0], cosine_table, sine_table))
    keys_low = low(rotate(projected[:, :, 1], cosine_table, sine_table))
    values_low = low(projected[:, :, 2])
    scores = low_back(jnp.einsum('bqhd,bkhd->bhqk', queries, keys_low, precision=lax.Precision.HIGHEST))
    same_doc = block_segments[:, None, :, None] == block_segments[:, None, None, :]
    logits = jnp.where(same_doc, scores * 0.125, masked_score)
    log_total = jax.nn.logsumexp(logits, axis=-1, keepdims=True)
    probs = jnp.exp(logits - log_total)
    attended = low_back(low(jnp.einsum('bhqk,bkhd->bqhd', low(probs), values_low, precision=lax.Precision.HIGHEST)))
    branch = low_back(matmul_high(attended.reshape(seq_count * key_count, feature_count), out_mat))
    normed_one = layer_norm(token_rows + branch, gain_one, bias_one)
    gate_up = low_back(matmul_high(low(normed_one), gate_up_mat))
    gate_part = gate_up[:, :FF]
    up_part = gate_up[:, FF:]
    hidden = low(jax.nn.silu(gate_part) * up_part)
    mlp_out = low_back(matmul_high(hidden, down_mat))
    result = layer_norm(normed_one + mlp_out, gain_two, bias_two)
    return result.reshape(seq_count, key_count, feature_count)

def reference(tokens, segments, positions, qkv_weight, out_weight, gate_up_weight, down_weight, first_gain, first_bias, second_gain, second_bias, output_grad):
    params = (qkv_weight.astype(jnp.float32).reshape(D, 3 * D), out_weight.astype(jnp.float32).reshape(D, D), gate_up_weight.astype(jnp.float32).reshape(D, 2 * FF), down_weight.astype(jnp.float32).reshape(FF, D), first_gain.astype(jnp.float32), first_bias.astype(jnp.float32), second_gain.astype(jnp.float32), second_bias.astype(jnp.float32))
    group_size = math.gcd(SEQS, max(1, 4096 // SEQ_LEN))
    block_total = SEQS // group_size
    cosine_table, sine_table = rotary_tables(positions, HEAD_DIM)

    def shape_blocks(array):
        return array.reshape((block_total, group_size) + array.shape[1:])

    def scan_step(totals, block_items):
        block_tokens, block_grad, block_segments, block_cos, block_sin = block_items

        def forward(weights, inputs):
            return block_forward(weights, inputs, block_segments, block_cos, block_sin)
        outputs, pullback = jax.vjp(forward, params, block_tokens)
        weight_grads, token_grad = pullback(block_grad)
        totals = jax.tree.map(lambda first, second: first + second, totals, weight_grads)
        return (totals, (outputs, token_grad))
    zero_grads = jax.tree.map(jnp.zeros_like, params)
    totals, (outputs, token_grad) = lax.scan(scan_step, zero_grads, (shape_blocks(tokens.astype(jnp.float32)), shape_blocks(output_grad.astype(jnp.float32)), shape_blocks(segments), shape_blocks(cosine_table), shape_blocks(sine_table)))
    output = outputs.reshape(SEQS, SEQ_LEN, D).astype(jnp.bfloat16)
    input_grad = token_grad.reshape(SEQS, SEQ_LEN, D)
    return (output, input_grad, totals[0].reshape(-1), totals[1].reshape(-1), totals[2].reshape(-1), totals[3].reshape(-1), totals[4], totals[5], totals[6], totals[7])
```

```python
import math

import jax
import jax.numpy as jnp
from jax import lax
from jax.experimental import pallas as pl
from jax.experimental.pallas import tpu as pltpu
from jax.sharding import PartitionSpec as P

D = 768
HEADS = 12
HEAD_DIM = 64
FF = 3072


norm_epsilon = 1e-05
rotary_base = 1000.0
masked_score = -1000000000.0


def rotary_tables(positions, head_size):
    half_dim = head_size // 2
    counter = jnp.arange(half_dim, dtype=jnp.float32)
    inverse = jnp.exp(counter * (-2.0 * math.log(rotary_base) / head_size))
    angles = positions.astype(jnp.float32)[..., None] * inverse
    return (jnp.cos(angles)[..., None, :], jnp.sin(angles)[..., None, :])


def rotate(values, cosine_table, sine_table):
    half_dim = values.shape[-1] // 2
    first_half = values[..., :half_dim]
    second_half = values[..., half_dim:]
    return jnp.concatenate(
        [
            first_half * cosine_table - second_half * sine_table,
            second_half * cosine_table + first_half * sine_table,
        ],
        axis=-1,
    )


def rotate_back(grads, cosine_table, sine_table):
    half_dim = grads.shape[-1] // 2
    first_half = grads[..., :half_dim]
    second_half = grads[..., half_dim:]
    return jnp.concatenate(
        [
            first_half * cosine_table + second_half * sine_table,
            second_half * cosine_table - first_half * sine_table,
        ],
        axis=-1,
    )


def layer_norm(hidden_sum, gain, bias):
    average = jnp.mean(hidden_sum, axis=-1, keepdims=True)
    centered = hidden_sum - average
    variance = jnp.mean(centered * centered, axis=-1, keepdims=True)
    reciprocal = lax.rsqrt(variance + norm_epsilon)
    normed = centered * reciprocal
    return (normed * gain + bias, normed, reciprocal)


def norm_back(upstream, normed, reciprocal, gain):
    gain_grad = jnp.sum(upstream * normed, axis=0)
    bias_grad = jnp.sum(upstream, axis=0)
    normed_grad = upstream * gain
    input_part = reciprocal * (
        normed_grad
        - jnp.mean(normed_grad, axis=-1, keepdims=True)
        - normed * jnp.mean(normed_grad * normed, axis=-1, keepdims=True)
    )
    return (input_part, gain_grad, bias_grad)


def contract_rows(left, right):
    return lax.dot_general(
        left, right, (((0,), (0,)), ((), ())), preferred_element_type=jnp.float32
    )


def back_dot(left, right):
    return lax.dot_general(
        left, right, (((1,), (1,)), ((), ())), preferred_element_type=jnp.float32
    )


def unpack(gathered):
    qkv_flat, out_flat, gate_up_flat, down_flat, gain_one, bias_one, gain_two, bias_two = gathered
    return (
        qkv_flat.reshape(D, 3 * D),
        out_flat.reshape(D, D),
        gate_up_flat.reshape(D, 2 * FF),
        down_flat.reshape(FF, D),
        gain_one.astype(jnp.float32),
        bias_one.astype(jnp.float32),
        gain_two.astype(jnp.float32),
        bias_two.astype(jnp.float32),
    )


def head_slice(array, offset, lanes):
    piece = lax.dynamic_slice_in_dim(array, offset, lanes, 2)
    return piece.reshape(array.shape[0], array.shape[1], 2, HEAD_DIM)


def pair_logits(query_pair, key_pair, same_doc):
    scores = jnp.einsum("sqhd,skhd->shqk", query_pair, key_pair, preferred_element_type=jnp.float32)
    return jnp.where(same_doc, scores * 0.125, masked_score)


def attend(queries, keys_all, values_all, same_doc):
    seq_count, row_count, feature_count = queries.shape
    lanes = 2 * HEAD_DIM

    def pair_step(head_pair, buffers):
        out_buffer, total_buffer = buffers
        offset = head_pair * lanes
        logits = pair_logits(
            head_slice(queries, offset, lanes), head_slice(keys_all, offset, lanes), same_doc
        )
        highest = jnp.max(logits, axis=-1, keepdims=True)
        log_total = highest + jnp.log(jnp.sum(jnp.exp(logits - highest), axis=-1, keepdims=True))
        probs_low = jnp.exp(logits - log_total).astype(jnp.bfloat16)
        attended = jnp.einsum(
            "shqk,skhd->sqhd",
            probs_low,
            head_slice(values_all, offset, lanes),
            preferred_element_type=jnp.float32,
        ).astype(jnp.bfloat16)
        out_buffer = lax.dynamic_update_slice_in_dim(
            out_buffer, attended.reshape(seq_count, row_count, lanes), offset, 2
        )
        total_buffer = lax.dynamic_update_slice_in_dim(
            total_buffer, log_total[..., 0], 2 * head_pair, 1
        )
        return (out_buffer, total_buffer)

    initial = (
        jnp.zeros((seq_count, row_count, feature_count), jnp.bfloat16),
        jnp.zeros((seq_count, HEADS, row_count), jnp.float32),
    )
    return lax.fori_loop(0, HEADS // 2, pair_step, initial)


def attend_back(queries, keys_all, values_all, same_doc, total_buffer, attended_grad):
    seq_count, row_count, feature_count = queries.shape
    key_count = keys_all.shape[1]
    lanes = 2 * HEAD_DIM

    def pair_step(head_pair, buffers):
        query_buffer, key_buffer, value_buffer = buffers
        offset = head_pair * lanes
        query_pair = head_slice(queries, offset, lanes)
        key_pair = head_slice(keys_all, offset, lanes)
        value_pair = head_slice(values_all, offset, lanes)
        grad_pair = head_slice(attended_grad, offset, lanes)
        logits = pair_logits(query_pair, key_pair, same_doc)
        log_total = lax.dynamic_slice_in_dim(total_buffer, 2 * head_pair, 2, 1)
        probs = jnp.exp(logits - log_total[..., None])
        prob_grad = jnp.einsum(
            "sqhd,skhd->shqk", grad_pair, value_pair, preferred_element_type=jnp.float32
        )
        logit_grad = probs * (prob_grad - jnp.sum(probs * prob_grad, axis=-1, keepdims=True))
        score_grad = (logit_grad * 0.125).astype(jnp.bfloat16)
        query_part = jnp.einsum(
            "shqk,skhd->sqhd", score_grad, key_pair, preferred_element_type=jnp.float32
        )
        key_part = jnp.einsum(
            "shqk,sqhd->skhd", score_grad, query_pair, preferred_element_type=jnp.float32
        )
        value_part = jnp.einsum(
            "shqk,sqhd->skhd",
            probs.astype(jnp.bfloat16),
            grad_pair,
            preferred_element_type=jnp.float32,
        )
        query_buffer = lax.dynamic_update_slice_in_dim(
            query_buffer, query_part.reshape(seq_count, row_count, lanes), offset, 2
        )
        key_buffer = lax.dynamic_update_slice_in_dim(
            key_buffer, key_part.reshape(seq_count, key_count, lanes), offset, 2
        )
        value_buffer = lax.dynamic_update_slice_in_dim(
            value_buffer, value_part.reshape(seq_count, key_count, lanes), offset, 2
        )
        return (query_buffer, key_buffer, value_buffer)

    initial = (
        jnp.zeros((seq_count, row_count, feature_count), jnp.float32),
        jnp.zeros((seq_count, key_count, feature_count), jnp.float32),
        jnp.zeros((seq_count, key_count, feature_count), jnp.float32),
    )
    return lax.fori_loop(0, HEADS // 2, pair_step, initial)


def local(
    tokens,
    segments,
    positions,
    qkv_weight,
    out_weight,
    gate_up_weight,
    down_weight,
    first_gain,
    first_bias,
    second_gain,
    second_bias,
    output_grad,
):
    seq_count = tokens.shape[0]
    row_count = tokens.shape[1]
    gathered = (
        lax.all_gather(qkv_weight, ("dp", "ctx"), axis=0, tiled=True),
        lax.all_gather(out_weight, ("dp", "ctx"), axis=0, tiled=True),
        lax.all_gather(gate_up_weight, ("dp", "ctx"), axis=0, tiled=True),
        lax.all_gather(down_weight, ("dp", "ctx"), axis=0, tiled=True),
        lax.all_gather(first_gain, ("dp", "ctx"), axis=0, tiled=True),
        lax.all_gather(first_bias, ("dp", "ctx"), axis=0, tiled=True),
        lax.all_gather(second_gain, ("dp", "ctx"), axis=0, tiled=True),
        lax.all_gather(second_bias, ("dp", "ctx"), axis=0, tiled=True),
    )
    qkv_mat, out_mat, gate_up_mat, down_mat, gain_one, bias_one, gain_two, bias_two = unpack(
        gathered
    )
    token_rows = tokens.reshape(seq_count * row_count, D)
    cosine_table, sine_table = rotary_tables(positions, HEAD_DIM)
    projected = jnp.dot(token_rows, qkv_mat, preferred_element_type=jnp.float32)
    projected = projected.reshape(seq_count, row_count, 3, HEADS, HEAD_DIM)
    queries = (
        rotate(projected[:, :, 0], cosine_table, sine_table)
        .astype(jnp.bfloat16)
        .reshape(seq_count, row_count, D)
    )
    keys_low = (
        rotate(projected[:, :, 1], cosine_table, sine_table)
        .astype(jnp.bfloat16)
        .reshape(seq_count, row_count, D)
    )
    values_low = projected[:, :, 2].astype(jnp.bfloat16).reshape(seq_count, row_count, D)
    key_ids = segments.astype(jnp.bfloat16)
    keys_all, values_all, ids_all = (
        lax.all_gather(keys_low, "ctx", axis=1, tiled=True),
        lax.all_gather(values_low, "ctx", axis=1, tiled=True),
        lax.all_gather(key_ids, "ctx", axis=1, tiled=True),
    )
    same_doc = (
        segments.astype(jnp.float32)[:, None, :, None]
        == ids_all.astype(jnp.float32)[:, None, None, :]
    )
    attended, total_buffer = attend(queries, keys_all, values_all, same_doc)
    attended_rows = attended.reshape(seq_count * row_count, D)
    branch = jnp.dot(attended_rows, out_mat, preferred_element_type=jnp.float32)
    normed_one, hat_one, recip_one = layer_norm(
        token_rows.astype(jnp.float32) + branch, gain_one, bias_one
    )
    normed_low = normed_one.astype(jnp.bfloat16)
    gate_up = jnp.dot(normed_low, gate_up_mat, preferred_element_type=jnp.float32)
    gate_part = gate_up[:, :FF]
    up_part = gate_up[:, FF:]
    sigmoid_gate = jax.nn.sigmoid(gate_part)
    silu_gate = gate_part * sigmoid_gate
    hidden = (silu_gate * up_part).astype(jnp.bfloat16)
    mlp_out = jnp.dot(hidden, down_mat, preferred_element_type=jnp.float32)
    result, hat_two, recip_two = layer_norm(normed_one + mlp_out, gain_two, bias_two)
    output = result.astype(jnp.bfloat16).reshape(tokens.shape)
    again = (
        lax.all_gather(qkv_weight, ("dp", "ctx"), axis=0, tiled=True),
        lax.all_gather(out_weight, ("dp", "ctx"), axis=0, tiled=True),
        lax.all_gather(gate_up_weight, ("dp", "ctx"), axis=0, tiled=True),
        lax.all_gather(down_weight, ("dp", "ctx"), axis=0, tiled=True),
        lax.all_gather(first_gain, ("dp", "ctx"), axis=0, tiled=True),
        lax.all_gather(first_bias, ("dp", "ctx"), axis=0, tiled=True),
        lax.all_gather(second_gain, ("dp", "ctx"), axis=0, tiled=True),
        lax.all_gather(second_bias, ("dp", "ctx"), axis=0, tiled=True),
    )
    qkv_mat, out_mat, gate_up_mat, down_mat, gain_one, bias_one, gain_two, bias_two = unpack(again)
    keys_all, values_all, ids_all = (
        lax.all_gather(keys_low, "ctx", axis=1, tiled=True),
        lax.all_gather(values_low, "ctx", axis=1, tiled=True),
        lax.all_gather(key_ids, "ctx", axis=1, tiled=True),
    )
    upstream = output_grad.reshape(seq_count * row_count, D).astype(jnp.float32)
    second_grad, second_gain_part, second_bias_part = norm_back(
        upstream, hat_two, recip_two, gain_two
    )
    mlp_grad = second_grad.astype(jnp.bfloat16)
    down_part = contract_rows(hidden, mlp_grad)
    hidden_grad = back_dot(mlp_grad, down_mat)
    gate_grad = hidden_grad * up_part * (sigmoid_gate * (1.0 + gate_part * (1.0 - sigmoid_gate)))
    up_grad = hidden_grad * silu_gate
    gate_up_grad = jnp.concatenate([gate_grad, up_grad], axis=1).astype(jnp.bfloat16)
    gate_up_part = contract_rows(normed_low, gate_up_grad)
    gate_up_flat = gate_up_part.reshape(-1)
    early = (
        lax.psum_scatter(gate_up_flat, ("dp", "ctx"), scatter_dimension=0, tiled=True),
        lax.psum_scatter(second_gain_part, ("dp", "ctx"), scatter_dimension=0, tiled=True),
        lax.psum_scatter(second_bias_part, ("dp", "ctx"), scatter_dimension=0, tiled=True),
    )
    gate_up_share, gain_two_share, bias_two_share = early
    normed_grad = second_grad + back_dot(gate_up_grad, gate_up_mat)
    first_grad, first_gain_part, first_bias_part = norm_back(
        normed_grad, hat_one, recip_one, gain_one
    )
    branch_grad = first_grad.astype(jnp.bfloat16)
    out_part = contract_rows(attended_rows, branch_grad)
    attended_grad = (
        back_dot(branch_grad, out_mat).astype(jnp.bfloat16).reshape(seq_count, row_count, D)
    )
    query_grad, key_partial, value_partial = attend_back(
        queries, keys_all, values_all, same_doc, total_buffer, attended_grad
    )
    key_grad, value_grad = (
        lax.psum_scatter(
            key_partial.astype(jnp.bfloat16), "ctx", scatter_dimension=1, tiled=True
        ).astype(jnp.float32),
        lax.psum_scatter(
            value_partial.astype(jnp.bfloat16), "ctx", scatter_dimension=1, tiled=True
        ).astype(jnp.float32),
    )
    head_shape = (seq_count, row_count, HEADS, HEAD_DIM)
    query_raw = rotate_back(query_grad.reshape(head_shape), cosine_table, sine_table).reshape(-1, D)
    key_raw = rotate_back(key_grad.reshape(head_shape), cosine_table, sine_table).reshape(-1, D)
    projected_grad = jnp.concatenate(
        [query_raw, key_raw, value_grad.reshape(-1, D)], axis=1
    ).astype(jnp.bfloat16)
    qkv_part = contract_rows(token_rows, projected_grad)
    input_grad = (back_dot(projected_grad, qkv_mat) + first_grad).reshape(tokens.shape)
    qkv_flat = qkv_part.reshape(-1)
    out_flat = out_part.reshape(-1)
    down_flat = down_part.reshape(-1)
    late = (
        lax.psum_scatter(qkv_flat, ("dp", "ctx"), scatter_dimension=0, tiled=True),
        lax.psum_scatter(out_flat, ("dp", "ctx"), scatter_dimension=0, tiled=True),
        lax.psum_scatter(down_flat, ("dp", "ctx"), scatter_dimension=0, tiled=True),
        lax.psum_scatter(first_gain_part, ("dp", "ctx"), scatter_dimension=0, tiled=True),
        lax.psum_scatter(first_bias_part, ("dp", "ctx"), scatter_dimension=0, tiled=True),
    )
    qkv_share, out_share, down_share, gain_one_share, bias_one_share = late
    return (
        output,
        input_grad,
        qkv_share,
        out_share,
        gate_up_share,
        down_share,
        gain_one_share,
        bias_one_share,
        gain_two_share,
        bias_two_share,
    )


PAIR = 2 * HEAD_DIM
HALF_D = D // 2
LOG2E = 1.4426950408889634
BF = jnp.bfloat16
F32 = jnp.float32
AXES = ("dp", "ctx")


def dot_nn(left, right):
    return lax.dot_general(left, right, (((1,), (0,)), ((), ())), preferred_element_type=F32)


def dot_nt(left, right):
    return lax.dot_general(left, right, (((1,), (1,)), ((), ())), preferred_element_type=F32)


def dot_tn(left, right):
    return lax.dot_general(left, right, (((0,), (0,)), ((), ())), preferred_element_type=F32)


def swap_halves(tile):
    lane = lax.broadcasted_iota(jnp.int32, tile.shape, 1)
    low_half = lax.rem(lane, HEAD_DIM) < HEAD_DIM // 2
    ahead = pltpu.roll(tile, PAIR - HEAD_DIM // 2, 1)
    behind = pltpu.roll(tile, HEAD_DIM // 2, 1)
    return jnp.where(low_half, ahead, behind)


def qkv_body(x_ref, w_ref, cos_ref, sin_ref, o_ref):
    product = dot_nn(x_ref[...], w_ref[0])
    part = pl.program_id(0)

    @pl.when(part < 2)
    def _():
        for c in range(HALF_D // PAIR):
            tile = product[:, c * PAIR : (c + 1) * PAIR]
            turned = tile * cos_ref[...] + swap_halves(tile) * sin_ref[...]
            o_ref[:, c * PAIR : (c + 1) * PAIR] = turned.astype(BF)

    @pl.when(part == 2)
    def _():
        o_ref[...] = product.astype(BF)


def project_qkv(tokens, weight, cosine, sine):
    rows = tokens.shape[0]
    tile = 256
    return pl.pallas_call(
        qkv_body,
        out_shape=jax.ShapeDtypeStruct((rows, 3 * HALF_D), BF),
        grid=(3, rows // tile),
        in_specs=[
            pl.BlockSpec((tile, D), lambda i, r: (r, 0)),
            pl.BlockSpec((1, D, HALF_D), lambda i, r: (i, 0, 0)),
            pl.BlockSpec((tile, PAIR), lambda i, r: (r, 0)),
            pl.BlockSpec((tile, PAIR), lambda i, r: (r, 0)),
        ],
        out_specs=pl.BlockSpec((tile, HALF_D), lambda i, r: (r, i)),
        cost_estimate=pl.CostEstimate(
            flops=2 * rows * D * 3 * HALF_D, bytes_accessed=6 * rows * D, transcendentals=0
        ),
        name="project_qkv",
    )(tokens, weight, cosine, sine)


Q_TILE = 256


def lane_head(shape):
    return lax.broadcasted_iota(jnp.int32, shape, 1) // HEAD_DIM


def row_head(shape):
    return lax.broadcasted_iota(jnp.int32, shape, 0) // HEAD_DIM


def attend_body(q_ref, k_ref, v_ref, segc_ref, segr_ref, o_ref, l_ref):
    keys = k_ref[...]
    values_t = v_ref[...].astype(F32).T.astype(BF)
    heads_down = row_head(values_t.shape)
    masked_values = [jnp.where(heads_down == h, values_t, jnp.zeros_like(values_t)) for h in range(2)]
    rows = q_ref.shape[0]
    scale = 0.125 * LOG2E
    for t in range(rows // Q_TILE):
        span = pl.ds(t * Q_TILE, Q_TILE)
        queries = q_ref[span, :]
        heads_across = lane_head(queries.shape)
        same = segc_ref[...] == segr_ref[:, span]
        total = jnp.zeros((PAIR, Q_TILE), F32)
        for h in range(2):
            scores = dot_nt(keys, jnp.where(heads_across == h, queries, jnp.zeros_like(queries)))
            scores = jnp.where(same, scores * scale, masked_score)
            highest = jnp.max(scores, axis=0, keepdims=True)
            weights = jnp.exp2(scores - highest)
            norm = jnp.sum(weights, axis=0, keepdims=True)
            l_ref[0, h : h + 1, span] = highest + jnp.log2(norm)
            total = total + dot_nn(masked_values[h], weights.astype(BF)) * (1.0 / norm)
        o_ref[span, :] = total.T.astype(BF)


def attend_chip(qkv, seg_col, seg_row):
    rows = qkv.shape[0]
    pairs = HALF_D // PAIR
    return pl.pallas_call(
        attend_body,
        out_shape=(
            jax.ShapeDtypeStruct((rows, HALF_D), BF),
            jax.ShapeDtypeStruct((pairs, 8, rows), F32),
        ),
        grid=(pairs,),
        in_specs=[
            pl.BlockSpec((rows, PAIR), lambda p: (0, p)),
            pl.BlockSpec((rows, PAIR), lambda p: (0, pairs + p)),
            pl.BlockSpec((rows, PAIR), lambda p: (0, 2 * pairs + p)),
            pl.BlockSpec((rows, 1), lambda p: (0, 0)),
            pl.BlockSpec((1, rows), lambda p: (0, 0)),
        ],
        out_specs=(
            pl.BlockSpec((rows, PAIR), lambda p: (0, p)),
            pl.BlockSpec((1, 8, rows), lambda p: (p, 0, 0)),
        ),
        compiler_params=pltpu.CompilerParams(vmem_limit_bytes=48 * 1024 * 1024),
        cost_estimate=pl.CostEstimate(
            flops=pairs * 8 * rows * rows * HEAD_DIM,
            bytes_accessed=8 * rows * HALF_D,
            transcendentals=2 * pairs * rows * rows,
        ),
        name="attend_chip",
    )(qkv, qkv, qkv, seg_col, seg_row)


def attend_back_body(
    q_ref, k_ref, v_ref, g_ref, l_ref, segc_ref, segr_ref, cos_ref, sin_ref, dq_ref, dk_ref, dv_ref,
    dk_sum, dv_sum,
):
    keys = k_ref[...]
    values = v_ref[...]
    keys_t = keys.astype(F32).T.astype(BF)
    heads_down = row_head(keys_t.shape)
    masked_keys = [jnp.where(heads_down == h, keys_t, jnp.zeros_like(keys_t)) for h in range(2)]
    rows = q_ref.shape[0]
    scale = 0.125 * LOG2E
    for t in range(rows // Q_TILE):
        span = pl.ds(t * Q_TILE, Q_TILE)
        queries = q_ref[span, :]
        grads = g_ref[span, :]
        heads_across = lane_head(queries.shape)
        same = segc_ref[...] == segr_ref[:, span]
        dq_t = jnp.zeros((PAIR, Q_TILE), F32)
        dk_part = None
        dv_part = None
        for h in range(2):
            own_q = jnp.where(heads_across == h, queries, jnp.zeros_like(queries))
            own_g = jnp.where(heads_across == h, grads, jnp.zeros_like(grads))
            scores = dot_nt(keys, own_q)
            logits = jnp.where(same, scores * scale, masked_score)
            probs = jnp.exp2(logits - l_ref[0, h : h + 1, span])
            prob_grad = dot_nt(values, own_g)
            mixed = probs * prob_grad
            mean = jnp.sum(mixed, axis=0, keepdims=True)
            score_grad = (mixed - probs * mean).astype(BF)
            dv_new = dot_nn(probs.astype(BF), own_g)
            dk_new = dot_nn(score_grad, own_q)
            dv_part = dv_new if dv_part is None else dv_part + dv_new
            dk_part = dk_new if dk_part is None else dk_part + dk_new
            dq_t = dq_t + dot_nn(masked_keys[h], score_grad)
        if t == 0:
            dk_sum[...] = dk_part
            dv_sum[...] = dv_part
        else:
            dk_sum[...] += dk_part
            dv_sum[...] += dv_part
        dq = dq_t.T * 0.125
        dq_ref[span, :] = (dq * cos_ref[span, :] - swap_halves(dq) * sin_ref[span, :]).astype(BF)
    dk = dk_sum[...] * 0.125
    dk_ref[...] = (dk * cos_ref[...] - swap_halves(dk) * sin_ref[...]).astype(BF)
    dv_ref[...] = dv_sum[...].astype(BF)


def attend_back_chip(qkv, grads, totals, seg_col, seg_row, cosine, sine):
    rows = qkv.shape[0]
    pairs = HALF_D // PAIR
    part = jax.ShapeDtypeStruct((rows, HALF_D), BF)
    column = pl.BlockSpec((rows, PAIR), lambda p: (0, p))
    whole = pl.BlockSpec((rows, PAIR), lambda p: (0, 0))
    return pl.pallas_call(
        attend_back_body,
        out_shape=(part, part, part),
        grid=(pairs,),
        in_specs=[
            column,
            pl.BlockSpec((rows, PAIR), lambda p: (0, pairs + p)),
            pl.BlockSpec((rows, PAIR), lambda p: (0, 2 * pairs + p)),
            column,
            pl.BlockSpec((1, 8, rows), lambda p: (p, 0, 0)),
            pl.BlockSpec((rows, 1), lambda p: (0, 0)),
            pl.BlockSpec((1, rows), lambda p: (0, 0)),
            whole,
            whole,
        ],
        out_specs=(column, column, column),
        scratch_shapes=[pltpu.VMEM((rows, PAIR), F32), pltpu.VMEM((rows, PAIR), F32)],
        compiler_params=pltpu.CompilerParams(vmem_limit_bytes=56 * 1024 * 1024),
        cost_estimate=pl.CostEstimate(
            flops=pairs * 20 * rows * rows * HEAD_DIM,
            bytes_accessed=16 * rows * HALF_D,
            transcendentals=2 * pairs * rows * rows,
        ),
        name="attend_back_chip",
    )(qkv, qkv, qkv, grads, totals, seg_col, seg_row, cosine, sine)


def at(array, index, axis):
    return lax.dynamic_index_in_dim(array, index, axis, keepdims=False)


class Chip:
    def __init__(self, side, depth):
        self.side, self.depth = side, depth
        place = lax.axis_index("dp")
        self.k = lax.rem(place, 2)
        self.x = lax.rem(place // 2, side)
        self.y = place // (2 * side)
        self.z = lax.axis_index("ctx")

    def move(self, array, target):
        pairs = []
        for y in range(self.side):
            for x in range(self.side):
                for k in range(2):
                    for z in range(self.depth):
                        ty, tx, tk, tz = target(y, x, k, z)
                        source = ((y * self.side + x) * 2 + k) * self.depth + z
                        goal = ((ty * self.side + tx) * 2 + tk) * self.depth + tz % self.depth
                        pairs.append((source, goal))
        return lax.ppermute(array, AXES, pairs)

    def core(self, array):
        return self.move(array, lambda y, x, k, z: (y, x, 1 - k, z))

    def across_x(self, array):
        return self.move(array, lambda y, x, k, z: (y, 1 - x, k, z))

    def across_y(self, array):
        return self.move(array, lambda y, x, k, z: (1 - y, x, k, z))

    def up(self, array):
        return self.move(array, lambda y, x, k, z: (y, x, k, z + 1))

    def down(self, array):
        return self.move(array, lambda y, x, k, z: (y, x, k, z - 1))

    def order(self, index, own, other, axis=0):
        own, other = jnp.expand_dims(own, axis), jnp.expand_dims(other, axis)
        shape = [1] * own.ndim
        shape[axis] = 2
        return jnp.where(jnp.arange(2).reshape(shape) == index, own, other)

    def gather_x(self, array, axis=0):
        return self.order(self.x, array, self.across_x(array), axis)

    def gather_y(self, array, axis=0):
        return self.order(self.y, array, self.across_y(array), axis)

    def ring_z(self, array):
        half = array.shape[0] // 2
        below, above = self.up(array), self.down(array)
        far_a = self.up(below[:half])
        far_b = self.down(above[half:])
        return (array, above, jnp.concatenate([far_a, far_b], 0), below)

    def gather_z(self, array, axis=0):
        pieces = self.ring_z(array)
        shape = list(array.shape)
        shape.insert(axis, self.depth)
        result = jnp.zeros(shape, array.dtype)
        for step, piece in enumerate(pieces):
            place = lax.rem(self.z + step, self.depth)
            result = lax.dynamic_update_index_in_dim(result, piece, place, axis)
        return result

    def scatter(self, array, index, across, axis):
        own = at(array, index, axis)
        got = across(at(array, 1 - index, axis).astype(BF))
        return own.astype(F32) + got.astype(F32)

    def scatter_x(self, array, axis=0):
        return self.scatter(array, self.x, self.across_x, axis)

    def scatter_y(self, array, axis=0):
        return self.scatter(array, self.y, self.across_y, axis)

    def scatter_z(self, array, axis=0):
        def share(step):
            return at(array, lax.rem(self.z + step, self.depth), axis)

        far = share(2).astype(BF)
        half = far.shape[0] // 2
        first = self.up(far[:half])
        second = self.down(far[half:])
        above, below = share(1), share(3)
        sum_above = (above[:half].astype(F32) + first.astype(F32)).astype(BF)
        sum_below = (below[half:].astype(F32) + second.astype(F32)).astype(BF)
        got_a = self.up(jnp.concatenate([sum_above, above[half:].astype(BF)], 0))
        got_b = self.down(jnp.concatenate([below[:half].astype(BF), sum_below], 0))
        return share(0).astype(F32) + got_a.astype(F32) + got_b.astype(F32)


def to_sequence(chip, blocks):
    got = []
    for r in range(2):
        j = lax.rem(chip.z + r, 2)
        got.append(
            chip.move(at(blocks, j, 0), lambda y, x, k, z, r=r: (y, x, z // 2, 2 * k + (r + z) % 2))
        )
    odd = lax.rem(chip.z, 2)
    return chip.order(odd, got[0], got[1])


def from_sequence(chip, halves):
    got = []
    for r in range(2):
        s = lax.rem(chip.z + r, 2)
        got.append(
            chip.move(at(halves, s, 0), lambda y, x, k, z, r=r: (y, x, z // 2, 2 * k + (z + r) % 2))
        )
    odd = lax.rem(chip.z, 2)
    return chip.order(odd, got[0], got[1])


def chip_local(
    tokens,
    segments,
    positions,
    qkv_weight,
    out_weight,
    gate_up_weight,
    down_weight,
    first_gain,
    first_bias,
    second_gain,
    second_bias,
    output_grad,
):
    depth = lax.axis_size("ctx")
    side = math.isqrt(lax.axis_size("dp") // 2)
    chip = Chip(side, depth)
    k, z = chip.k, chip.z
    quarter = tokens.shape[1]
    rows = depth * quarter
    half = rows // 2
    owners = 2 * side * side * depth
    d_rows, ff_rows = D // owners, FF // owners
    planes = side * side
    ff_cols = FF // (2 * planes)
    ff_half = FF // 2

    extra = jnp.stack(
        [segments, positions // 32, lax.rem(positions, 32)], axis=1
    ).astype(BF)
    extra = jnp.pad(extra, ((0, 0), (0, 13), (0, D - quarter)))
    own_tokens = to_sequence(chip, jnp.concatenate([tokens, extra], axis=1))

    qkv_own = qkv_weight.reshape(d_rows, 3, 2, HALF_D)
    gate_up_own = gate_up_weight.reshape(d_rows, 2, planes, 2, ff_cols)

    def column_half(core):
        q = at(qkv_own, core, 2).reshape(d_rows, 3 * HALF_D)
        g = at(gate_up_own, core, 3).reshape(d_rows, FF)
        return jnp.concatenate([q, g], axis=1)

    shard = chip.order(k, column_half(k), chip.core(column_half(1 - k)))
    qkv_block = shard[:, :, : 3 * HALF_D].reshape(2, d_rows, 3, HALF_D).transpose(2, 0, 1, 3)
    gate_up_block = shard[:, :, 3 * HALF_D :]

    qkv_z = chip.gather_z(qkv_block.reshape(6 * d_rows, HALF_D)).reshape(depth, 3, 2, d_rows, HALF_D)
    qkv_a = chip.gather_y(chip.gather_x(qkv_z[:, :, 0]), 0)
    qkv_b = chip.gather_x(chip.gather_y(qkv_z[:, :, 1]), 1)
    qkv_mat = jnp.stack([qkv_a, qkv_b], axis=2).transpose(4, 0, 1, 2, 3, 5, 6)
    qkv_mat = qkv_mat.reshape(3, D, HALF_D)

    both = chip.order(k, own_tokens, chip.core(own_tokens)).reshape(depth, quarter + 16, D)
    all_tokens = both[:, :quarter].reshape(rows, D)
    all_extra = both[:, quarter:, :quarter].astype(F32)
    seg_all = all_extra[:, 0].reshape(rows)
    pos_all = (all_extra[:, 1] * 32.0 + all_extra[:, 2]).reshape(rows)
    token_half = own_tokens[:, :quarter].reshape(half, D)
    lane = jnp.arange(PAIR)
    counter = lax.rem(lane, HEAD_DIM // 2).astype(F32)
    inverse = jnp.exp(counter * (-2.0 * math.log(rotary_base) / HEAD_DIM))
    angles = pos_all[:, None] * inverse
    cosine = jnp.cos(angles)
    sine = jnp.where(lax.rem(lane, HEAD_DIM) < HEAD_DIM // 2, -1.0, 1.0) * jnp.sin(angles)
    seg_col, seg_row = seg_all[:, None], seg_all[None, :]

    gate_up_xy = chip.gather_y(chip.gather_x(gate_up_block))
    gate_up_xy = gate_up_xy.reshape(planes * 2, d_rows, FF)
    gate_up_mat = chip.gather_z(gate_up_xy, 1).reshape(D, FF)

    norms = jnp.concatenate([first_gain, first_bias, second_gain, second_bias])
    norm_rows = jnp.pad(norms[None], ((0, 7), (0, D - 4 * d_rows)))
    shared = jnp.concatenate(
        [down_weight.reshape(ff_rows, D), out_weight.reshape(d_rows, D), norm_rows], axis=0
    )
    mid = shared.shape[0] // 2
    shared_z = chip.gather_z(shared)
    shared_a = chip.gather_y(chip.gather_x(shared_z[:, :mid]))
    shared_b = chip.gather_x(chip.gather_y(shared_z[:, mid:]), 1)
    shared_all = jnp.concatenate([shared_a, shared_b], axis=3)
    down_mat = shared_all[:, :, :, :ff_rows].reshape(ff_half, D)
    rest = shared_all[:, :, :, ff_rows:]
    rest = chip.order(k, rest, chip.core(rest), 2)
    out_mat = rest[..., :d_rows, :].reshape(D, D)
    norms_all = rest[..., d_rows, : 4 * d_rows].reshape(owners, 4, d_rows)
    norms_all = norms_all.transpose(1, 0, 2).reshape(4, D).astype(F32)
    gain_one, bias_one, gain_two, bias_two = (norms_all[i] for i in range(4))

    grad_half = to_sequence(chip, output_grad).reshape(half, D).astype(F32)

    qkv = project_qkv(all_tokens, qkv_mat, cosine, sine)
    attended, totals = attend_chip(qkv, seg_col, seg_row)
    parts = attended.reshape(2, half, HALF_D)
    other = chip.core(at(parts, 1 - k, 0))
    attended_rows = chip.order(k, at(parts, k, 0), other, 1).reshape(half, D)
    branch = dot_nn(attended_rows, out_mat)
    normed_one, hat_one, recip_one = layer_norm(token_half.astype(F32) + branch, gain_one, bias_one)
    normed_own = normed_one.astype(BF)
    normed_low = chip.order(k, normed_own, chip.core(normed_own)).reshape(rows, D)
    gate_up = dot_nn(normed_low, gate_up_mat)
    gate_part, up_part = gate_up[:, :ff_half], gate_up[:, ff_half:]
    sigmoid_gate = jax.nn.sigmoid(gate_part)
    silu_gate = gate_part * sigmoid_gate
    hidden = (silu_gate * up_part).astype(BF)

    def sum_cores(left, right):
        both_parts = left.reshape(2, half, left.shape[1])
        product = right(at(both_parts, 1 - k, 0)).astype(BF)
        got = chip.core(product)
        return right(at(both_parts, k, 0)) + got.astype(F32)

    mlp_out = sum_cores(hidden, lambda part: dot_nn(part, down_mat))
    result, hat_two, recip_two = layer_norm(normed_one + mlp_out, gain_two, bias_two)
    output = from_sequence(chip, result.astype(BF).reshape(2, quarter, D))

    second_grad, second_gain_part, second_bias_part = norm_back(
        grad_half, hat_two, recip_two, gain_two
    )
    mlp_own = second_grad.astype(BF)
    mlp_grad = chip.order(k, mlp_own, chip.core(mlp_own)).reshape(rows, D)
    hidden_grad = dot_nt(mlp_grad, down_mat)
    gate_grad = hidden_grad * up_part * (sigmoid_gate * (1.0 + gate_part * (1.0 - sigmoid_gate)))
    up_grad = hidden_grad * silu_gate
    gate_up_grad = jnp.concatenate([gate_grad, up_grad], axis=1).astype(BF)
    gate_up_part = dot_tn(normed_low, gate_up_grad).astype(BF)
    down_part = dot_tn(hidden, mlp_grad).astype(BF)

    gate_up_z = chip.scatter_z(gate_up_part.reshape(planes * 2, depth, d_rows, FF), 1)
    gate_up_y = chip.scatter_y(gate_up_z.reshape(side, side, 2, d_rows, FF))
    gate_up_x = chip.scatter_x(gate_up_y)
    gate_up_got = chip.core(at(gate_up_x, 1 - k, 0).astype(BF)).astype(F32)
    gate_up_share = chip.order(
        k,
        at(gate_up_x, k, 0).reshape(d_rows, 2, planes, ff_cols),
        gate_up_got.reshape(d_rows, 2, planes, ff_cols),
        3,
    ).reshape(-1)

    normed_grad = second_grad + sum_cores(gate_up_grad, lambda part: dot_nt(part, gate_up_mat))
    first_grad, first_gain_part, first_bias_part = norm_back(
        normed_grad, hat_one, recip_one, gain_one
    )
    branch_grad = first_grad.astype(BF)
    out_part = dot_tn(attended_rows, branch_grad)
    attended_own = dot_nt(branch_grad, out_mat).astype(BF).reshape(half, 2, HALF_D)
    attended_got = chip.core(at(attended_own, 1 - k, 1))
    attended_grad = chip.order(k, at(attended_own, k, 1), attended_got).reshape(rows, HALF_D)

    norm_parts = jnp.stack([first_gain_part, first_bias_part, second_gain_part, second_bias_part])
    norm_parts = norm_parts.reshape(4, owners, d_rows).transpose(1, 0, 2).reshape(owners, 1, 4 * d_rows)
    norm_parts = jnp.pad(norm_parts, ((0, 0), (0, 7), (0, D - 4 * d_rows)))
    rest_part = jnp.concatenate([out_part.reshape(owners, d_rows, D), norm_parts], axis=1)
    rest_part = rest_part.reshape(side, side, 2, depth, d_rows + 8, D).astype(BF)
    rest_own = at(rest_part, k, 2).astype(F32) + chip.core(at(rest_part, 1 - k, 2)).astype(F32)
    shared_part = jnp.concatenate(
        [down_part.reshape(side, side, depth, ff_rows, D), rest_own.astype(BF)], axis=3
    )
    part_a = chip.scatter_y(chip.scatter_x(shared_part[:, :, :, :mid], 1).astype(BF))
    part_b = chip.scatter_x(chip.scatter_y(shared_part[:, :, :, mid:], 0).astype(BF))
    shared_share = chip.scatter_z(jnp.concatenate([part_a, part_b], axis=1).astype(BF))
    down_share = shared_share[:ff_rows].reshape(-1)
    out_share = shared_share[ff_rows : ff_rows + d_rows].reshape(-1)
    norm_share = shared_share[ff_rows + d_rows, : 4 * d_rows].reshape(4, d_rows)

    dq, dk, dv = attend_back_chip(qkv, attended_grad, totals, seg_col, seg_row, cosine, sine)
    projected_grad = jnp.concatenate([dq, dk, dv], axis=1)
    qkv_part = dot_tn(all_tokens, projected_grad).astype(BF)
    qkv_part = qkv_part.reshape(side, side, 2, depth, d_rows, 3 * HALF_D)
    qkv_pa = chip.scatter_y(chip.scatter_x(qkv_part[:, :, 0], 1).astype(BF))
    qkv_pb = chip.scatter_x(chip.scatter_y(qkv_part[:, :, 1], 0).astype(BF))
    qkv_sum = chip.scatter_z(jnp.stack([qkv_pa, qkv_pb], axis=1).astype(BF))
    qkv_got = chip.core(at(qkv_sum, 1 - k, 0).astype(BF)).astype(F32)
    qkv_share = chip.order(
        k,
        at(qkv_sum, k, 0).reshape(d_rows, 3, HALF_D),
        qkv_got.reshape(d_rows, 3, HALF_D),
        2,
    ).reshape(-1)

    flat_weight = qkv_mat.transpose(1, 0, 2).reshape(D, 3 * HALF_D)
    input_half = first_grad + sum_cores(projected_grad, lambda part: dot_nt(part, flat_weight))
    input_grad = from_sequence(chip, input_half.astype(BF).reshape(2, quarter, D)).astype(F32)
    return (
        output,
        input_grad,
        qkv_share,
        out_share,
        gate_up_share,
        down_share,
        norm_share[0],
        norm_share[1],
        norm_share[2],
        norm_share[3],
    )


def solution(mesh):
    in_specs = (
        P("dp", "ctx", None),
        P("dp", "ctx"),
        P("dp", "ctx"),
        P(("dp", "ctx")),
        P(("dp", "ctx")),
        P(("dp", "ctx")),
        P(("dp", "ctx")),
        P(("dp", "ctx")),
        P(("dp", "ctx")),
        P(("dp", "ctx")),
        P(("dp", "ctx")),
        P("dp", "ctx", None),
    )
    out_specs = (
        P("dp", "ctx", None),
        P("dp", "ctx", None),
        P(("dp", "ctx")),
        P(("dp", "ctx")),
        P(("dp", "ctx")),
        P(("dp", "ctx")),
        P(("dp", "ctx")),
        P(("dp", "ctx")),
        P(("dp", "ctx")),
        P(("dp", "ctx")),
    )
    planes = mesh.shape["dp"] // 2
    fits = planes == 4 and mesh.shape["ctx"] == 4
    body = chip_local if fits else local
    return jax.shard_map(body, mesh=mesh, in_specs=in_specs, out_specs=out_specs, check_vma=False)
```

```python
import math

import jax
import jax.numpy as jnp
from jax import lax
from jax.experimental import pallas as pl
from jax.experimental.pallas import tpu as pltpu
from jax.sharding import PartitionSpec as P

D = 768
HEADS = 12
HEAD_DIM = 64
FF = 3072


norm_epsilon = 1e-05
rotary_base = 1000.0
masked_score = -1000000000.0


def rotary_tables(positions, head_size):
    half_dim = head_size // 2
    counter = jnp.arange(half_dim, dtype=jnp.float32)
    inverse = jnp.exp(counter * (-2.0 * math.log(rotary_base) / head_size))
    angles = positions.astype(jnp.float32)[..., None] * inverse
    return (jnp.cos(angles)[..., None, :], jnp.sin(angles)[..., None, :])


def rotate(values, cosine_table, sine_table):
    half_dim = values.shape[-1] // 2
    first_half = values[..., :half_dim]
    second_half = values[..., half_dim:]
    return jnp.concatenate(
        [
            first_half * cosine_table - second_half * sine_table,
            second_half * cosine_table + first_half * sine_table,
        ],
        axis=-1,
    )


def rotate_back(grads, cosine_table, sine_table):
    half_dim = grads.shape[-1] // 2
    first_half = grads[..., :half_dim]
    second_half = grads[..., half_dim:]
    return jnp.concatenate(
        [
            first_half * cosine_table + second_half * sine_table,
            second_half * cosine_table - first_half * sine_table,
        ],
        axis=-1,
    )


def layer_norm(hidden_sum, gain, bias):
    average = jnp.mean(hidden_sum, axis=-1, keepdims=True)
    centered = hidden_sum - average
    variance = jnp.mean(centered * centered, axis=-1, keepdims=True)
    reciprocal = lax.rsqrt(variance + norm_epsilon)
    normed = centered * reciprocal
    return (normed * gain + bias, normed, reciprocal)


def norm_back(upstream, normed, reciprocal, gain):
    gain_grad = jnp.sum(upstream * normed, axis=0)
    bias_grad = jnp.sum(upstream, axis=0)
    normed_grad = upstream * gain
    input_part = reciprocal * (
        normed_grad
        - jnp.mean(normed_grad, axis=-1, keepdims=True)
        - normed * jnp.mean(normed_grad * normed, axis=-1, keepdims=True)
    )
    return (input_part, gain_grad, bias_grad)


def contract_rows(left, right):
    return lax.dot_general(
        left, right, (((0,), (0,)), ((), ())), preferred_element_type=jnp.float32
    )


def back_dot(left, right):
    return lax.dot_general(
        left, right, (((1,), (1,)), ((), ())), preferred_element_type=jnp.float32
    )


def unpack(gathered):
    qkv_flat, out_flat, gate_up_flat, down_flat, gain_one, bias_one, gain_two, bias_two = gathered
    return (
        qkv_flat.reshape(D, 3 * D),
        out_flat.reshape(D, D),
        gate_up_flat.reshape(D, 2 * FF),
        down_flat.reshape(FF, D),
        gain_one.astype(jnp.float32),
        bias_one.astype(jnp.float32),
        gain_two.astype(jnp.float32),
        bias_two.astype(jnp.float32),
    )


def head_slice(array, offset, lanes):
    piece = lax.dynamic_slice_in_dim(array, offset, lanes, 2)
    return piece.reshape(array.shape[0], array.shape[1], 2, HEAD_DIM)


def pair_logits(query_pair, key_pair, same_doc):
    scores = jnp.einsum("sqhd,skhd->shqk", query_pair, key_pair, preferred_element_type=jnp.float32)
    return jnp.where(same_doc, scores * 0.125, masked_score)


def attend(queries, keys_all, values_all, same_doc):
    seq_count, row_count, feature_count = queries.shape
    lanes = 2 * HEAD_DIM

    def pair_step(head_pair, buffers):
        out_buffer, total_buffer = buffers
        offset = head_pair * lanes
        logits = pair_logits(
            head_slice(queries, offset, lanes), head_slice(keys_all, offset, lanes), same_doc
        )
        highest = jnp.max(logits, axis=-1, keepdims=True)
        log_total = highest + jnp.log(jnp.sum(jnp.exp(logits - highest), axis=-1, keepdims=True))
        probs_low = jnp.exp(logits - log_total).astype(jnp.bfloat16)
        attended = jnp.einsum(
            "shqk,skhd->sqhd",
            probs_low,
            head_slice(values_all, offset, lanes),
            preferred_element_type=jnp.float32,
        ).astype(jnp.bfloat16)
        out_buffer = lax.dynamic_update_slice_in_dim(
            out_buffer, attended.reshape(seq_count, row_count, lanes), offset, 2
        )
        total_buffer = lax.dynamic_update_slice_in_dim(
            total_buffer, log_total[..., 0], 2 * head_pair, 1
        )
        return (out_buffer, total_buffer)

    initial = (
        jnp.zeros((seq_count, row_count, feature_count), jnp.bfloat16),
        jnp.zeros((seq_count, HEADS, row_count), jnp.float32),
    )
    return lax.fori_loop(0, HEADS // 2, pair_step, initial)


def attend_back(queries, keys_all, values_all, same_doc, total_buffer, attended_grad):
    seq_count, row_count, feature_count = queries.shape
    key_count = keys_all.shape[1]
    lanes = 2 * HEAD_DIM

    def pair_step(head_pair, buffers):
        query_buffer, key_buffer, value_buffer = buffers
        offset = head_pair * lanes
        query_pair = head_slice(queries, offset, lanes)
        key_pair = head_slice(keys_all, offset, lanes)
        value_pair = head_slice(values_all, offset, lanes)
        grad_pair = head_slice(attended_grad, offset, lanes)
        logits = pair_logits(query_pair, key_pair, same_doc)
        log_total = lax.dynamic_slice_in_dim(total_buffer, 2 * head_pair, 2, 1)
        probs = jnp.exp(logits - log_total[..., None])
        prob_grad = jnp.einsum(
            "sqhd,skhd->shqk", grad_pair, value_pair, preferred_element_type=jnp.float32
        )
        logit_grad = probs * (prob_grad - jnp.sum(probs * prob_grad, axis=-1, keepdims=True))
        score_grad = (logit_grad * 0.125).astype(jnp.bfloat16)
        query_part = jnp.einsum(
            "shqk,skhd->sqhd", score_grad, key_pair, preferred_element_type=jnp.float32
        )
        key_part = jnp.einsum(
            "shqk,sqhd->skhd", score_grad, query_pair, preferred_element_type=jnp.float32
        )
        value_part = jnp.einsum(
            "shqk,sqhd->skhd",
            probs.astype(jnp.bfloat16),
            grad_pair,
            preferred_element_type=jnp.float32,
        )
        query_buffer = lax.dynamic_update_slice_in_dim(
            query_buffer, query_part.reshape(seq_count, row_count, lanes), offset, 2
        )
        key_buffer = lax.dynamic_update_slice_in_dim(
            key_buffer, key_part.reshape(seq_count, key_count, lanes), offset, 2
        )
        value_buffer = lax.dynamic_update_slice_in_dim(
            value_buffer, value_part.reshape(seq_count, key_count, lanes), offset, 2
        )
        return (query_buffer, key_buffer, value_buffer)

    initial = (
        jnp.zeros((seq_count, row_count, feature_count), jnp.float32),
        jnp.zeros((seq_count, key_count, feature_count), jnp.float32),
        jnp.zeros((seq_count, key_count, feature_count), jnp.float32),
    )
    return lax.fori_loop(0, HEADS // 2, pair_step, initial)


def local(
    tokens,
    segments,
    positions,
    qkv_weight,
    out_weight,
    gate_up_weight,
    down_weight,
    first_gain,
    first_bias,
    second_gain,
    second_bias,
    output_grad,
):
    seq_count = tokens.shape[0]
    row_count = tokens.shape[1]
    gathered = (
        lax.all_gather(qkv_weight, ("dp", "ctx"), axis=0, tiled=True),
        lax.all_gather(out_weight, ("dp", "ctx"), axis=0, tiled=True),
        lax.all_gather(gate_up_weight, ("dp", "ctx"), axis=0, tiled=True),
        lax.all_gather(down_weight, ("dp", "ctx"), axis=0, tiled=True),
        lax.all_gather(first_gain, ("dp", "ctx"), axis=0, tiled=True),
        lax.all_gather(first_bias, ("dp", "ctx"), axis=0, tiled=True),
        lax.all_gather(second_gain, ("dp", "ctx"), axis=0, tiled=True),
        lax.all_gather(second_bias, ("dp", "ctx"), axis=0, tiled=True),
    )
    qkv_mat, out_mat, gate_up_mat, down_mat, gain_one, bias_one, gain_two, bias_two = unpack(
        gathered
    )
    token_rows = tokens.reshape(seq_count * row_count, D)
    cosine_table, sine_table = rotary_tables(positions, HEAD_DIM)
    projected = jnp.dot(token_rows, qkv_mat, preferred_element_type=jnp.float32)
    projected = projected.reshape(seq_count, row_count, 3, HEADS, HEAD_DIM)
    queries = (
        rotate(projected[:, :, 0], cosine_table, sine_table)
        .astype(jnp.bfloat16)
        .reshape(seq_count, row_count, D)
    )
    keys_low = (
        rotate(projected[:, :, 1], cosine_table, sine_table)
        .astype(jnp.bfloat16)
        .reshape(seq_count, row_count, D)
    )
    values_low = projected[:, :, 2].astype(jnp.bfloat16).reshape(seq_count, row_count, D)
    key_ids = segments.astype(jnp.bfloat16)
    keys_all, values_all, ids_all = (
        lax.all_gather(keys_low, "ctx", axis=1, tiled=True),
        lax.all_gather(values_low, "ctx", axis=1, tiled=True),
        lax.all_gather(key_ids, "ctx", axis=1, tiled=True),
    )
    same_doc = (
        segments.astype(jnp.float32)[:, None, :, None]
        == ids_all.astype(jnp.float32)[:, None, None, :]
    )
    attended, total_buffer = attend(queries, keys_all, values_all, same_doc)
    attended_rows = attended.reshape(seq_count * row_count, D)
    branch = jnp.dot(attended_rows, out_mat, preferred_element_type=jnp.float32)
    normed_one, hat_one, recip_one = layer_norm(
        token_rows.astype(jnp.float32) + branch, gain_one, bias_one
    )
    normed_low = normed_one.astype(jnp.bfloat16)
    gate_up = jnp.dot(normed_low, gate_up_mat, preferred_element_type=jnp.float32)
    gate_part = gate_up[:, :FF]
    up_part = gate_up[:, FF:]
    sigmoid_gate = jax.nn.sigmoid(gate_part)
    silu_gate = gate_part * sigmoid_gate
    hidden = (silu_gate * up_part).astype(jnp.bfloat16)
    mlp_out = jnp.dot(hidden, down_mat, preferred_element_type=jnp.float32)
    result, hat_two, recip_two = layer_norm(normed_one + mlp_out, gain_two, bias_two)
    output = result.astype(jnp.bfloat16).reshape(tokens.shape)
    again = (
        lax.all_gather(qkv_weight, ("dp", "ctx"), axis=0, tiled=True),
        lax.all_gather(out_weight, ("dp", "ctx"), axis=0, tiled=True),
        lax.all_gather(gate_up_weight, ("dp", "ctx"), axis=0, tiled=True),
        lax.all_gather(down_weight, ("dp", "ctx"), axis=0, tiled=True),
        lax.all_gather(first_gain, ("dp", "ctx"), axis=0, tiled=True),
        lax.all_gather(first_bias, ("dp", "ctx"), axis=0, tiled=True),
        lax.all_gather(second_gain, ("dp", "ctx"), axis=0, tiled=True),
        lax.all_gather(second_bias, ("dp", "ctx"), axis=0, tiled=True),
    )
    qkv_mat, out_mat, gate_up_mat, down_mat, gain_one, bias_one, gain_two, bias_two = unpack(again)
    keys_all, values_all, ids_all = (
        lax.all_gather(keys_low, "ctx", axis=1, tiled=True),
        lax.all_gather(values_low, "ctx", axis=1, tiled=True),
        lax.all_gather(key_ids, "ctx", axis=1, tiled=True),
    )
    upstream = output_grad.reshape(seq_count * row_count, D).astype(jnp.float32)
    second_grad, second_gain_part, second_bias_part = norm_back(
        upstream, hat_two, recip_two, gain_two
    )
    mlp_grad = second_grad.astype(jnp.bfloat16)
    down_part = contract_rows(hidden, mlp_grad)
    hidden_grad = back_dot(mlp_grad, down_mat)
    gate_grad = hidden_grad * up_part * (sigmoid_gate * (1.0 + gate_part * (1.0 - sigmoid_gate)))
    up_grad = hidden_grad * silu_gate
    gate_up_grad = jnp.concatenate([gate_grad, up_grad], axis=1).astype(jnp.bfloat16)
    gate_up_part = contract_rows(normed_low, gate_up_grad)
    gate_up_flat = gate_up_part.reshape(-1)
    early = (
        lax.psum_scatter(gate_up_flat, ("dp", "ctx"), scatter_dimension=0, tiled=True),
        lax.psum_scatter(second_gain_part, ("dp", "ctx"), scatter_dimension=0, tiled=True),
        lax.psum_scatter(second_bias_part, ("dp", "ctx"), scatter_dimension=0, tiled=True),
    )
    gate_up_share, gain_two_share, bias_two_share = early
    normed_grad = second_grad + back_dot(gate_up_grad, gate_up_mat)
    first_grad, first_gain_part, first_bias_part = norm_back(
        normed_grad, hat_one, recip_one, gain_one
    )
    branch_grad = first_grad.astype(jnp.bfloat16)
    out_part = contract_rows(attended_rows, branch_grad)
    attended_grad = (
        back_dot(branch_grad, out_mat).astype(jnp.bfloat16).reshape(seq_count, row_count, D)
    )
    query_grad, key_partial, value_partial = attend_back(
        queries, keys_all, values_all, same_doc, total_buffer, attended_grad
    )
    key_grad, value_grad = (
        lax.psum_scatter(
            key_partial.astype(jnp.bfloat16), "ctx", scatter_dimension=1, tiled=True
        ).astype(jnp.float32),
        lax.psum_scatter(
            value_partial.astype(jnp.bfloat16), "ctx", scatter_dimension=1, tiled=True
        ).astype(jnp.float32),
    )
    head_shape = (seq_count, row_count, HEADS, HEAD_DIM)
    query_raw = rotate_back(query_grad.reshape(head_shape), cosine_table, sine_table).reshape(-1, D)
    key_raw = rotate_back(key_grad.reshape(head_shape), cosine_table, sine_table).reshape(-1, D)
    projected_grad = jnp.concatenate(
        [query_raw, key_raw, value_grad.reshape(-1, D)], axis=1
    ).astype(jnp.bfloat16)
    qkv_part = contract_rows(token_rows, projected_grad)
    input_grad = (back_dot(projected_grad, qkv_mat) + first_grad).reshape(tokens.shape)
    qkv_flat = qkv_part.reshape(-1)
    out_flat = out_part.reshape(-1)
    down_flat = down_part.reshape(-1)
    late = (
        lax.psum_scatter(qkv_flat, ("dp", "ctx"), scatter_dimension=0, tiled=True),
        lax.psum_scatter(out_flat, ("dp", "ctx"), scatter_dimension=0, tiled=True),
        lax.psum_scatter(down_flat, ("dp", "ctx"), scatter_dimension=0, tiled=True),
        lax.psum_scatter(first_gain_part, ("dp", "ctx"), scatter_dimension=0, tiled=True),
        lax.psum_scatter(first_bias_part, ("dp", "ctx"), scatter_dimension=0, tiled=True),
    )
    qkv_share, out_share, down_share, gain_one_share, bias_one_share = late
    return (
        output,
        input_grad,
        qkv_share,
        out_share,
        gate_up_share,
        down_share,
        gain_one_share,
        bias_one_share,
        gain_two_share,
        bias_two_share,
    )


PAIR = 2 * HEAD_DIM
HALF_D = D // 2
LOG2E = 1.4426950408889634
BF = jnp.bfloat16
F32 = jnp.float32
AXES = ("dp", "ctx")
LIGHT = pl.CostEstimate(flops=1024, bytes_accessed=1024, transcendentals=0)
SIDE, DEPTH = 2, 4
OWNERS = 2 * SIDE * SIDE * DEPTH
D_ROWS, FF_ROWS = D // OWNERS, FF // OWNERS
FF_HALF = FF // 2
FF_COLS = FF_HALF // (SIDE * SIDE)
NORM_COLS = 128
OUT_COLS = HALF_D + NORM_COLS
Q_COLS = 3 * HALF_D
NEAR_COLS = Q_COLS + OUT_COLS


def dot_nn(left, right):
    return lax.dot_general(left, right, (((1,), (0,)), ((), ())), preferred_element_type=F32)


def dot_nt(left, right):
    return lax.dot_general(left, right, (((1,), (1,)), ((), ())), preferred_element_type=F32)


def dot_tn(left, right):
    return lax.dot_general(left, right, (((0,), (0,)), ((), ())), preferred_element_type=F32)


def swap_halves(tile):
    lane = lax.broadcasted_iota(jnp.int32, tile.shape, 1)
    low_half = lax.rem(lane, HEAD_DIM) < HEAD_DIM // 2
    ahead = pltpu.roll(tile, PAIR - HEAD_DIM // 2, 1)
    behind = pltpu.roll(tile, HEAD_DIM // 2, 1)
    return jnp.where(low_half, ahead, behind)


def qkv_body(x_ref, w_ref, cos_ref, sin_ref, o_ref):
    product = dot_nn(x_ref[...], w_ref[...])
    part = pl.program_id(0)

    @pl.when(part < 2)
    def _():
        for c in range(HALF_D // PAIR):
            tile = product[:, c * PAIR : (c + 1) * PAIR]
            turned = tile * cos_ref[...] + swap_halves(tile) * sin_ref[...]
            o_ref[:, c * PAIR : (c + 1) * PAIR] = turned.astype(BF)

    @pl.when(part == 2)
    def _():
        o_ref[...] = product.astype(BF)


def project_qkv(tokens, weight, cosine, sine):
    rows = tokens.shape[0]
    tile = rows
    return pl.pallas_call(
        qkv_body,
        out_shape=jax.ShapeDtypeStruct((rows, 3 * HALF_D), BF),
        grid=(3, rows // tile),
        in_specs=[
            pl.BlockSpec((tile, D), lambda i, r: (r, 0)),
            pl.BlockSpec((D, HALF_D), lambda i, r: (0, i)),
            pl.BlockSpec((tile, PAIR), lambda i, r: (r, 0)),
            pl.BlockSpec((tile, PAIR), lambda i, r: (r, 0)),
        ],
        out_specs=pl.BlockSpec((tile, HALF_D), lambda i, r: (r, i)),
        cost_estimate=LIGHT,
        compiler_params=pltpu.CompilerParams(vmem_limit_bytes=32 * 2**20),
        name="project_qkv",
    )(tokens, weight, cosine, sine)


Q_TILE = 256


def lane_head(shape):
    return lax.broadcasted_iota(jnp.int32, shape, 1) // HEAD_DIM


def row_head(shape):
    return lax.broadcasted_iota(jnp.int32, shape, 0) // HEAD_DIM


def attend_body(q_ref, k_ref, v_ref, segc_ref, segr_ref, o_ref, l_ref):
    keys = k_ref[...]
    values_t = v_ref[...].astype(F32).T.astype(BF)
    heads_down = row_head(values_t.shape)
    masked_values = [jnp.where(heads_down == h, values_t, jnp.zeros_like(values_t)) for h in range(2)]
    rows = q_ref.shape[0]
    scale = 0.125 * LOG2E
    for t in range(rows // Q_TILE):
        span = pl.ds(t * Q_TILE, Q_TILE)
        queries = q_ref[span, :]
        heads_across = lane_head(queries.shape)
        same = segc_ref[...] == segr_ref[:, span]
        total = jnp.zeros((PAIR, Q_TILE), F32)
        for h in range(2):
            scores = dot_nt(keys, jnp.where(heads_across == h, queries, jnp.zeros_like(queries)))
            scores = jnp.where(same, scores * scale, masked_score)
            highest = jnp.max(scores, axis=0, keepdims=True)
            weights = jnp.exp2(scores - highest)
            norm = jnp.sum(weights, axis=0, keepdims=True)
            l_ref[h : h + 1, span] = highest + jnp.log2(norm)
            total = total + dot_nn(masked_values[h], weights.astype(BF)) * (1.0 / norm)
        o_ref[span, :] = total.T.astype(BF)


def attend_pair(pair, qkv, seg_col, seg_row):
    rows = qkv.shape[0]
    pairs = HALF_D // PAIR
    return pl.pallas_call(
        attend_body,
        out_shape=(
            jax.ShapeDtypeStruct((rows, PAIR), BF),
            jax.ShapeDtypeStruct((8, rows), F32),
        ),
        grid=(1,),
        in_specs=[
            pl.BlockSpec((rows, PAIR), lambda i: (0, pair)),
            pl.BlockSpec((rows, PAIR), lambda i: (0, pairs + pair)),
            pl.BlockSpec((rows, PAIR), lambda i: (0, 2 * pairs + pair)),
            pl.BlockSpec((rows, 1), lambda i: (0, 0)),
            pl.BlockSpec((1, rows), lambda i: (0, 0)),
        ],
        out_specs=(
            pl.BlockSpec((rows, PAIR), lambda i: (0, 0)),
            pl.BlockSpec((8, rows), lambda i: (0, 0)),
        ),
        compiler_params=pltpu.CompilerParams(vmem_limit_bytes=40 * 2**20),
        cost_estimate=LIGHT,
        name="attend_pair",
    )(qkv, qkv, qkv, seg_col, seg_row)


def attend_back_body(
    q_ref, k_ref, v_ref, g_ref, l_ref, segc_ref, segr_ref, cos_ref, sin_ref, *others
):
    d_ref, dk_sum, dv_sum = others[-3:]
    keys = k_ref[...]
    values = v_ref[...]
    keys_t = keys.astype(F32).T.astype(BF)
    heads_down = row_head(keys_t.shape)
    masked_keys = [jnp.where(heads_down == h, keys_t, jnp.zeros_like(keys_t)) for h in range(2)]
    rows = q_ref.shape[0]
    scale = 0.125 * LOG2E
    for t in range(rows // Q_TILE):
        span = pl.ds(t * Q_TILE, Q_TILE)
        queries = q_ref[span, :]
        grads = g_ref[span, :]
        heads_across = lane_head(queries.shape)
        same = segc_ref[...] == segr_ref[:, span]
        dq_t = jnp.zeros((PAIR, Q_TILE), F32)
        dk_part = None
        dv_part = None
        for h in range(2):
            own_q = jnp.where(heads_across == h, queries, jnp.zeros_like(queries))
            own_g = jnp.where(heads_across == h, grads, jnp.zeros_like(grads))
            scores = dot_nt(keys, own_q)
            logits = jnp.where(same, scores * scale, masked_score)
            probs = jnp.exp2(logits - l_ref[h : h + 1, span])
            prob_grad = dot_nt(values, own_g)
            mixed = probs * prob_grad
            mean = jnp.sum(mixed, axis=0, keepdims=True)
            score_grad = (mixed - probs * mean).astype(BF)
            dv_new = dot_nn(probs.astype(BF), own_g)
            dk_new = dot_nn(score_grad, own_q)
            dv_part = dv_new if dv_part is None else dv_part + dv_new
            dk_part = dk_new if dk_part is None else dk_part + dk_new
            dq_t = dq_t + dot_nn(masked_keys[h], score_grad)
        if t == 0:
            dk_sum[...] = dk_part
            dv_sum[...] = dv_part
        else:
            dk_sum[...] += dk_part
            dv_sum[...] += dv_part
        dq = dq_t.T * 0.125
        d_ref[0, span, :] = (dq * cos_ref[span, :] - swap_halves(dq) * sin_ref[span, :]).astype(BF)
    dk = dk_sum[...] * 0.125
    d_ref[1] = (dk * cos_ref[...] - swap_halves(dk) * sin_ref[...]).astype(BF)
    d_ref[2] = dv_sum[...].astype(BF)


def attend_back_pair(pair, earlier, qkv, grads, totals, seg_col, seg_row, cosine, sine):
    rows = qkv.shape[0]
    pairs = HALF_D // PAIR
    column = pl.BlockSpec((rows, PAIR), lambda i: (0, pair))
    whole = pl.BlockSpec((rows, PAIR), lambda i: (0, 0))
    carried = [] if earlier is None else [earlier]
    return pl.pallas_call(
        attend_back_body,
        out_shape=jax.ShapeDtypeStruct((3, rows, HALF_D), BF),
        grid=(1,),
        in_specs=[
            column,
            pl.BlockSpec((rows, PAIR), lambda i: (0, pairs + pair)),
            pl.BlockSpec((rows, PAIR), lambda i: (0, 2 * pairs + pair)),
            column,
            pl.BlockSpec((8, rows), lambda i: (0, 0)),
            pl.BlockSpec((rows, 1), lambda i: (0, 0)),
            pl.BlockSpec((1, rows), lambda i: (0, 0)),
            whole,
            whole,
        ] + [pl.BlockSpec(memory_space=pl.ANY)] * len(carried),
        out_specs=pl.BlockSpec((3, rows, PAIR), lambda i: (0, 0, pair)),
        scratch_shapes=[pltpu.VMEM((rows, PAIR), F32), pltpu.VMEM((rows, PAIR), F32)],
        input_output_aliases={9: 0} if carried else {},
        compiler_params=pltpu.CompilerParams(vmem_limit_bytes=44 * 2**20),
        cost_estimate=LIGHT,
        name="attend_back_pair",
    )(qkv, qkv, qkv, grads, totals, seg_col, seg_row, cosine, sine, *carried)


def near_part_body(x_ref, g_ref, s_ref, o_ref):
    for n in range(3):
        o_ref[:, n * HALF_D : (n + 1) * HALF_D] = dot_tn(x_ref[...], g_ref[n]).astype(BF)
    o_ref[:, 3 * HALF_D :] = s_ref[...]


def near_weight_part(tokens, grads, out_sum):
    rows = tokens.shape[0]
    return pl.pallas_call(
        near_part_body,
        out_shape=jax.ShapeDtypeStruct((D, NEAR_COLS), BF),
        compiler_params=pltpu.CompilerParams(vmem_limit_bytes=32 * 2**20),
        cost_estimate=LIGHT,
        name="near_weight_part",
    )(tokens, grads, out_sum)


def row_sum_body(x_ref, g_ref, o_ref):
    o_ref[...] = dot_tn(x_ref[...], g_ref[...]).astype(BF)


def gate_up_weight_part(normed, grads):
    rows, tile = normed.shape[0], 512
    return pl.pallas_call(
        row_sum_body,
        out_shape=jax.ShapeDtypeStruct((D, FF), BF),
        grid=(FF // tile,),
        in_specs=[
            pl.BlockSpec((rows, D), lambda i: (0, 0)),
            pl.BlockSpec((rows, tile), lambda i: (0, i)),
        ],
        out_specs=pl.BlockSpec((D, tile), lambda i: (0, i)),
        compiler_params=pltpu.CompilerParams(vmem_limit_bytes=24 * 2**20),
        cost_estimate=LIGHT,
        name="gate_up_weight_part",
    )(normed, grads)


def down_weight_part(hidden, grads):
    rows, tile = hidden.shape[0], 512
    return pl.pallas_call(
        row_sum_body,
        out_shape=jax.ShapeDtypeStruct((FF_HALF, D), BF),
        grid=(FF_HALF // tile,),
        in_specs=[
            pl.BlockSpec((rows, tile), lambda i: (0, i)),
            pl.BlockSpec((rows, D), lambda i: (0, 0)),
        ],
        out_specs=pl.BlockSpec((tile, D), lambda i: (i, 0)),
        compiler_params=pltpu.CompilerParams(vmem_limit_bytes=24 * 2**20),
        cost_estimate=LIGHT,
        name="down_weight_part",
    )(hidden, grads)


def input_part_body(g_ref, w_ref, o_ref):
    total = dot_nt(g_ref[0], w_ref[:, :HALF_D])
    for n in range(1, 3):
        total = total + dot_nt(g_ref[n], w_ref[:, n * HALF_D : (n + 1) * HALF_D])
    o_ref[...] = total.astype(o_ref.dtype)


def input_part(grads, weight, block, dtype):
    rows = grads.shape[1] // 2
    return pl.pallas_call(
        input_part_body,
        out_shape=jax.ShapeDtypeStruct((rows, D), dtype),
        grid=(1,),
        in_specs=[
            pl.BlockSpec((3, rows, HALF_D), lambda i: (0, block, 0)),
            pl.BlockSpec((D, 3 * HALF_D), lambda i: (0, 0)),
        ],
        out_specs=pl.BlockSpec((rows, D), lambda i: (0, 0)),
        compiler_params=pltpu.CompilerParams(vmem_limit_bytes=24 * 2**20),
        cost_estimate=LIGHT,
        name="input_part",
    )(grads, weight)


def at(array, index, axis=0):
    return lax.dynamic_index_in_dim(array, index, axis, keepdims=False)


def after(value, earlier):
    return lax.optimization_barrier((value, earlier))[0]


def coordinates():
    place = lax.axis_index("dp")
    return place // (2 * SIDE), (place // 2) & 1, place & 1, lax.axis_index("ctx")


def place(pieces, shapes, moves):
    dtype = pieces[0].dtype
    count = len(moves(0, 0, 0, 0))
    inputs = len(pieces)

    def body(*refs):
        sources, results, sems = refs[:inputs], refs[inputs:-1], refs[-1]
        copies = []
        for n, (piece, part, result, spot) in enumerate(moves(*coordinates())):
            source = sources[piece] if part is None else sources[piece].at[part]
            copies.append(pltpu.make_async_copy(source, results[result].at[spot], sems.at[n]))
        for copy in copies:
            copy.start()
        for copy in copies:
            copy.wait()

    anywhere = pl.BlockSpec(memory_space=pl.ANY)
    size = sum(math.prod(shape) for shape in shapes) * 2 * jnp.dtype(dtype).itemsize
    return pl.pallas_call(
        body,
        out_shape=tuple(jax.ShapeDtypeStruct(shape, dtype) for shape in shapes),
        in_specs=[anywhere] * inputs,
        out_specs=tuple(pl.BlockSpec(memory_space=pltpu.VMEM) for _ in shapes),
        scratch_shapes=[pltpu.SemaphoreType.DMA((count,))],
        compiler_params=pltpu.CompilerParams(vmem_limit_bytes=max(8 * 2**20, 2 * size)),
        cost_estimate=LIGHT,
        name="place",
    )(*pieces)


def move(array, target):
    pairs = []
    for y in range(SIDE):
        for x in range(SIDE):
            for k in range(2):
                for z in range(DEPTH):
                    ty, tx, tk, tz = target(y, x, k, z)
                    source = ((y * SIDE + x) * 2 + k) * DEPTH + z
                    goal = ((ty * SIDE + tx) * 2 + tk) * DEPTH + tz % DEPTH
                    pairs.append((source, goal))
    return lax.ppermute(array, AXES, pairs)


def core(array):
    return move(array, lambda y, x, k, z: (y, x, 1 - k, z))


def across_x(array):
    return move(array, lambda y, x, k, z: (y, 1 - x, k, z))


def across_y(array):
    return move(array, lambda y, x, k, z: (1 - y, x, k, z))


def up(array):
    return move(array, lambda y, x, k, z: (y, x, k, z + 1))


def down(array):
    return move(array, lambda y, x, k, z: (y, x, k, z - 1))


def order(index, own, other, axis=0):
    first = jnp.where(index == 0, own, other)
    second = jnp.where(index == 0, other, own)
    return jnp.stack([first, second], axis)


def ring_near(array):
    return down(array), up(array)


def ring_far(above, below):
    half = above.shape[0] // 2
    return up(below[:half]), down(above[half:])


def pair_x(array, got):
    return place(
        (array, got), [(SIDE, *array.shape)], lambda y, x, k, z: [(n, None, 0, (x ^ n,)) for n in range(2)]
    )[0]


def pair_y(array, got):
    return place(
        (array, got), [(SIDE, *array.shape)], lambda y, x, k, z: [(n, None, 0, (y ^ n,)) for n in range(2)]
    )[0]


def spread_z(block, pieces):
    both = range(2)
    return place(
        (block, *pieces),
        [(DEPTH, *block.shape[1:])] * 2,
        lambda y, x, k, z: [
            (n, (m,), m, ((z + step) & 3,)) for n, step in ((0, 0), (1, 1), (2, 3)) for m in both
        ] + [(3 + m, (0,), m, ((z + 2) & 3,)) for m in both],
    )


def scatter(array, index, across, axis=0):
    got = across(at(array, 1 - index, axis).astype(BF))
    return at(array, index, axis).astype(F32) + got.astype(F32)


def scatter_far(array, z, axis):
    far = at(array, (z + 2) & 3, axis).astype(BF)
    half = far.shape[0] // 2
    return up(far[:half]), down(far[half:])


def scatter_near(array, z, axis, first, second):
    above, below = at(array, (z + 1) & 3, axis), at(array, (z + 3) & 3, axis)
    half = above.shape[0] // 2
    sum_above = (above[:half].astype(F32) + first.astype(F32)).astype(BF)
    sum_below = (below[half:].astype(F32) + second.astype(F32)).astype(BF)
    got_a = up(jnp.concatenate([sum_above, above[half:].astype(BF)], 0))
    got_b = down(jnp.concatenate([below[:half].astype(BF), sum_below], 0))
    return got_a, got_b


def scatter_own(array, z, axis, got_a, got_b):
    return at(array, z, axis).astype(F32) + got_a.astype(F32) + got_b.astype(F32)


def sequence_step(r):
    return lambda y, x, k, z: (y, x, z // 2, 2 * k + ((r + z) & 1))


def to_sequence(blocks, z):
    return [move(at(blocks, (z + r) & 1), sequence_step(r)) for r in range(2)]


def from_sequence(quarters):
    return [move(quarters[r], sequence_step(r)) for r in range(2)]


def chip_local(
    tokens,
    segments,
    positions,
    qkv_weight,
    out_weight,
    gate_up_weight,
    down_weight,
    first_gain,
    first_bias,
    second_gain,
    second_bias,
    output_grad,
):
    y, x, k, z = coordinates()
    quarter = tokens.shape[1]
    rows = DEPTH * quarter
    half = rows // 2
    planes = SIDE * SIDE

    norms = jnp.stack([first_gain, first_bias, second_gain, second_bias], axis=1)
    norms = jnp.pad(norms, ((0, 0), (0, NORM_COLS - 4)))
    qkv_own = qkv_weight.reshape(D_ROWS, 3 * D)
    gate_up_own = gate_up_weight.reshape(D_ROWS, 2 * FF)
    out_own = out_weight.reshape(D_ROWS, D)

    def column_half(index):
        def part(matrix, start, width):
            left, right = matrix[:, start : start + width], matrix[:, start + width : start + 2 * width]
            return jnp.where(index == 0, left, right)

        pieces = [part(qkv_own, n * D, HALF_D) for n in range(3)]
        pieces += [part(out_own, 0, HALF_D), norms]
        pieces += [part(gate_up_own, n * 2 * FF_COLS, FF_COLS) for n in range(2 * planes)]
        return jnp.concatenate(pieces, axis=1)

    mine, theirs = column_half(k), core(column_half(1 - k))
    both, every = range(2), slice(None)
    near_span, gate_up_span = pl.ds(0, NEAR_COLS), pl.ds(NEAR_COLS, FF)
    near_block, gate_up_block = place(
        (mine, theirs),
        [(2, D_ROWS, NEAR_COLS), (2, D_ROWS, FF)],
        lambda y, x, k, z: [
            (n, (every, span), r, (k ^ n,)) for n in both for r, span in enumerate((near_span, gate_up_span))
        ],
    )

    near_close = ring_near(near_block)
    near_ring = (*near_close, *ring_far(*near_close))
    near_a, near_b = spread_z(near_block, near_ring)
    down_block = after(down_weight.reshape(FF_ROWS, D), near_block)
    down_x = pair_x(down_block, across_x(down_block))
    down_y = pair_y(down_x, across_y(down_x)).reshape(planes, FF_ROWS, D)

    extra = jnp.stack([segments, positions >> 5, positions & 31], axis=1).astype(BF)
    extra = jnp.pad(extra, ((0, 0), (0, 13), (0, D - quarter)))
    packed = jnp.concatenate([tokens, extra], axis=1)
    own_tokens = jnp.concatenate(to_sequence(packed, z), axis=0)
    near_ax = pair_x(near_a, across_x(near_a))
    near_by = pair_y(near_b, across_y(near_b))
    gate_up_close = ring_near(after(gate_up_block, (own_tokens, near_ring)))
    gate_up_far = ring_far(*after(gate_up_close, (near_ax, near_by)))
    gate_up_ring = (*gate_up_close, *gate_up_far)

    other_tokens = core(after(own_tokens, near_ring))
    blocks = jnp.concatenate([own_tokens, other_tokens], 0).reshape(DEPTH, quarter + 16, D)
    all_tokens = blocks[:, :quarter].reshape(rows, D)
    all_extra = blocks[:, quarter:, :quarter].astype(F32)
    seg_all = all_extra[:, 0].reshape(rows)
    pos_all = (all_extra[:, 1] * 32.0 + all_extra[:, 2]).reshape(rows)
    lane = jnp.arange(PAIR)
    counter = (lane & (HEAD_DIM // 2 - 1)).astype(F32)
    inverse = jnp.exp(counter * (-2.0 * math.log(rotary_base) / HEAD_DIM))
    angles = pos_all[:, None] * inverse
    cosine = jnp.cos(angles)
    sine = jnp.where((lane & (HEAD_DIM - 1)) < HEAD_DIM // 2, -1.0, 1.0) * jnp.sin(angles)
    seg_col, seg_row = seg_all[:, None], seg_all[None, :]

    qkv_mat, out_half = place(
        (near_ax, across_y(near_ax), near_by, across_x(near_by)),
        [(SIDE, SIDE, 2, DEPTH, D_ROWS, Q_COLS), (SIDE, SIDE, 2, DEPTH, D_ROWS, OUT_COLS)],
        lambda y, x, k, z: [
            (n, (row, every, every, cols), r, ((y ^ n) ^ (k * r), row, 0))
            for n in both for row in both for r, cols in ((0, pl.ds(0, Q_COLS)), (1, pl.ds(Q_COLS, OUT_COLS)))
        ] + [
            (2 + n, (row, every, every, cols), r, (row ^ (k * r), x ^ n, 1))
            for n in both for row in both for r, cols in ((0, pl.ds(0, Q_COLS)), (1, pl.ds(Q_COLS, OUT_COLS)))
        ],
    )
    qkv_mat, out_half = qkv_mat.reshape(D, Q_COLS), out_half.reshape(D, OUT_COLS)
    out_other = core(out_half)
    swapped = jnp.concatenate([out_other[HALF_D:, :HALF_D], out_other[:HALF_D, :HALF_D]], axis=0)
    own_cols = out_half[:, :HALF_D]
    out_mat = jnp.concatenate(
        [jnp.where(k == 0, own_cols, swapped), jnp.where(k == 0, swapped, own_cols)], axis=1
    )
    norm_cols = out_half[:, HALF_D : HALF_D + 8].astype(F32)
    norm_cols = jnp.where(k == 0, norm_cols, jnp.roll(norm_cols, HALF_D, axis=0)).T
    gain_one, bias_one, gain_two, bias_two = (norm_cols[n] for n in range(4))

    gate_up_a, gate_up_b = after(spread_z(gate_up_block, gate_up_ring), qkv_mat)
    gate_up_ax = pair_x(gate_up_a, across_x(gate_up_a))
    gate_up_by = pair_y(gate_up_b, across_y(gate_up_b))
    down_close = ring_near(after(down_y, gate_up_far))

    token_half = all_tokens[:half].astype(F32)
    qkv = project_qkv(all_tokens, qkv_mat, cosine, sine)
    pairs = range(HALF_D // PAIR)
    attended, totals = [], []
    for pair in pairs:
        one, total = attend_pair(pair, qkv, seg_col, seg_row)
        attended.append(one)
        totals.append(total)
    gate_up_ax, gate_up_by = after((gate_up_ax, gate_up_by), attended[1])
    gate_up_mat = place(
        (gate_up_ax, across_y(gate_up_ax), gate_up_by, across_x(gate_up_by)),
        [(SIDE, SIDE, 2, DEPTH, D_ROWS, FF)],
        lambda y, x, k, z: [
            (n, (row,), 0, (y ^ n, row, 0)) for n in both for row in both
        ] + [(2 + n, (row,), 0, (row, x ^ n, 1)) for n in both for row in both],
    )[0].reshape(D, FF)
    down_ring = (*down_close, *ring_far(*after(down_close, attended[1])))
    first, second = pl.ds(0, planes // 2), pl.ds(planes // 2, planes // 2)
    down_mat = place(
        (down_y, *down_ring),
        [(planes, DEPTH, FF_ROWS, D)],
        lambda y, x, k, z: [
            (0, None, 0, (every, z)),
            (1, None, 0, (every, (z + 1) & 3)),
            (2, None, 0, (every, (z + 3) & 3)),
            (3, None, 0, (first, (z + 2) & 3)),
            (4, None, 0, (second, (z + 2) & 3)),
        ],
    )[0].reshape(FF_HALF, D)
    attended = jnp.concatenate(attended, axis=1)
    attended_rows = jnp.concatenate([attended[:half], core(attended[half:])], axis=1)
    branch = dot_nn(attended_rows, out_mat)
    normed_one, hat_one, recip_one = layer_norm(token_half + branch, gain_one, bias_one)
    normed_own = normed_one.astype(BF)
    normed_low = jnp.concatenate([normed_own, core(normed_own)], axis=0)
    grad_quarters = to_sequence(after(output_grad, down_mat), z)
    gate_up = dot_nn(normed_low, gate_up_mat)
    gate_part, up_part = gate_up[:, :FF_HALF], gate_up[:, FF_HALF:]
    sigmoid_gate = jax.nn.sigmoid(gate_part)
    silu_gate = gate_part * sigmoid_gate
    hidden = (silu_gate * up_part).astype(BF)

    def sum_cores(left, right):
        got = core(right(left[half:]).astype(BF))
        return right(left[:half]) + got.astype(F32)

    mlp_out = sum_cores(hidden, lambda part: dot_nn(part, down_mat))
    result, hat_two, recip_two = layer_norm(normed_one + mlp_out, gain_two, bias_two)
    result = result.astype(BF)
    output_got = from_sequence([result[:quarter], result[quarter:]])

    grad_half = jnp.concatenate(grad_quarters, axis=0).astype(F32)
    second_grad, second_gain_part, second_bias_part = norm_back(
        grad_half, hat_two, recip_two, gain_two
    )
    mlp_own = second_grad.astype(BF)
    mlp_grad = jnp.concatenate([mlp_own, core(mlp_own)], axis=0)
    hidden_grad = dot_nt(mlp_grad, down_mat)
    gate_grad = hidden_grad * up_part * (sigmoid_gate * (1.0 + gate_part * (1.0 - sigmoid_gate)))
    up_grad = hidden_grad * silu_gate
    gate_up_grad = jnp.concatenate([gate_grad, up_grad], axis=1).astype(BF)
    down_part = down_weight_part(hidden, mlp_grad)
    gate_up_part = gate_up_weight_part(normed_low, gate_up_grad)
    normed_grad = second_grad + sum_cores(gate_up_grad, lambda part: dot_nt(part, gate_up_mat))
    first_grad, first_gain_part, first_bias_part = norm_back(
        normed_grad, hat_one, recip_one, gain_one
    )
    branch_grad = first_grad.astype(BF)
    attended_own = dot_nt(branch_grad, out_mat).astype(BF)
    attended_grad = jnp.concatenate(
        [attended_own[:, :HALF_D], core(attended_own[:, HALF_D:])], axis=0
    )

    output_got = after(output_got, gate_up_part)
    output = order(z & 1, output_got[0], output_got[1])
    down_part = down_part.reshape(planes, DEPTH, FF_ROWS, D)
    down_far = scatter_far(down_part, z, 1)
    gate_up_part = gate_up_part.reshape(SIDE, SIDE, 2, DEPTH, D_ROWS, FF)
    part_a = scatter(gate_up_part[:, :, 0], x, across_x, 1)
    part_b = scatter(gate_up_part[:, :, 1], y, across_y, 0)
    down_near = scatter_near(down_part, z, 1, *down_far)
    down_z = scatter_own(down_part, z, 1, *down_near)
    attended_grad, part_a, part_b, down_z = lax.optimization_barrier(
        (attended_grad, part_a, part_b, down_z)
    )
    down_y = scatter(down_z.reshape(SIDE, SIDE, FF_ROWS, D), y, across_y)
    part_a = scatter(part_a, y, across_y)
    part_b = scatter(part_b, x, across_x)

    out_part = dot_tn(attended_rows, branch_grad)
    own_rows, other_rows = out_part[:HALF_D], out_part[HALF_D:]
    out_part = jnp.concatenate(
        [jnp.where(k == 0, own_rows, other_rows), jnp.where(k == 0, other_rows, own_rows)], axis=0
    )
    norm_part = jnp.stack([first_gain_part, first_bias_part, second_gain_part, second_bias_part])
    norm_part = jnp.pad(norm_part.T, ((0, 0), (0, NORM_COLS - 4)))
    left_cols, right_cols = out_part[:, :HALF_D], out_part[:, HALF_D:]
    keep = jnp.concatenate([jnp.where(k == 0, left_cols, right_cols), norm_part], axis=1)
    give = jnp.concatenate([jnp.where(k == 0, right_cols, left_cols), norm_part], axis=1)
    out_sum = (keep + core(give.astype(BF)).astype(F32)).astype(BF)

    projected_grad = None
    for pair in pairs:
        if pair == 1:
            attended_grad, down_y = lax.optimization_barrier((attended_grad, down_y))
        if pair == 2:
            attended_grad, part_a, part_b = lax.optimization_barrier((attended_grad, part_a, part_b))
        projected_grad = attend_back_pair(
            pair, projected_grad, qkv, attended_grad, totals[pair], seg_col, seg_row, cosine, sine
        )
    down_share = scatter(down_y, x, across_x).reshape(-1)
    gate_up_half = jnp.concatenate([part_a, part_b], axis=1)
    gate_up_far = scatter_far(gate_up_half, z, 0)
    near_part = near_weight_part(all_tokens, projected_grad, out_sum)
    near_part = near_part.reshape(SIDE, SIDE, 2, DEPTH, D_ROWS, NEAR_COLS)
    near_a = scatter(near_part[:, :, 0], x, across_x, 1)
    near_b = scatter(near_part[:, :, 1], y, across_y, 0)
    gate_up_near = scatter_near(gate_up_half, z, 0, *gate_up_far)
    near_a = scatter(near_a, y, across_y)
    near_b = scatter(near_b, x, across_x)
    near_half = jnp.concatenate([near_a, near_b], axis=1)
    near_sum = scatter_own(
        near_half, z, 0, *scatter_near(near_half, z, 0, *scatter_far(near_half, z, 0))
    ).reshape(2, D_ROWS, NEAR_COLS)
    gate_up_sum = scatter_own(gate_up_half, z, 0, *gate_up_near).reshape(2, D_ROWS, FF)
    gate_up_got = core(at(gate_up_sum, 1 - k).astype(BF)).astype(F32)
    gate_up_share = order(
        k,
        at(gate_up_sum, k).reshape(D_ROWS, 2 * planes, FF_COLS),
        gate_up_got.reshape(D_ROWS, 2 * planes, FF_COLS),
        2,
    ).reshape(-1)
    near_mine = at(near_sum, k)
    near_got = core(at(near_sum, 1 - k)[:, : Q_COLS + HALF_D].astype(BF)).astype(F32)
    qkv_share = order(
        k,
        near_mine[:, :Q_COLS].reshape(D_ROWS, 3, HALF_D),
        near_got[:, :Q_COLS].reshape(D_ROWS, 3, HALF_D),
        2,
    ).reshape(-1)
    out_share = order(k, near_mine[:, Q_COLS : Q_COLS + HALF_D], near_got[:, Q_COLS:], 1).reshape(-1)
    norm_share = near_mine[:, Q_COLS + HALF_D : Q_COLS + HALF_D + 4].T

    projected_grad = after(projected_grad, near_part)
    input_got = core(input_part(projected_grad, qkv_mat, 1, BF))
    input_half = first_grad + input_part(projected_grad, qkv_mat, 0, F32) + input_got.astype(F32)
    input_half = input_half.astype(BF)
    input_grad = from_sequence([input_half[:quarter], input_half[quarter:]])
    input_grad = order(z & 1, input_grad[0], input_grad[1]).astype(F32)
    return (
        output,
        input_grad,
        qkv_share,
        out_share,
        gate_up_share,
        down_share,
        norm_share[0],
        norm_share[1],
        norm_share[2],
        norm_share[3],
    )


def solution(mesh):
    in_specs = (
        P("dp", "ctx", None),
        P("dp", "ctx"),
        P("dp", "ctx"),
        P(("dp", "ctx")),
        P(("dp", "ctx")),
        P(("dp", "ctx")),
        P(("dp", "ctx")),
        P(("dp", "ctx")),
        P(("dp", "ctx")),
        P(("dp", "ctx")),
        P(("dp", "ctx")),
        P("dp", "ctx", None),
    )
    out_specs = (
        P("dp", "ctx", None),
        P("dp", "ctx", None),
        P(("dp", "ctx")),
        P(("dp", "ctx")),
        P(("dp", "ctx")),
        P(("dp", "ctx")),
        P(("dp", "ctx")),
        P(("dp", "ctx")),
        P(("dp", "ctx")),
        P(("dp", "ctx")),
    )
    fits = mesh.shape["dp"] == 8 and mesh.shape["ctx"] == 4
    body = chip_local if fits else local
    return jax.shard_map(body, mesh=mesh, in_specs=in_specs, out_specs=out_specs, check_vma=False)
```

```python
import math

import jax
import jax.numpy as jnp
from jax import lax
from jax.experimental import pallas as pl
from jax.experimental.pallas import tpu as pltpu
from jax.sharding import PartitionSpec as P

D = 768
HEADS = 12
HEAD_DIM = 64
FF = 3072


norm_epsilon = 1e-05
rotary_base = 1000.0
masked_score = -1000000000.0


def rotary_tables(positions, head_size):
    half_dim = head_size // 2
    counter = jnp.arange(half_dim, dtype=jnp.float32)
    inverse = jnp.exp(counter * (-2.0 * math.log(rotary_base) / head_size))
    angles = positions.astype(jnp.float32)[..., None] * inverse
    return (jnp.cos(angles)[..., None, :], jnp.sin(angles)[..., None, :])


def rotate(values, cosine_table, sine_table):
    half_dim = values.shape[-1] // 2
    first_half = values[..., :half_dim]
    second_half = values[..., half_dim:]
    return jnp.concatenate(
        [
            first_half * cosine_table - second_half * sine_table,
            second_half * cosine_table + first_half * sine_table,
        ],
        axis=-1,
    )


def rotate_back(grads, cosine_table, sine_table):
    half_dim = grads.shape[-1] // 2
    first_half = grads[..., :half_dim]
    second_half = grads[..., half_dim:]
    return jnp.concatenate(
        [
            first_half * cosine_table + second_half * sine_table,
            second_half * cosine_table - first_half * sine_table,
        ],
        axis=-1,
    )


def layer_norm(hidden_sum, gain, bias):
    average = jnp.mean(hidden_sum, axis=-1, keepdims=True)
    centered = hidden_sum - average
    variance = jnp.mean(centered * centered, axis=-1, keepdims=True)
    reciprocal = lax.rsqrt(variance + norm_epsilon)
    normed = centered * reciprocal
    return (normed * gain + bias, normed, reciprocal)


def norm_back(upstream, normed, reciprocal, gain):
    gain_grad = jnp.sum(upstream * normed, axis=0)
    bias_grad = jnp.sum(upstream, axis=0)
    normed_grad = upstream * gain
    input_part = reciprocal * (
        normed_grad
        - jnp.mean(normed_grad, axis=-1, keepdims=True)
        - normed * jnp.mean(normed_grad * normed, axis=-1, keepdims=True)
    )
    return (input_part, gain_grad, bias_grad)


def contract_rows(left, right):
    return lax.dot_general(
        left, right, (((0,), (0,)), ((), ())), preferred_element_type=jnp.float32
    )


def back_dot(left, right):
    return lax.dot_general(
        left, right, (((1,), (1,)), ((), ())), preferred_element_type=jnp.float32
    )


def unpack(gathered):
    qkv_flat, out_flat, gate_up_flat, down_flat, gain_one, bias_one, gain_two, bias_two = gathered
    return (
        qkv_flat.reshape(D, 3 * D),
        out_flat.reshape(D, D),
        gate_up_flat.reshape(D, 2 * FF),
        down_flat.reshape(FF, D),
        gain_one.astype(jnp.float32),
        bias_one.astype(jnp.float32),
        gain_two.astype(jnp.float32),
        bias_two.astype(jnp.float32),
    )


def head_slice(array, offset, lanes):
    piece = lax.dynamic_slice_in_dim(array, offset, lanes, 2)
    return piece.reshape(array.shape[0], array.shape[1], 2, HEAD_DIM)


def pair_logits(query_pair, key_pair, same_doc):
    scores = jnp.einsum("sqhd,skhd->shqk", query_pair, key_pair, preferred_element_type=jnp.float32)
    return jnp.where(same_doc, scores * 0.125, masked_score)


def attend(queries, keys_all, values_all, same_doc):
    seq_count, row_count, feature_count = queries.shape
    lanes = 2 * HEAD_DIM

    def pair_step(head_pair, buffers):
        out_buffer, total_buffer = buffers
        offset = head_pair * lanes
        logits = pair_logits(
            head_slice(queries, offset, lanes), head_slice(keys_all, offset, lanes), same_doc
        )
        highest = jnp.max(logits, axis=-1, keepdims=True)
        log_total = highest + jnp.log(jnp.sum(jnp.exp(logits - highest), axis=-1, keepdims=True))
        probs_low = jnp.exp(logits - log_total).astype(jnp.bfloat16)
        attended = jnp.einsum(
            "shqk,skhd->sqhd",
            probs_low,
            head_slice(values_all, offset, lanes),
            preferred_element_type=jnp.float32,
        ).astype(jnp.bfloat16)
        out_buffer = lax.dynamic_update_slice_in_dim(
            out_buffer, attended.reshape(seq_count, row_count, lanes), offset, 2
        )
        total_buffer = lax.dynamic_update_slice_in_dim(
            total_buffer, log_total[..., 0], 2 * head_pair, 1
        )
        return (out_buffer, total_buffer)

    initial = (
        jnp.zeros((seq_count, row_count, feature_count), jnp.bfloat16),
        jnp.zeros((seq_count, HEADS, row_count), jnp.float32),
    )
    return lax.fori_loop(0, HEADS // 2, pair_step, initial)


def attend_back(queries, keys_all, values_all, same_doc, total_buffer, attended_grad):
    seq_count, row_count, feature_count = queries.shape
    key_count = keys_all.shape[1]
    lanes = 2 * HEAD_DIM

    def pair_step(head_pair, buffers):
        query_buffer, key_buffer, value_buffer = buffers
        offset = head_pair * lanes
        query_pair = head_slice(queries, offset, lanes)
        key_pair = head_slice(keys_all, offset, lanes)
        value_pair = head_slice(values_all, offset, lanes)
        grad_pair = head_slice(attended_grad, offset, lanes)
        logits = pair_logits(query_pair, key_pair, same_doc)
        log_total = lax.dynamic_slice_in_dim(total_buffer, 2 * head_pair, 2, 1)
        probs = jnp.exp(logits - log_total[..., None])
        prob_grad = jnp.einsum(
            "sqhd,skhd->shqk", grad_pair, value_pair, preferred_element_type=jnp.float32
        )
        logit_grad = probs * (prob_grad - jnp.sum(probs * prob_grad, axis=-1, keepdims=True))
        score_grad = (logit_grad * 0.125).astype(jnp.bfloat16)
        query_part = jnp.einsum(
            "shqk,skhd->sqhd", score_grad, key_pair, preferred_element_type=jnp.float32
        )
        key_part = jnp.einsum(
            "shqk,sqhd->skhd", score_grad, query_pair, preferred_element_type=jnp.float32
        )
        value_part = jnp.einsum(
            "shqk,sqhd->skhd",
            probs.astype(jnp.bfloat16),
            grad_pair,
            preferred_element_type=jnp.float32,
        )
        query_buffer = lax.dynamic_update_slice_in_dim(
            query_buffer, query_part.reshape(seq_count, row_count, lanes), offset, 2
        )
        key_buffer = lax.dynamic_update_slice_in_dim(
            key_buffer, key_part.reshape(seq_count, key_count, lanes), offset, 2
        )
        value_buffer = lax.dynamic_update_slice_in_dim(
            value_buffer, value_part.reshape(seq_count, key_count, lanes), offset, 2
        )
        return (query_buffer, key_buffer, value_buffer)

    initial = (
        jnp.zeros((seq_count, row_count, feature_count), jnp.float32),
        jnp.zeros((seq_count, key_count, feature_count), jnp.float32),
        jnp.zeros((seq_count, key_count, feature_count), jnp.float32),
    )
    return lax.fori_loop(0, HEADS // 2, pair_step, initial)


def local(
    tokens,
    segments,
    positions,
    qkv_weight,
    out_weight,
    gate_up_weight,
    down_weight,
    first_gain,
    first_bias,
    second_gain,
    second_bias,
    output_grad,
):
    seq_count = tokens.shape[0]
    row_count = tokens.shape[1]
    gathered = (
        lax.all_gather(qkv_weight, ("dp", "ctx"), axis=0, tiled=True),
        lax.all_gather(out_weight, ("dp", "ctx"), axis=0, tiled=True),
        lax.all_gather(gate_up_weight, ("dp", "ctx"), axis=0, tiled=True),
        lax.all_gather(down_weight, ("dp", "ctx"), axis=0, tiled=True),
        lax.all_gather(first_gain, ("dp", "ctx"), axis=0, tiled=True),
        lax.all_gather(first_bias, ("dp", "ctx"), axis=0, tiled=True),
        lax.all_gather(second_gain, ("dp", "ctx"), axis=0, tiled=True),
        lax.all_gather(second_bias, ("dp", "ctx"), axis=0, tiled=True),
    )
    qkv_mat, out_mat, gate_up_mat, down_mat, gain_one, bias_one, gain_two, bias_two = unpack(
        gathered
    )
    token_rows = tokens.reshape(seq_count * row_count, D)
    cosine_table, sine_table = rotary_tables(positions, HEAD_DIM)
    projected = jnp.dot(token_rows, qkv_mat, preferred_element_type=jnp.float32)
    projected = projected.reshape(seq_count, row_count, 3, HEADS, HEAD_DIM)
    queries = (
        rotate(projected[:, :, 0], cosine_table, sine_table)
        .astype(jnp.bfloat16)
        .reshape(seq_count, row_count, D)
    )
    keys_low = (
        rotate(projected[:, :, 1], cosine_table, sine_table)
        .astype(jnp.bfloat16)
        .reshape(seq_count, row_count, D)
    )
    values_low = projected[:, :, 2].astype(jnp.bfloat16).reshape(seq_count, row_count, D)
    key_ids = segments.astype(jnp.bfloat16)
    keys_all, values_all, ids_all = (
        lax.all_gather(keys_low, "ctx", axis=1, tiled=True),
        lax.all_gather(values_low, "ctx", axis=1, tiled=True),
        lax.all_gather(key_ids, "ctx", axis=1, tiled=True),
    )
    same_doc = (
        segments.astype(jnp.float32)[:, None, :, None]
        == ids_all.astype(jnp.float32)[:, None, None, :]
    )
    attended, total_buffer = attend(queries, keys_all, values_all, same_doc)
    attended_rows = attended.reshape(seq_count * row_count, D)
    branch = jnp.dot(attended_rows, out_mat, preferred_element_type=jnp.float32)
    normed_one, hat_one, recip_one = layer_norm(
        token_rows.astype(jnp.float32) + branch, gain_one, bias_one
    )
    normed_low = normed_one.astype(jnp.bfloat16)
    gate_up = jnp.dot(normed_low, gate_up_mat, preferred_element_type=jnp.float32)
    gate_part = gate_up[:, :FF]
    up_part = gate_up[:, FF:]
    sigmoid_gate = jax.nn.sigmoid(gate_part)
    silu_gate = gate_part * sigmoid_gate
    hidden = (silu_gate * up_part).astype(jnp.bfloat16)
    mlp_out = jnp.dot(hidden, down_mat, preferred_element_type=jnp.float32)
    result, hat_two, recip_two = layer_norm(normed_one + mlp_out, gain_two, bias_two)
    output = result.astype(jnp.bfloat16).reshape(tokens.shape)
    again = (
        lax.all_gather(qkv_weight, ("dp", "ctx"), axis=0, tiled=True),
        lax.all_gather(out_weight, ("dp", "ctx"), axis=0, tiled=True),
        lax.all_gather(gate_up_weight, ("dp", "ctx"), axis=0, tiled=True),
        lax.all_gather(down_weight, ("dp", "ctx"), axis=0, tiled=True),
        lax.all_gather(first_gain, ("dp", "ctx"), axis=0, tiled=True),
        lax.all_gather(first_bias, ("dp", "ctx"), axis=0, tiled=True),
        lax.all_gather(second_gain, ("dp", "ctx"), axis=0, tiled=True),
        lax.all_gather(second_bias, ("dp", "ctx"), axis=0, tiled=True),
    )
    qkv_mat, out_mat, gate_up_mat, down_mat, gain_one, bias_one, gain_two, bias_two = unpack(again)
    keys_all, values_all, ids_all = (
        lax.all_gather(keys_low, "ctx", axis=1, tiled=True),
        lax.all_gather(values_low, "ctx", axis=1, tiled=True),
        lax.all_gather(key_ids, "ctx", axis=1, tiled=True),
    )
    upstream = output_grad.reshape(seq_count * row_count, D).astype(jnp.float32)
    second_grad, second_gain_part, second_bias_part = norm_back(
        upstream, hat_two, recip_two, gain_two
    )
    mlp_grad = second_grad.astype(jnp.bfloat16)
    down_part = contract_rows(hidden, mlp_grad)
    hidden_grad = back_dot(mlp_grad, down_mat)
    gate_grad = hidden_grad * up_part * (sigmoid_gate * (1.0 + gate_part * (1.0 - sigmoid_gate)))
    up_grad = hidden_grad * silu_gate
    gate_up_grad = jnp.concatenate([gate_grad, up_grad], axis=1).astype(jnp.bfloat16)
    gate_up_part = contract_rows(normed_low, gate_up_grad)
    gate_up_flat = gate_up_part.reshape(-1)
    early = (
        lax.psum_scatter(gate_up_flat, ("dp", "ctx"), scatter_dimension=0, tiled=True),
        lax.psum_scatter(second_gain_part, ("dp", "ctx"), scatter_dimension=0, tiled=True),
        lax.psum_scatter(second_bias_part, ("dp", "ctx"), scatter_dimension=0, tiled=True),
    )
    gate_up_share, gain_two_share, bias_two_share = early
    normed_grad = second_grad + back_dot(gate_up_grad, gate_up_mat)
    first_grad, first_gain_part, first_bias_part = norm_back(
        normed_grad, hat_one, recip_one, gain_one
    )
    branch_grad = first_grad.astype(jnp.bfloat16)
    out_part = contract_rows(attended_rows, branch_grad)
    attended_grad = (
        back_dot(branch_grad, out_mat).astype(jnp.bfloat16).reshape(seq_count, row_count, D)
    )
    query_grad, key_partial, value_partial = attend_back(
        queries, keys_all, values_all, same_doc, total_buffer, attended_grad
    )
    key_grad, value_grad = (
        lax.psum_scatter(
            key_partial.astype(jnp.bfloat16), "ctx", scatter_dimension=1, tiled=True
        ).astype(jnp.float32),
        lax.psum_scatter(
            value_partial.astype(jnp.bfloat16), "ctx", scatter_dimension=1, tiled=True
        ).astype(jnp.float32),
    )
    head_shape = (seq_count, row_count, HEADS, HEAD_DIM)
    query_raw = rotate_back(query_grad.reshape(head_shape), cosine_table, sine_table).reshape(-1, D)
    key_raw = rotate_back(key_grad.reshape(head_shape), cosine_table, sine_table).reshape(-1, D)
    projected_grad = jnp.concatenate(
        [query_raw, key_raw, value_grad.reshape(-1, D)], axis=1
    ).astype(jnp.bfloat16)
    qkv_part = contract_rows(token_rows, projected_grad)
    input_grad = (back_dot(projected_grad, qkv_mat) + first_grad).reshape(tokens.shape)
    qkv_flat = qkv_part.reshape(-1)
    out_flat = out_part.reshape(-1)
    down_flat = down_part.reshape(-1)
    late = (
        lax.psum_scatter(qkv_flat, ("dp", "ctx"), scatter_dimension=0, tiled=True),
        lax.psum_scatter(out_flat, ("dp", "ctx"), scatter_dimension=0, tiled=True),
        lax.psum_scatter(down_flat, ("dp", "ctx"), scatter_dimension=0, tiled=True),
        lax.psum_scatter(first_gain_part, ("dp", "ctx"), scatter_dimension=0, tiled=True),
        lax.psum_scatter(first_bias_part, ("dp", "ctx"), scatter_dimension=0, tiled=True),
    )
    qkv_share, out_share, down_share, gain_one_share, bias_one_share = late
    return (
        output,
        input_grad,
        qkv_share,
        out_share,
        gate_up_share,
        down_share,
        gain_one_share,
        bias_one_share,
        gain_two_share,
        bias_two_share,
    )


PAIR = 2 * HEAD_DIM
HALF_D = D // 2
LOG2E = 1.4426950408889634
BF = jnp.bfloat16
F32 = jnp.float32
AXES = ("dp", "ctx")
LIGHT = pl.CostEstimate(flops=1024, bytes_accessed=1024, transcendentals=0)
SIDE, DEPTH = 2, 4
OWNERS = 2 * SIDE * SIDE * DEPTH
D_ROWS, FF_ROWS = D // OWNERS, FF // OWNERS
FF_HALF = FF // 2
FF_COLS = FF_HALF // (SIDE * SIDE)
NORM_COLS = 128
OUT_COLS = HALF_D + NORM_COLS
Q_COLS = 3 * HALF_D
NEAR_COLS = Q_COLS + OUT_COLS


def dot_nn(left, right):
    return lax.dot_general(left, right, (((1,), (0,)), ((), ())), preferred_element_type=F32)


def dot_nt(left, right):
    return lax.dot_general(left, right, (((1,), (1,)), ((), ())), preferred_element_type=F32)


def dot_tn(left, right):
    return lax.dot_general(left, right, (((0,), (0,)), ((), ())), preferred_element_type=F32)


def swap_halves(tile):
    lane = lax.broadcasted_iota(jnp.int32, tile.shape, 1)
    low_half = lax.rem(lane, HEAD_DIM) < HEAD_DIM // 2
    ahead = pltpu.roll(tile, PAIR - HEAD_DIM // 2, 1)
    behind = pltpu.roll(tile, HEAD_DIM // 2, 1)
    return jnp.where(low_half, ahead, behind)


def qkv_body(x_ref, w_ref, cos_ref, sin_ref, o_ref):
    product = dot_nn(x_ref[...], w_ref[...])
    part = pl.program_id(0)

    @pl.when(part < 2)
    def _():
        for c in range(HALF_D // PAIR):
            tile = product[:, c * PAIR : (c + 1) * PAIR]
            turned = tile * cos_ref[...] + swap_halves(tile) * sin_ref[...]
            o_ref[:, c * PAIR : (c + 1) * PAIR] = turned.astype(BF)

    @pl.when(part == 2)
    def _():
        o_ref[...] = product.astype(BF)


def project_qkv(tokens, weight, cosine, sine):
    rows = tokens.shape[0]
    tile = rows
    return pl.pallas_call(
        qkv_body,
        out_shape=jax.ShapeDtypeStruct((rows, 3 * HALF_D), BF),
        grid=(3, rows // tile),
        in_specs=[
            pl.BlockSpec((tile, D), lambda i, r: (r, 0)),
            pl.BlockSpec((D, HALF_D), lambda i, r: (0, i)),
            pl.BlockSpec((tile, PAIR), lambda i, r: (r, 0)),
            pl.BlockSpec((tile, PAIR), lambda i, r: (r, 0)),
        ],
        out_specs=pl.BlockSpec((tile, HALF_D), lambda i, r: (r, i)),
        cost_estimate=LIGHT,
        compiler_params=pltpu.CompilerParams(vmem_limit_bytes=32 * 2**20),
        name="project_qkv",
    )(tokens, weight, cosine, sine)


Q_TILE = 256


def lane_head(shape):
    return lax.broadcasted_iota(jnp.int32, shape, 1) // HEAD_DIM


def row_head(shape):
    return lax.broadcasted_iota(jnp.int32, shape, 0) // HEAD_DIM


def attend_body(q_ref, k_ref, v_ref, segc_ref, segr_ref, o_ref, l_ref):
    keys = k_ref[...]
    values_t = v_ref[...].astype(F32).T.astype(BF)
    heads_down = row_head(values_t.shape)
    masked_values = [jnp.where(heads_down == h, values_t, jnp.zeros_like(values_t)) for h in range(2)]
    rows = q_ref.shape[0]
    scale = 0.125 * LOG2E
    for t in range(rows // Q_TILE):
        span = pl.ds(t * Q_TILE, Q_TILE)
        queries = q_ref[span, :]
        heads_across = lane_head(queries.shape)
        same = segc_ref[...] == segr_ref[:, span]
        total = jnp.zeros((PAIR, Q_TILE), F32)
        for h in range(2):
            scores = dot_nt(keys, jnp.where(heads_across == h, queries, jnp.zeros_like(queries)))
            scores = jnp.where(same, scores * scale, masked_score)
            highest = jnp.max(scores, axis=0, keepdims=True)
            weights = jnp.exp2(scores - highest)
            norm = jnp.sum(weights, axis=0, keepdims=True)
            l_ref[h : h + 1, span] = highest + jnp.log2(norm)
            total = total + dot_nn(masked_values[h], weights.astype(BF)) * (1.0 / norm)
        o_ref[span, :] = total.T.astype(BF)


def attend_pair(pair, qkv, seg_col, seg_row):
    rows = qkv.shape[0]
    pairs = HALF_D // PAIR
    return pl.pallas_call(
        attend_body,
        out_shape=(
            jax.ShapeDtypeStruct((rows, PAIR), BF),
            jax.ShapeDtypeStruct((8, rows), F32),
        ),
        grid=(1,),
        in_specs=[
            pl.BlockSpec((rows, PAIR), lambda i: (0, pair)),
            pl.BlockSpec((rows, PAIR), lambda i: (0, pairs + pair)),
            pl.BlockSpec((rows, PAIR), lambda i: (0, 2 * pairs + pair)),
            pl.BlockSpec((rows, 1), lambda i: (0, 0)),
            pl.BlockSpec((1, rows), lambda i: (0, 0)),
        ],
        out_specs=(
            pl.BlockSpec((rows, PAIR), lambda i: (0, 0)),
            pl.BlockSpec((8, rows), lambda i: (0, 0)),
        ),
        compiler_params=pltpu.CompilerParams(vmem_limit_bytes=40 * 2**20),
        cost_estimate=LIGHT,
        name="attend_pair",
    )(qkv, qkv, qkv, seg_col, seg_row)


def attend_back_body(
    q_ref, k_ref, v_ref, g_ref, l_ref, segc_ref, segr_ref, cos_ref, sin_ref, *others
):
    d_ref, dk_sum, dv_sum = others[-3:]
    keys = k_ref[...]
    values = v_ref[...]
    keys_t = keys.astype(F32).T.astype(BF)
    heads_down = row_head(keys_t.shape)
    masked_keys = [jnp.where(heads_down == h, keys_t, jnp.zeros_like(keys_t)) for h in range(2)]
    rows = q_ref.shape[0]
    scale = 0.125 * LOG2E
    for t in range(rows // Q_TILE):
        span = pl.ds(t * Q_TILE, Q_TILE)
        queries = q_ref[span, :]
        grads = g_ref[span, :]
        heads_across = lane_head(queries.shape)
        same = segc_ref[...] == segr_ref[:, span]
        dq_t = jnp.zeros((PAIR, Q_TILE), F32)
        dk_part = None
        dv_part = None
        for h in range(2):
            own_q = jnp.where(heads_across == h, queries, jnp.zeros_like(queries))
            own_g = jnp.where(heads_across == h, grads, jnp.zeros_like(grads))
            scores = dot_nt(keys, own_q)
            logits = jnp.where(same, scores * scale, masked_score)
            probs = jnp.exp2(logits - l_ref[h : h + 1, span])
            prob_grad = dot_nt(values, own_g)
            mixed = probs * prob_grad
            mean = jnp.sum(mixed, axis=0, keepdims=True)
            score_grad = (mixed - probs * mean).astype(BF)
            dv_new = dot_nn(probs.astype(BF), own_g)
            dk_new = dot_nn(score_grad, own_q)
            dv_part = dv_new if dv_part is None else dv_part + dv_new
            dk_part = dk_new if dk_part is None else dk_part + dk_new
            dq_t = dq_t + dot_nn(masked_keys[h], score_grad)
        if t == 0:
            dk_sum[...] = dk_part
            dv_sum[...] = dv_part
        else:
            dk_sum[...] += dk_part
            dv_sum[...] += dv_part
        dq = dq_t.T * 0.125
        d_ref[0, span, :] = (dq * cos_ref[span, :] - swap_halves(dq) * sin_ref[span, :]).astype(BF)
    dk = dk_sum[...] * 0.125
    d_ref[1] = (dk * cos_ref[...] - swap_halves(dk) * sin_ref[...]).astype(BF)
    d_ref[2] = dv_sum[...].astype(BF)


def attend_back_pair(pair, earlier, qkv, grads, totals, seg_col, seg_row, cosine, sine):
    rows = qkv.shape[0]
    pairs = HALF_D // PAIR
    column = pl.BlockSpec((rows, PAIR), lambda i: (0, pair))
    whole = pl.BlockSpec((rows, PAIR), lambda i: (0, 0))
    carried = [] if earlier is None else [earlier]
    return pl.pallas_call(
        attend_back_body,
        out_shape=jax.ShapeDtypeStruct((3, rows, HALF_D), BF),
        grid=(1,),
        in_specs=[
            column,
            pl.BlockSpec((rows, PAIR), lambda i: (0, pairs + pair)),
            pl.BlockSpec((rows, PAIR), lambda i: (0, 2 * pairs + pair)),
            column,
            pl.BlockSpec((8, rows), lambda i: (0, 0)),
            pl.BlockSpec((rows, 1), lambda i: (0, 0)),
            pl.BlockSpec((1, rows), lambda i: (0, 0)),
            whole,
            whole,
        ] + [pl.BlockSpec(memory_space=pl.ANY)] * len(carried),
        out_specs=pl.BlockSpec((3, rows, PAIR), lambda i: (0, 0, pair)),
        scratch_shapes=[pltpu.VMEM((rows, PAIR), F32), pltpu.VMEM((rows, PAIR), F32)],
        input_output_aliases={9: 0} if carried else {},
        compiler_params=pltpu.CompilerParams(vmem_limit_bytes=44 * 2**20),
        cost_estimate=LIGHT,
        name="attend_back_pair",
    )(qkv, qkv, qkv, grads, totals, seg_col, seg_row, cosine, sine, *carried)


def coordinates():
    place = lax.axis_index("dp")
    return place // (2 * SIDE), (place // 2) & 1, place & 1, lax.axis_index("ctx")


def whole(*shape):
    return pl.BlockSpec(shape, lambda *_: (0,) * len(shape))


def kernel(body, name, mebibytes, **arguments):
    return pl.pallas_call(
        body,
        compiler_params=pltpu.CompilerParams(vmem_limit_bytes=mebibytes * 2**20),
        cost_estimate=LIGHT,
        name=name,
        **arguments,
    )


def normalize(hidden_sum):
    centered = hidden_sum - jnp.mean(hidden_sum, axis=-1, keepdims=True)
    reciprocal = lax.rsqrt(jnp.mean(centered * centered, axis=-1, keepdims=True) + norm_epsilon)
    return centered * reciprocal, reciprocal


def norm_grad(upstream, normed, reciprocal, gain):
    grad = upstream * gain
    return reciprocal * (
        grad
        - jnp.mean(grad, axis=-1, keepdims=True)
        - normed * jnp.mean(grad * normed, axis=-1, keepdims=True)
    )


def add_sums(sums_ref, start, upstream, normed):
    first, second = pl.ds(start, 1), pl.ds(start + 1, 1)
    sums_ref[first, :] += jnp.sum(upstream * normed, axis=0, keepdims=True)
    sums_ref[second, :] += jnp.sum(upstream, axis=0, keepdims=True)


ROW_TILE = 256


def first_norm_body(a_ref, b_ref, w_ref, t_ref, p_ref, sum_ref, low_ref):
    total = t_ref[...].astype(F32)
    total = total + dot_nn(a_ref[...], w_ref[:HALF_D, :]) + dot_nn(b_ref[...], w_ref[HALF_D:, :])
    sum_ref[...] = total
    hat, _ = normalize(total)
    low_ref[...] = (hat * p_ref[0:1, :] + p_ref[1:2, :]).astype(BF)


def first_norm(attended_own, attended_got, out_mat, tokens, norms):
    rows = attended_own.shape[0]
    part = pl.BlockSpec((ROW_TILE, HALF_D), lambda i: (i, 0))
    full = pl.BlockSpec((ROW_TILE, D), lambda i: (i, 0))
    return kernel(
        first_norm_body,
        "first_norm",
        24,
        out_shape=(jax.ShapeDtypeStruct((rows, D), F32), jax.ShapeDtypeStruct((rows, D), BF)),
        grid=(rows // ROW_TILE,),
        in_specs=[part, part, whole(D, D), full, whole(8, D)],
        out_specs=(full, full),
    )(attended_own, attended_got, out_mat, tokens, norms)


FF_TILE = 256


def gate_up_body(x_ref, wg_ref, wu_ref, gate_ref, up_ref, h_ref):
    gate = dot_nn(x_ref[...], wg_ref[...])
    up_part = dot_nn(x_ref[...], wu_ref[...])
    gate_ref[...] = gate.astype(BF)
    up_ref[...] = up_part.astype(BF)
    h_ref[...] = (gate * lax.logistic(gate) * up_part).astype(BF)


def gate_up_forward(normed, weight):
    rows = normed.shape[0]
    tiles = FF_HALF // FF_TILE
    part = jax.ShapeDtypeStruct((rows, FF_HALF), BF)
    column = pl.BlockSpec((rows, FF_TILE), lambda i: (0, i))
    return kernel(
        gate_up_body,
        "gate_up_forward",
        24,
        out_shape=(part, part, part),
        grid=(tiles,),
        in_specs=[
            whole(rows, D),
            pl.BlockSpec((D, FF_TILE), lambda i: (0, i)),
            pl.BlockSpec((D, FF_TILE), lambda i: (0, tiles + i)),
        ],
        out_specs=(column, column, column),
    )(normed, weight, weight)


def second_norm_body(
    h_ref, w_ref, got_ref, sum_ref, p_ref, g_ref, result_ref, grad_ref, low_ref, sums_ref
):
    @pl.when(pl.program_id(0) == 0)
    def _():
        sums_ref[...] = jnp.zeros_like(sums_ref)

    hat, _ = normalize(sum_ref[...])
    total = hat * p_ref[0:1, :] + p_ref[1:2, :]
    total = total + dot_nn(h_ref[...], w_ref[...]) + got_ref[...].astype(F32)
    hat, reciprocal = normalize(total)
    gain = p_ref[2:3, :]
    result_ref[...] = (hat * gain + p_ref[3:4, :]).astype(BF)
    upstream = g_ref[...].astype(F32)
    add_sums(sums_ref, 2, upstream, hat)
    grad = norm_grad(upstream, hat, reciprocal, gain)
    grad_ref[...] = grad
    low_ref[...] = grad.astype(BF)


def second_norm(hidden, down_mat, got, first_sum, norms, output_grad):
    rows = hidden.shape[0]
    full = pl.BlockSpec((ROW_TILE, D), lambda i: (i, 0))
    return kernel(
        second_norm_body,
        "second_norm",
        32,
        out_shape=(
            jax.ShapeDtypeStruct((rows, D), BF),
            jax.ShapeDtypeStruct((rows, D), F32),
            jax.ShapeDtypeStruct((rows, D), BF),
            jax.ShapeDtypeStruct((8, D), F32),
        ),
        grid=(rows // ROW_TILE,),
        in_specs=[
            pl.BlockSpec((ROW_TILE, FF_HALF), lambda i: (i, 0)),
            whole(FF_HALF, D),
            full,
            full,
            whole(8, D),
            full,
        ],
        out_specs=(full, full, full, whole(8, D)),
    )(hidden, down_mat, got, first_sum, norms, output_grad)


def hidden_back_body(m_ref, w_ref, gate_ref, up_ref, o_ref):
    hidden_grad = dot_nt(m_ref[...], w_ref[...])
    gate, up_part = gate_ref[...].astype(F32), up_ref[...].astype(F32)
    sigmoid = lax.logistic(gate)
    o_ref[0] = (hidden_grad * up_part * (sigmoid * (1.0 + gate * (1.0 - sigmoid)))).astype(BF)
    o_ref[1] = (hidden_grad * (gate * sigmoid)).astype(BF)


def hidden_back(mlp_grad, down_mat, gate, up_part):
    rows = mlp_grad.shape[0]
    column = pl.BlockSpec((rows, FF_TILE), lambda i: (0, i))
    return kernel(
        hidden_back_body,
        "hidden_back",
        24,
        out_shape=jax.ShapeDtypeStruct((2, rows, FF_HALF), BF),
        grid=(FF_HALF // FF_TILE,),
        in_specs=[whole(rows, D), pl.BlockSpec((FF_TILE, D), lambda i: (i, 0)), column, column],
        out_specs=pl.BlockSpec((2, rows, FF_TILE), lambda i: (0, 0, i)),
    )(mlp_grad, down_mat, gate, up_part)


def normed_part_body(g_ref, w_ref, o_ref, acc_ref):
    product = dot_nt(g_ref[0], w_ref[...])
    step = pl.program_id(0)

    @pl.when(step == 0)
    def _():
        acc_ref[...] = product

    @pl.when(step > 0)
    def _():
        acc_ref[...] += product

    @pl.when(step == pl.num_programs(0) - 1)
    def _():
        o_ref[...] = acc_ref[...].astype(BF)


BACK_TILE = 768


def normed_part(grads, weight):
    rows = grads.shape[1]
    tiles = FF_HALF // BACK_TILE
    return kernel(
        normed_part_body,
        "normed_part",
        24,
        out_shape=jax.ShapeDtypeStruct((rows, D), BF),
        grid=(2 * tiles,),
        in_specs=[
            pl.BlockSpec((1, rows, BACK_TILE), lambda i: (i // tiles, 0, i % tiles)),
            pl.BlockSpec((D, BACK_TILE), lambda i: (0, i)),
        ],
        out_specs=whole(rows, D),
        scratch_shapes=[pltpu.VMEM((rows, D), F32)],
    )(grads, weight)


def first_back_body(
    g_ref, w_ref, got_ref, upper_ref, sum_ref, p_ref, out_ref, s_ref, grad_ref, own_ref, give_ref, sums_ref, acc_ref
):
    product = dot_nt(g_ref[0], w_ref[...])
    step = pl.program_id(0)

    @pl.when(step == 0)
    def _():
        acc_ref[...] = product

    @pl.when(step > 0)
    def _():
        acc_ref[...] += product

    @pl.when(step == pl.num_programs(0) - 1)
    def _():
        sums_ref[...] = s_ref[...]
        for n in range(acc_ref.shape[0] // ROW_TILE):
            span = pl.ds(n * ROW_TILE, ROW_TILE)
            upstream = acc_ref[span, :] + got_ref[span, :].astype(F32) + upper_ref[span, :]
            hat, reciprocal = normalize(sum_ref[span, :])
            add_sums(sums_ref, 0, upstream, hat)
            grad = norm_grad(upstream, hat, reciprocal, p_ref[0:1, :])
            grad_ref[span, :] = grad
            low = grad.astype(BF)
            own_ref[span, :] = dot_nt(low, out_ref[:HALF_D, :]).astype(BF)
            give_ref[span, :] = dot_nt(low, out_ref[HALF_D:, :]).astype(BF)


def first_back(grads, weight, got, second_grad, first_sum, norms, out_mat, sums):
    rows = grads.shape[1]
    tiles = FF_HALF // BACK_TILE
    part = jax.ShapeDtypeStruct((rows, HALF_D), BF)
    return kernel(
        first_back_body,
        "first_back",
        40,
        out_shape=(
            jax.ShapeDtypeStruct((rows, D), F32),
            part,
            part,
            jax.ShapeDtypeStruct((8, D), F32),
        ),
        grid=(2 * tiles,),
        in_specs=[
            pl.BlockSpec((1, rows, BACK_TILE), lambda i: (i // tiles, 0, i % tiles)),
            pl.BlockSpec((D, BACK_TILE), lambda i: (0, i)),
            whole(rows, D),
            whole(rows, D),
            whole(rows, D),
            whole(8, D),
            whole(D, D),
            whole(8, D),
        ],
        out_specs=(whole(rows, D), whole(rows, HALF_D), whole(rows, HALF_D), whole(8, D)),
        scratch_shapes=[pltpu.VMEM((rows, D), F32)],
    )(grads, weight, got, second_grad, first_sum, norms, out_mat, sums)


def out_part_body(a_ref, b_ref, g_ref, s_ref, keep_ref, give_ref):
    _, _, k, _ = coordinates()
    low = g_ref[...].astype(BF)
    parts = [dot_tn(a_ref[...], low), dot_tn(b_ref[...], low)]
    pad = jnp.zeros((NORM_COLS - 8, D), F32)
    sums = jnp.concatenate([s_ref[...], pad], axis=0).T
    for n in range(2):
        rows = jnp.where(k == n, parts[0], parts[1])
        left, right = rows[:, :HALF_D], rows[:, HALF_D:]
        span = slice(n * HALF_D, (n + 1) * HALF_D)
        keep_ref[span, :HALF_D] = jnp.where(k == 0, left, right)
        give_ref[span, :HALF_D] = jnp.where(k == 0, right, left).astype(BF)
    keep_ref[:, HALF_D:] = sums
    give_ref[:, HALF_D:] = sums.astype(BF)


def out_weight_part(attended_own, attended_got, first_grad, sums):
    rows = attended_own.shape[0]
    return kernel(
        out_part_body,
        "out_weight_part",
        32,
        out_shape=(
            jax.ShapeDtypeStruct((D, OUT_COLS), F32),
            jax.ShapeDtypeStruct((D, OUT_COLS), BF),
        ),
    )(attended_own, attended_got, first_grad, sums)


CHUNK = DEPTH * D_ROWS


def store_split(product, x, y, a_keep, a_send, b_keep, b_send, span=slice(None)):
    def block(yy, xx, kk):
        start = ((yy * SIDE + xx) * 2 + kk) * CHUNK
        return product[start : start + CHUNK]

    for n in range(2):
        a_keep[n, :, span] = jnp.where(x == 0, block(n, 0, 0), block(n, 1, 0))
        a_send[n, :, span] = jnp.where(x == 0, block(n, 1, 0), block(n, 0, 0))
        b_keep[n, :, span] = jnp.where(y == 0, block(0, n, 1), block(1, n, 1))
        b_send[n, :, span] = jnp.where(y == 0, block(1, n, 1), block(0, n, 1))


def second_split_body(a_ref, a_got, b_ref, b_got, a_keep, a_send, b_keep, b_send):
    y, x, _, _ = coordinates()
    for own, got, keep, send, index in (
        (a_ref, a_got, a_keep, a_send, y),
        (b_ref, b_got, b_keep, b_send, x),
    ):
        keep[...] = own[index].astype(F32) + got[index].astype(F32)
        send[...] = (own[1 - index].astype(F32) + got[1 - index].astype(F32)).astype(BF)


def second_split(a_keep, a_got, b_keep, b_got):
    cols = a_keep.shape[-1]
    keep, send = (jax.ShapeDtypeStruct((CHUNK, cols), kind) for kind in (F32, BF))
    return kernel(second_split_body, "second_split", 32, out_shape=(keep, send, keep, send))(
        a_keep, a_got, b_keep, b_got
    )


def far_split_body(a_ref, a_got, b_ref, b_got, sum_ref, up_ref, down_ref):
    _, _, _, z = coordinates()
    for n, (own, got) in enumerate(((a_ref, a_got), (b_ref, b_got))):
        total = own[...] + got[...].astype(F32)
        for m in range(DEPTH):
            sum_ref[m, n] = total[m * D_ROWS : (m + 1) * D_ROWS]
    far = (z + 2) & 3
    up_ref[...] = sum_ref[far, 0].astype(BF)
    down_ref[...] = sum_ref[far, 1].astype(BF)


def far_split(a_keep, a_got, b_keep, b_got):
    cols = a_keep.shape[-1]
    send = jax.ShapeDtypeStruct((D_ROWS, cols), BF)
    return kernel(
        far_split_body,
        "far_split",
        32,
        out_shape=(jax.ShapeDtypeStruct((DEPTH, 2, D_ROWS, cols), F32), send, send),
    )(a_keep, a_got, b_keep, b_got)


def close_split_body(sum_ref, first_ref, second_ref, up_ref, down_ref):
    _, _, _, z = coordinates()
    above, below = (z + 1) & 3, (z + 3) & 3
    up_ref[0] = (sum_ref[above, 0] + first_ref[...].astype(F32)).astype(BF)
    up_ref[1] = sum_ref[above, 1].astype(BF)
    down_ref[0] = sum_ref[below, 0].astype(BF)
    down_ref[1] = (sum_ref[below, 1] + second_ref[...].astype(F32)).astype(BF)


def close_split(sums, first, second):
    send = jax.ShapeDtypeStruct(sums.shape[1:], BF)
    return kernel(close_split_body, "close_split", 24, out_shape=(send, send))(sums, first, second)


def core_split_body(sum_ref, up_ref, down_ref, keep_ref, send_ref):
    _, _, k, z = coordinates()

    def total(index):
        return sum_ref[z, index] + up_ref[index].astype(F32) + down_ref[index].astype(F32)

    keep_ref[...] = total(k)
    send_ref[...] = total(1 - k)[:, : send_ref.shape[1]].astype(BF)


def core_split(sums, from_below, from_above, give_cols):
    return kernel(
        core_split_body,
        "core_split",
        24,
        out_shape=(
            jax.ShapeDtypeStruct(sums.shape[2:], F32),
            jax.ShapeDtypeStruct((D_ROWS, give_cols), BF),
        ),
    )(sums, from_below, from_above)


def near_part_body(x_ref, g_ref, out_ref, got_ref, a_keep, a_send, b_keep, b_send):
    y, x, _, _ = coordinates()
    outs = (a_keep, a_send, b_keep, b_send)
    for n in range(3):
        product = dot_tn(x_ref[...], g_ref[n]).astype(BF)
        store_split(product, x, y, *outs, span=slice(n * HALF_D, (n + 1) * HALF_D))
    rest = (out_ref[...] + got_ref[...].astype(F32)).astype(BF)
    store_split(rest, x, y, *outs, span=slice(Q_COLS, NEAR_COLS))


def near_weight_part(tokens, grads, out_keep, out_got):
    part = jax.ShapeDtypeStruct((SIDE, CHUNK, NEAR_COLS), BF)
    return kernel(near_part_body, "near_weight_part", 40, out_shape=(part,) * 4)(
        tokens, grads, out_keep, out_got
    )


def gate_up_part_body(x_ref, y_ref, g_ref, h_ref, *outs):
    y, x, _, _ = coordinates()
    product = (dot_tn(x_ref[...], g_ref[0]) + dot_tn(y_ref[...], h_ref[0])).astype(BF)
    store_split(product, x, y, *outs)


def row_sum_body(x_ref, y_ref, g_ref, h_ref, o_ref):
    o_ref[...] = (dot_tn(x_ref[...], g_ref[...]) + dot_tn(y_ref[...], h_ref[...])).astype(BF)


def gate_up_weight_part(normed, grads):
    rows, tile = normed[0].shape[0], 512
    tiles = FF_HALF // tile
    column = pl.BlockSpec((1, rows, tile), lambda i: (i // tiles, 0, i % tiles))
    return kernel(
        gate_up_part_body,
        "gate_up_weight_part",
        24,
        out_shape=(jax.ShapeDtypeStruct((SIDE, CHUNK, FF), BF),) * 4,
        grid=(FF // tile,),
        in_specs=[whole(rows, D), whole(rows, D), column, column],
        out_specs=(pl.BlockSpec((SIDE, CHUNK, tile), lambda i: (0, 0, i)),) * 4,
    )(*normed, *grads)


def down_weight_part(hidden, grads):
    rows, tile = hidden[0].shape[0], 512
    column = pl.BlockSpec((rows, tile), lambda i: (0, i))
    return kernel(
        row_sum_body,
        "down_weight_part",
        24,
        out_shape=jax.ShapeDtypeStruct((FF_HALF, D), BF),
        grid=(FF_HALF // tile,),
        in_specs=[column, column, whole(rows, D), whole(rows, D)],
        out_specs=pl.BlockSpec((tile, D), lambda i: (i, 0)),
    )(*hidden, *grads)


def input_part_body(g_ref, w_ref, o_ref):
    total = dot_nt(g_ref[0], w_ref[:, :HALF_D])
    for n in range(1, 3):
        total = total + dot_nt(g_ref[n], w_ref[:, n * HALF_D : (n + 1) * HALF_D])
    o_ref[...] = total.astype(o_ref.dtype)


def input_part(grads, weight, block, dtype):
    rows = grads.shape[1] // 2
    return pl.pallas_call(
        input_part_body,
        out_shape=jax.ShapeDtypeStruct((rows, D), dtype),
        grid=(1,),
        in_specs=[
            pl.BlockSpec((3, rows, HALF_D), lambda i: (0, block, 0)),
            pl.BlockSpec((D, 3 * HALF_D), lambda i: (0, 0)),
        ],
        out_specs=pl.BlockSpec((rows, D), lambda i: (0, 0)),
        compiler_params=pltpu.CompilerParams(vmem_limit_bytes=24 * 2**20),
        cost_estimate=LIGHT,
        name="input_part",
    )(grads, weight)


def at(array, index, axis=0):
    return lax.dynamic_index_in_dim(array, index, axis, keepdims=False)


def after(value, earlier):
    return lax.optimization_barrier((value, earlier))[0]


def place(pieces, shapes, moves):
    dtype = pieces[0].dtype
    count = len(moves(0, 0, 0, 0))
    inputs = len(pieces)

    def body(*refs):
        sources, results, sems = refs[:inputs], refs[inputs:-1], refs[-1]
        copies = []
        for n, (piece, part, result, spot) in enumerate(moves(*coordinates())):
            source = sources[piece] if part is None else sources[piece].at[part]
            copies.append(pltpu.make_async_copy(source, results[result].at[spot], sems.at[n]))
        for copy in copies:
            copy.start()
        for copy in copies:
            copy.wait()

    anywhere = pl.BlockSpec(memory_space=pl.ANY)
    size = sum(math.prod(shape) for shape in shapes) * 2 * jnp.dtype(dtype).itemsize
    return pl.pallas_call(
        body,
        out_shape=tuple(jax.ShapeDtypeStruct(shape, dtype) for shape in shapes),
        in_specs=[anywhere] * inputs,
        out_specs=tuple(pl.BlockSpec(memory_space=pltpu.VMEM) for _ in shapes),
        scratch_shapes=[pltpu.SemaphoreType.DMA((count,))],
        compiler_params=pltpu.CompilerParams(vmem_limit_bytes=max(8 * 2**20, 2 * size)),
        cost_estimate=LIGHT,
        name="place",
    )(*pieces)


def move(array, target):
    pairs = []
    for y in range(SIDE):
        for x in range(SIDE):
            for k in range(2):
                for z in range(DEPTH):
                    ty, tx, tk, tz = target(y, x, k, z)
                    source = ((y * SIDE + x) * 2 + k) * DEPTH + z
                    goal = ((ty * SIDE + tx) * 2 + tk) * DEPTH + tz % DEPTH
                    pairs.append((source, goal))
    return lax.ppermute(array, AXES, pairs)


def core(array):
    return move(array, lambda y, x, k, z: (y, x, 1 - k, z))


def across_x(array):
    return move(array, lambda y, x, k, z: (y, 1 - x, k, z))


def across_y(array):
    return move(array, lambda y, x, k, z: (1 - y, x, k, z))


def up(array):
    return move(array, lambda y, x, k, z: (y, x, k, z + 1))


def down(array):
    return move(array, lambda y, x, k, z: (y, x, k, z - 1))


def order(index, own, other, axis=0):
    first = jnp.where(index == 0, own, other)
    second = jnp.where(index == 0, other, own)
    return jnp.stack([first, second], axis)


def ring_near(array):
    return down(array), up(array)


def ring_far(above, below):
    half = above.shape[0] // 2
    return up(below[:half]), down(above[half:])


def pair_x(array, got):
    return place(
        (array, got), [(SIDE, *array.shape)], lambda y, x, k, z: [(n, None, 0, (x ^ n,)) for n in range(2)]
    )[0]


def pair_y(array, got):
    return place(
        (array, got), [(SIDE, *array.shape)], lambda y, x, k, z: [(n, None, 0, (y ^ n,)) for n in range(2)]
    )[0]


def spread_z(block, pieces):
    both = range(2)
    return place(
        (block, *pieces),
        [(DEPTH, *block.shape[1:])] * 2,
        lambda y, x, k, z: [
            (n, (m,), m, ((z + step) & 3,)) for n, step in ((0, 0), (1, 1), (2, 3)) for m in both
        ] + [(3 + m, (0,), m, ((z + 2) & 3,)) for m in both],
    )


def scatter(array, index, across, axis=0, gate=None):
    got = across(at(array, 1 - index, axis).astype(BF))
    if gate is not None:
        got = after(got, gate)
    return at(array, index, axis).astype(F32) + got.astype(F32)


def scatter_far(array, z, axis):
    far = at(array, (z + 2) & 3, axis).astype(BF)
    half = far.shape[0] // 2
    return up(far[:half]), down(far[half:])


def scatter_near(array, z, axis, first, second):
    above, below = at(array, (z + 1) & 3, axis), at(array, (z + 3) & 3, axis)
    half = above.shape[0] // 2
    sum_above = (above[:half].astype(F32) + first.astype(F32)).astype(BF)
    sum_below = (below[half:].astype(F32) + second.astype(F32)).astype(BF)
    got_a = up(jnp.concatenate([sum_above, above[half:].astype(BF)], 0))
    got_b = down(jnp.concatenate([below[:half].astype(BF), sum_below], 0))
    return got_a, got_b


def scatter_own(array, z, axis, got_a, got_b):
    return at(array, z, axis).astype(F32) + got_a.astype(F32) + got_b.astype(F32)


def sequence_step(r):
    return lambda y, x, k, z: (y, x, z // 2, 2 * k + ((r + z) & 1))


def to_sequence(blocks, z):
    return [move(at(blocks, (z + r) & 1), sequence_step(r)) for r in range(2)]


def from_sequence(quarters):
    return [move(quarters[r], sequence_step(r)) for r in range(2)]


def chip_local(
    tokens,
    segments,
    positions,
    qkv_weight,
    out_weight,
    gate_up_weight,
    down_weight,
    first_gain,
    first_bias,
    second_gain,
    second_bias,
    output_grad,
):
    y, x, k, z = coordinates()
    quarter = tokens.shape[1]
    rows = DEPTH * quarter
    half = rows // 2
    planes = SIDE * SIDE

    norms = jnp.stack([first_gain, first_bias, second_gain, second_bias], axis=1)
    norms = jnp.pad(norms, ((0, 0), (0, NORM_COLS - 4)))
    qkv_own = qkv_weight.reshape(D_ROWS, 3 * D)
    gate_up_own = gate_up_weight.reshape(D_ROWS, 2 * FF)
    out_own = out_weight.reshape(D_ROWS, D)

    def column_half(index):
        def part(matrix, start, width):
            left, right = matrix[:, start : start + width], matrix[:, start + width : start + 2 * width]
            return jnp.where(index == 0, left, right)

        pieces = [part(qkv_own, n * D, HALF_D) for n in range(3)]
        pieces += [part(out_own, 0, HALF_D), norms]
        pieces += [part(gate_up_own, n * 2 * FF_COLS, FF_COLS) for n in range(2 * planes)]
        return jnp.concatenate(pieces, axis=1)

    mine, theirs = column_half(k), core(column_half(1 - k))
    both, every = range(2), slice(None)
    near_span, gate_up_span = pl.ds(0, NEAR_COLS), pl.ds(NEAR_COLS, FF)
    near_block, gate_up_block = place(
        (mine, theirs),
        [(2, D_ROWS, NEAR_COLS), (2, D_ROWS, FF)],
        lambda y, x, k, z: [
            (n, (every, span), r, (k ^ n,)) for n in both for r, span in enumerate((near_span, gate_up_span))
        ],
    )

    near_close = ring_near(near_block)
    near_ring = (*near_close, *ring_far(*near_close))
    near_a, near_b = spread_z(near_block, near_ring)
    down_x = down_weight.reshape(FF_ROWS, D)
    down_x = pair_x(down_x, across_x(down_x))
    near_a, near_b, down_x = lax.optimization_barrier((near_a, near_b, down_x))
    near_ax = pair_x(near_a, across_x(near_a))
    near_by = pair_y(near_b, across_y(near_b))
    down_x = (down_x, across_y(down_x))
    gate_up_close = ring_near(after(gate_up_block, near_ring))
    gate_up_far = ring_far(*gate_up_close)

    extra = jnp.stack([segments, positions >> 5, positions & 31], axis=1).astype(BF)
    extra = jnp.pad(extra, ((0, 0), (0, 13), (0, D - quarter)))
    packed = after(jnp.concatenate([tokens, extra], axis=1), gate_up_far[0])
    own_tokens = jnp.concatenate(to_sequence(packed, z), axis=0)
    other_tokens = core(own_tokens)
    blocks = jnp.concatenate([own_tokens, other_tokens], 0).reshape(DEPTH, quarter + 16, D)
    all_tokens = blocks[:, :quarter].reshape(rows, D)
    all_extra = blocks[:, quarter:, :quarter].astype(F32)
    seg_all = all_extra[:, 0].reshape(rows)
    pos_all = (all_extra[:, 1] * 32.0 + all_extra[:, 2]).reshape(rows)
    lane = jnp.arange(PAIR)
    counter = (lane & (HEAD_DIM // 2 - 1)).astype(F32)
    inverse = jnp.exp(counter * (-2.0 * math.log(rotary_base) / HEAD_DIM))
    angles = pos_all[:, None] * inverse
    cosine = jnp.cos(angles)
    sine = jnp.where((lane & (HEAD_DIM - 1)) < HEAD_DIM // 2, -1.0, 1.0) * jnp.sin(angles)
    seg_col, seg_row = seg_all[:, None], seg_all[None, :]

    qkv_mat, out_half = place(
        (near_ax, across_y(near_ax), near_by, across_x(near_by)),
        [(SIDE, SIDE, 2, DEPTH, D_ROWS, Q_COLS), (SIDE, SIDE, 2, DEPTH, D_ROWS, OUT_COLS)],
        lambda y, x, k, z: [
            (n, (row, every, every, cols), r, ((y ^ n) ^ (k * r), row, 0))
            for n in both for row in both for r, cols in ((0, pl.ds(0, Q_COLS)), (1, pl.ds(Q_COLS, OUT_COLS)))
        ] + [
            (2 + n, (row, every, every, cols), r, (row ^ (k * r), x ^ n, 1))
            for n in both for row in both for r, cols in ((0, pl.ds(0, Q_COLS)), (1, pl.ds(Q_COLS, OUT_COLS)))
        ],
    )
    qkv_mat, out_half = qkv_mat.reshape(D, Q_COLS), out_half.reshape(D, OUT_COLS)

    out_other = core(out_half)
    swapped = jnp.concatenate([out_other[HALF_D:, :HALF_D], out_other[:HALF_D, :HALF_D]], axis=0)
    own_cols = out_half[:, :HALF_D]
    out_mat = jnp.concatenate(
        [jnp.where(k == 0, own_cols, swapped), jnp.where(k == 0, swapped, own_cols)], axis=1
    )
    norms_all = out_half[:, HALF_D : HALF_D + 8].astype(F32)
    norms_all = jnp.where(k == 0, norms_all, jnp.roll(norms_all, HALF_D, axis=0)).T

    gate_up_a, gate_up_b = spread_z(gate_up_block, (*gate_up_close, *gate_up_far))
    gate_up_ax = pair_x(gate_up_a, across_x(gate_up_a))
    gate_up_by = pair_y(gate_up_b, across_y(gate_up_b))

    token_half = all_tokens[:half]
    all_tokens, gate_up_ax, gate_up_by = lax.optimization_barrier((all_tokens, gate_up_ax, gate_up_by))
    qkv = project_qkv(all_tokens, qkv_mat, cosine, sine)
    down_y = pair_y(*after(down_x, qkv)).reshape(planes, FF_ROWS, D)
    down_close = ring_near(down_y)
    pairs = range(HALF_D // PAIR)
    attended, totals = [], []
    for pair in pairs:
        if pair:
            qkv, attended[-1] = lax.optimization_barrier((qkv, attended[-1]))
        one, total = attend_pair(pair, qkv, seg_col, seg_row)
        attended.append(one)
        totals.append(total)
    gate_up_mat = place(
        (gate_up_ax, across_y(gate_up_ax), gate_up_by, across_x(gate_up_by)),
        [(SIDE, SIDE, 2, DEPTH, D_ROWS, FF)],
        lambda y, x, k, z: [
            (n, (row,), 0, (y ^ n, row, 0)) for n in both for row in both
        ] + [(2 + n, (row,), 0, (row, x ^ n, 1)) for n in both for row in both],
    )[0].reshape(D, FF)
    attended = jnp.concatenate(attended, axis=1)
    attended_own, attended_got = attended[:half], core(attended[half:])
    down_ring = (*down_close, *ring_far(*after(down_close, attended_got)))
    first, second = pl.ds(0, planes // 2), pl.ds(planes // 2, planes // 2)
    first_sum, normed_own = first_norm(attended_own, attended_got, out_mat, token_half, norms_all)
    normed_got = core(normed_own)
    gate_own, up_own, hidden_own = gate_up_forward(normed_own, gate_up_mat)
    gate_got, up_got, hidden_got = gate_up_forward(after(normed_got, hidden_own), gate_up_mat)
    grad_quarters = to_sequence(after(output_grad, gate_up_mat), z)
    down_ring = after(down_ring, hidden_got)
    down_mat = place(
        (down_y, *down_ring),
        [(planes, DEPTH, FF_ROWS, D)],
        lambda y, x, k, z: [
            (0, None, 0, (every, z)),
            (1, None, 0, (every, (z + 1) & 3)),
            (2, None, 0, (every, (z + 3) & 3)),
            (3, None, 0, (first, (z + 2) & 3)),
            (4, None, 0, (second, (z + 2) & 3)),
        ],
    )[0].reshape(FF_HALF, D)
    mlp_got = core(dot_nn(hidden_got, down_mat).astype(BF))
    grad_half = jnp.concatenate(grad_quarters, axis=0)
    result, second_grad, mlp_own, sums = second_norm(
        hidden_own, down_mat, mlp_got, first_sum, norms_all, grad_half
    )

    other_grad = core(mlp_own)
    output_got = from_sequence([result[:quarter], result[quarter:]])
    gate_up_own = hidden_back(mlp_own, down_mat, gate_own, up_own)
    gate_up_other = hidden_back(after(other_grad, gate_up_own), down_mat, gate_got, up_got)
    normed_back = normed_part(gate_up_other, gate_up_mat)
    normed_got_back = core(normed_back)
    down_part = down_weight_part((hidden_own, hidden_got), (mlp_own, after(other_grad, normed_back)))
    gate_up_part = gate_up_weight_part(
        (normed_own, normed_got), (gate_up_own, after(gate_up_other, down_part))
    )
    first_grad, attended_mine, attended_give, sums = first_back(
        gate_up_own,
        gate_up_mat,
        after(normed_got_back, (gate_up_part, output_got)),
        second_grad,
        first_sum,
        norms_all,
        out_mat,
        sums,
    )
    attended_grad = jnp.concatenate([attended_mine, core(attended_give)], axis=0)

    output = order(z & 1, output_got[0], output_got[1])
    down_part = down_part.reshape(planes, DEPTH, FF_ROWS, D)
    down_far = scatter_far(down_part, z, 1)
    down_near = scatter_near(down_part, z, 1, *after(down_far, first_grad))
    far_ak, far_as, far_bk, far_bs = gate_up_part
    far_as, far_bs = across_x(far_as), across_y(far_bs)

    out_keep, out_give = out_weight_part(attended_own, attended_got, first_grad, sums)
    out_got = core(out_give)

    projected_grad = None
    for pair in pairs:
        if pair == 1:
            far_as, far_bs = after((far_as, far_bs), projected_grad)
            far_ak, far_as, far_bk, far_bs = second_split(far_ak, far_as, far_bk, far_bs)
            attended_grad, far_ak, projected_grad = lax.optimization_barrier(
                (attended_grad, far_ak, projected_grad)
            )
            far_as, far_bs = across_y(far_as), across_x(far_bs)
        if pair == 2:
            far_as, far_bs, down_near = after((far_as, far_bs, down_near), projected_grad)
            down_z = scatter_own(down_part, z, 1, *down_near)
            far_sum, far_up, far_down = far_split(far_ak, far_as, far_bk, far_bs)
            attended_grad, far_sum, down_z, projected_grad = lax.optimization_barrier(
                (attended_grad, far_sum, down_z, projected_grad)
            )
            far_up, far_down = up(far_up), down(far_down)
            down_y = across_y(at(down_z.reshape(SIDE, SIDE, FF_ROWS, D), 1 - y).astype(BF))
        projected_grad = attend_back_pair(
            pair, projected_grad, qkv, attended_grad, totals[pair], seg_col, seg_row, cosine, sine
        )
    far_up, far_down, down_y = after((far_up, far_down, down_y), projected_grad)
    down_y = at(down_z.reshape(SIDE, SIDE, FF_ROWS, D), y) + down_y.astype(F32)
    far_up, far_down = close_split(far_sum, far_up, far_down)
    input_give = input_part(projected_grad, qkv_mat, 1, BF)
    projected_grad, far_up, far_down, input_give = lax.optimization_barrier(
        (projected_grad, far_up, far_down, input_give)
    )
    far_up, far_down = up(far_up), down(far_down)
    input_got = core(input_give)
    near_ak, near_as, near_bk, near_bs = near_weight_part(
        all_tokens, projected_grad, out_keep, out_got
    )
    near_as, near_bs = across_x(near_as), across_y(near_bs)
    input_own = input_part(after(projected_grad, near_ak), qkv_mat, 0, F32)
    input_half = (first_grad + input_own + input_got.astype(F32)).astype(BF)
    near_as, near_bs = after((near_as, near_bs), input_half)
    near_ak, near_as, near_bk, near_bs = second_split(near_ak, near_as, near_bk, near_bs)
    near_as, near_bs = across_y(near_as), across_x(near_bs)
    down_x = after(across_x(at(down_y, 1 - x).astype(BF)), near_ak)
    down_share = (at(down_y, x) + down_x.astype(F32)).reshape(-1)
    far_up, far_down = after((far_up, far_down), near_ak)
    far_own, far_give = core_split(far_sum, far_up, far_down, FF)
    far_got = core(far_give).astype(F32)
    near_sum, near_up, near_down = far_split(near_ak, near_as, near_bk, near_bs)
    near_up, near_down = close_split(near_sum, up(near_up), down(near_down))
    gate_up_share = order(
        k,
        far_own.reshape(D_ROWS, 2 * planes, FF_COLS),
        after(far_got, near_up).reshape(D_ROWS, 2 * planes, FF_COLS),
        2,
    ).reshape(-1)
    near_own, near_give = core_split(near_sum, up(near_up), down(near_down), Q_COLS + HALF_D)
    near_got = core(near_give).astype(F32)
    qkv_share = order(
        k,
        near_own[:, :Q_COLS].reshape(D_ROWS, 3, HALF_D),
        near_got[:, :Q_COLS].reshape(D_ROWS, 3, HALF_D),
        2,
    ).reshape(-1)
    out_share = order(k, near_own[:, Q_COLS : Q_COLS + HALF_D], near_got[:, Q_COLS:], 1).reshape(-1)
    norm_share = near_own[:, Q_COLS + HALF_D : Q_COLS + HALF_D + 4].T
    input_grad = from_sequence([input_half[:quarter], input_half[quarter:]])
    input_grad = order(z & 1, input_grad[0], input_grad[1]).astype(F32)
    return (
        output,
        input_grad,
        qkv_share,
        out_share,
        gate_up_share,
        down_share,
        norm_share[0],
        norm_share[1],
        norm_share[2],
        norm_share[3],
    )


def solution(mesh):
    in_specs = (
        P("dp", "ctx", None),
        P("dp", "ctx"),
        P("dp", "ctx"),
        P(("dp", "ctx")),
        P(("dp", "ctx")),
        P(("dp", "ctx")),
        P(("dp", "ctx")),
        P(("dp", "ctx")),
        P(("dp", "ctx")),
        P(("dp", "ctx")),
        P(("dp", "ctx")),
        P("dp", "ctx", None),
    )
    out_specs = (
        P("dp", "ctx", None),
        P("dp", "ctx", None),
        P(("dp", "ctx")),
        P(("dp", "ctx")),
        P(("dp", "ctx")),
        P(("dp", "ctx")),
        P(("dp", "ctx")),
        P(("dp", "ctx")),
        P(("dp", "ctx")),
        P(("dp", "ctx")),
    )
    fits = mesh.shape["dp"] == 8 and mesh.shape["ctx"] == 4
    body = chip_local if fits else local
    return jax.shard_map(body, mesh=mesh, in_specs=in_specs, out_specs=out_specs, check_vma=False)
```

```python
import math

import jax
import jax.numpy as jnp
from jax import lax
from jax.experimental import pallas as pl
from jax.experimental.pallas import tpu as pltpu
from jax.sharding import PartitionSpec as P

D = 768
HEADS = 12
HEAD_DIM = 64
FF = 3072


norm_epsilon = 1e-05
rotary_base = 1000.0
masked_score = -1000000000.0


def rotary_tables(positions, head_size):
    half_dim = head_size // 2
    counter = jnp.arange(half_dim, dtype=jnp.float32)
    inverse = jnp.exp(counter * (-2.0 * math.log(rotary_base) / head_size))
    angles = positions.astype(jnp.float32)[..., None] * inverse
    return (jnp.cos(angles)[..., None, :], jnp.sin(angles)[..., None, :])


def rotate(values, cosine_table, sine_table):
    half_dim = values.shape[-1] // 2
    first_half = values[..., :half_dim]
    second_half = values[..., half_dim:]
    return jnp.concatenate(
        [
            first_half * cosine_table - second_half * sine_table,
            second_half * cosine_table + first_half * sine_table,
        ],
        axis=-1,
    )


def rotate_back(grads, cosine_table, sine_table):
    half_dim = grads.shape[-1] // 2
    first_half = grads[..., :half_dim]
    second_half = grads[..., half_dim:]
    return jnp.concatenate(
        [
            first_half * cosine_table + second_half * sine_table,
            second_half * cosine_table - first_half * sine_table,
        ],
        axis=-1,
    )


def layer_norm(hidden_sum, gain, bias):
    average = jnp.mean(hidden_sum, axis=-1, keepdims=True)
    centered = hidden_sum - average
    variance = jnp.mean(centered * centered, axis=-1, keepdims=True)
    reciprocal = lax.rsqrt(variance + norm_epsilon)
    normed = centered * reciprocal
    return (normed * gain + bias, normed, reciprocal)


def norm_back(upstream, normed, reciprocal, gain):
    gain_grad = jnp.sum(upstream * normed, axis=0)
    bias_grad = jnp.sum(upstream, axis=0)
    normed_grad = upstream * gain
    input_part = reciprocal * (
        normed_grad
        - jnp.mean(normed_grad, axis=-1, keepdims=True)
        - normed * jnp.mean(normed_grad * normed, axis=-1, keepdims=True)
    )
    return (input_part, gain_grad, bias_grad)


def contract_rows(left, right):
    return lax.dot_general(
        left, right, (((0,), (0,)), ((), ())), preferred_element_type=jnp.float32
    )


def back_dot(left, right):
    return lax.dot_general(
        left, right, (((1,), (1,)), ((), ())), preferred_element_type=jnp.float32
    )


def unpack(gathered):
    qkv_flat, out_flat, gate_up_flat, down_flat, gain_one, bias_one, gain_two, bias_two = gathered
    return (
        qkv_flat.reshape(D, 3 * D),
        out_flat.reshape(D, D),
        gate_up_flat.reshape(D, 2 * FF),
        down_flat.reshape(FF, D),
        gain_one.astype(jnp.float32),
        bias_one.astype(jnp.float32),
        gain_two.astype(jnp.float32),
        bias_two.astype(jnp.float32),
    )


def head_slice(array, offset, lanes):
    piece = lax.dynamic_slice_in_dim(array, offset, lanes, 2)
    return piece.reshape(array.shape[0], array.shape[1], 2, HEAD_DIM)


def pair_logits(query_pair, key_pair, same_doc):
    scores = jnp.einsum("sqhd,skhd->shqk", query_pair, key_pair, preferred_element_type=jnp.float32)
    return jnp.where(same_doc, scores * 0.125, masked_score)


def attend(queries, keys_all, values_all, same_doc):
    seq_count, row_count, feature_count = queries.shape
    lanes = 2 * HEAD_DIM

    def pair_step(head_pair, buffers):
        out_buffer, total_buffer = buffers
        offset = head_pair * lanes
        logits = pair_logits(
            head_slice(queries, offset, lanes), head_slice(keys_all, offset, lanes), same_doc
        )
        highest = jnp.max(logits, axis=-1, keepdims=True)
        log_total = highest + jnp.log(jnp.sum(jnp.exp(logits - highest), axis=-1, keepdims=True))
        probs_low = jnp.exp(logits - log_total).astype(jnp.bfloat16)
        attended = jnp.einsum(
            "shqk,skhd->sqhd",
            probs_low,
            head_slice(values_all, offset, lanes),
            preferred_element_type=jnp.float32,
        ).astype(jnp.bfloat16)
        out_buffer = lax.dynamic_update_slice_in_dim(
            out_buffer, attended.reshape(seq_count, row_count, lanes), offset, 2
        )
        total_buffer = lax.dynamic_update_slice_in_dim(
            total_buffer, log_total[..., 0], 2 * head_pair, 1
        )
        return (out_buffer, total_buffer)

    initial = (
        jnp.zeros((seq_count, row_count, feature_count), jnp.bfloat16),
        jnp.zeros((seq_count, HEADS, row_count), jnp.float32),
    )
    return lax.fori_loop(0, HEADS // 2, pair_step, initial)


def attend_back(queries, keys_all, values_all, same_doc, total_buffer, attended_grad):
    seq_count, row_count, feature_count = queries.shape
    key_count = keys_all.shape[1]
    lanes = 2 * HEAD_DIM

    def pair_step(head_pair, buffers):
        query_buffer, key_buffer, value_buffer = buffers
        offset = head_pair * lanes
        query_pair = head_slice(queries, offset, lanes)
        key_pair = head_slice(keys_all, offset, lanes)
        value_pair = head_slice(values_all, offset, lanes)
        grad_pair = head_slice(attended_grad, offset, lanes)
        logits = pair_logits(query_pair, key_pair, same_doc)
        log_total = lax.dynamic_slice_in_dim(total_buffer, 2 * head_pair, 2, 1)
        probs = jnp.exp(logits - log_total[..., None])
        prob_grad = jnp.einsum(
            "sqhd,skhd->shqk", grad_pair, value_pair, preferred_element_type=jnp.float32
        )
        logit_grad = probs * (prob_grad - jnp.sum(probs * prob_grad, axis=-1, keepdims=True))
        score_grad = (logit_grad * 0.125).astype(jnp.bfloat16)
        query_part = jnp.einsum(
            "shqk,skhd->sqhd", score_grad, key_pair, preferred_element_type=jnp.float32
        )
        key_part = jnp.einsum(
            "shqk,sqhd->skhd", score_grad, query_pair, preferred_element_type=jnp.float32
        )
        value_part = jnp.einsum(
            "shqk,sqhd->skhd",
            probs.astype(jnp.bfloat16),
            grad_pair,
            preferred_element_type=jnp.float32,
        )
        query_buffer = lax.dynamic_update_slice_in_dim(
            query_buffer, query_part.reshape(seq_count, row_count, lanes), offset, 2
        )
        key_buffer = lax.dynamic_update_slice_in_dim(
            key_buffer, key_part.reshape(seq_count, key_count, lanes), offset, 2
        )
        value_buffer = lax.dynamic_update_slice_in_dim(
            value_buffer, value_part.reshape(seq_count, key_count, lanes), offset, 2
        )
        return (query_buffer, key_buffer, value_buffer)

    initial = (
        jnp.zeros((seq_count, row_count, feature_count), jnp.float32),
        jnp.zeros((seq_count, key_count, feature_count), jnp.float32),
        jnp.zeros((seq_count, key_count, feature_count), jnp.float32),
    )
    return lax.fori_loop(0, HEADS // 2, pair_step, initial)


def local(
    tokens,
    segments,
    positions,
    qkv_weight,
    out_weight,
    gate_up_weight,
    down_weight,
    first_gain,
    first_bias,
    second_gain,
    second_bias,
    output_grad,
):
    seq_count = tokens.shape[0]
    row_count = tokens.shape[1]
    gathered = (
        lax.all_gather(qkv_weight, ("dp", "ctx"), axis=0, tiled=True),
        lax.all_gather(out_weight, ("dp", "ctx"), axis=0, tiled=True),
        lax.all_gather(gate_up_weight, ("dp", "ctx"), axis=0, tiled=True),
        lax.all_gather(down_weight, ("dp", "ctx"), axis=0, tiled=True),
        lax.all_gather(first_gain, ("dp", "ctx"), axis=0, tiled=True),
        lax.all_gather(first_bias, ("dp", "ctx"), axis=0, tiled=True),
        lax.all_gather(second_gain, ("dp", "ctx"), axis=0, tiled=True),
        lax.all_gather(second_bias, ("dp", "ctx"), axis=0, tiled=True),
    )
    qkv_mat, out_mat, gate_up_mat, down_mat, gain_one, bias_one, gain_two, bias_two = unpack(
        gathered
    )
    token_rows = tokens.reshape(seq_count * row_count, D)
    cosine_table, sine_table = rotary_tables(positions, HEAD_DIM)
    projected = jnp.dot(token_rows, qkv_mat, preferred_element_type=jnp.float32)
    projected = projected.reshape(seq_count, row_count, 3, HEADS, HEAD_DIM)
    queries = (
        rotate(projected[:, :, 0], cosine_table, sine_table)
        .astype(jnp.bfloat16)
        .reshape(seq_count, row_count, D)
    )
    keys_low = (
        rotate(projected[:, :, 1], cosine_table, sine_table)
        .astype(jnp.bfloat16)
        .reshape(seq_count, row_count, D)
    )
    values_low = projected[:, :, 2].astype(jnp.bfloat16).reshape(seq_count, row_count, D)
    key_ids = segments.astype(jnp.bfloat16)
    keys_all, values_all, ids_all = (
        lax.all_gather(keys_low, "ctx", axis=1, tiled=True),
        lax.all_gather(values_low, "ctx", axis=1, tiled=True),
        lax.all_gather(key_ids, "ctx", axis=1, tiled=True),
    )
    same_doc = (
        segments.astype(jnp.float32)[:, None, :, None]
        == ids_all.astype(jnp.float32)[:, None, None, :]
    )
    attended, total_buffer = attend(queries, keys_all, values_all, same_doc)
    attended_rows = attended.reshape(seq_count * row_count, D)
    branch = jnp.dot(attended_rows, out_mat, preferred_element_type=jnp.float32)
    normed_one, hat_one, recip_one = layer_norm(
        token_rows.astype(jnp.float32) + branch, gain_one, bias_one
    )
    normed_low = normed_one.astype(jnp.bfloat16)
    gate_up = jnp.dot(normed_low, gate_up_mat, preferred_element_type=jnp.float32)
    gate_part = gate_up[:, :FF]
    up_part = gate_up[:, FF:]
    sigmoid_gate = jax.nn.sigmoid(gate_part)
    silu_gate = gate_part * sigmoid_gate
    hidden = (silu_gate * up_part).astype(jnp.bfloat16)
    mlp_out = jnp.dot(hidden, down_mat, preferred_element_type=jnp.float32)
    result, hat_two, recip_two = layer_norm(normed_one + mlp_out, gain_two, bias_two)
    output = result.astype(jnp.bfloat16).reshape(tokens.shape)
    again = (
        lax.all_gather(qkv_weight, ("dp", "ctx"), axis=0, tiled=True),
        lax.all_gather(out_weight, ("dp", "ctx"), axis=0, tiled=True),
        lax.all_gather(gate_up_weight, ("dp", "ctx"), axis=0, tiled=True),
        lax.all_gather(down_weight, ("dp", "ctx"), axis=0, tiled=True),
        lax.all_gather(first_gain, ("dp", "ctx"), axis=0, tiled=True),
        lax.all_gather(first_bias, ("dp", "ctx"), axis=0, tiled=True),
        lax.all_gather(second_gain, ("dp", "ctx"), axis=0, tiled=True),
        lax.all_gather(second_bias, ("dp", "ctx"), axis=0, tiled=True),
    )
    qkv_mat, out_mat, gate_up_mat, down_mat, gain_one, bias_one, gain_two, bias_two = unpack(again)
    keys_all, values_all, ids_all = (
        lax.all_gather(keys_low, "ctx", axis=1, tiled=True),
        lax.all_gather(values_low, "ctx", axis=1, tiled=True),
        lax.all_gather(key_ids, "ctx", axis=1, tiled=True),
    )
    upstream = output_grad.reshape(seq_count * row_count, D).astype(jnp.float32)
    second_grad, second_gain_part, second_bias_part = norm_back(
        upstream, hat_two, recip_two, gain_two
    )
    mlp_grad = second_grad.astype(jnp.bfloat16)
    down_part = contract_rows(hidden, mlp_grad)
    hidden_grad = back_dot(mlp_grad, down_mat)
    gate_grad = hidden_grad * up_part * (sigmoid_gate * (1.0 + gate_part * (1.0 - sigmoid_gate)))
    up_grad = hidden_grad * silu_gate
    gate_up_grad = jnp.concatenate([gate_grad, up_grad], axis=1).astype(jnp.bfloat16)
    gate_up_part = contract_rows(normed_low, gate_up_grad)
    gate_up_flat = gate_up_part.reshape(-1)
    early = (
        lax.psum_scatter(gate_up_flat, ("dp", "ctx"), scatter_dimension=0, tiled=True),
        lax.psum_scatter(second_gain_part, ("dp", "ctx"), scatter_dimension=0, tiled=True),
        lax.psum_scatter(second_bias_part, ("dp", "ctx"), scatter_dimension=0, tiled=True),
    )
    gate_up_share, gain_two_share, bias_two_share = early
    normed_grad = second_grad + back_dot(gate_up_grad, gate_up_mat)
    first_grad, first_gain_part, first_bias_part = norm_back(
        normed_grad, hat_one, recip_one, gain_one
    )
    branch_grad = first_grad.astype(jnp.bfloat16)
    out_part = contract_rows(attended_rows, branch_grad)
    attended_grad = (
        back_dot(branch_grad, out_mat).astype(jnp.bfloat16).reshape(seq_count, row_count, D)
    )
    query_grad, key_partial, value_partial = attend_back(
        queries, keys_all, values_all, same_doc, total_buffer, attended_grad
    )
    key_grad, value_grad = (
        lax.psum_scatter(
            key_partial.astype(jnp.bfloat16), "ctx", scatter_dimension=1, tiled=True
        ).astype(jnp.float32),
        lax.psum_scatter(
            value_partial.astype(jnp.bfloat16), "ctx", scatter_dimension=1, tiled=True
        ).astype(jnp.float32),
    )
    head_shape = (seq_count, row_count, HEADS, HEAD_DIM)
    query_raw = rotate_back(query_grad.reshape(head_shape), cosine_table, sine_table).reshape(-1, D)
    key_raw = rotate_back(key_grad.reshape(head_shape), cosine_table, sine_table).reshape(-1, D)
    projected_grad = jnp.concatenate(
        [query_raw, key_raw, value_grad.reshape(-1, D)], axis=1
    ).astype(jnp.bfloat16)
    qkv_part = contract_rows(token_rows, projected_grad)
    input_grad = (back_dot(projected_grad, qkv_mat) + first_grad).reshape(tokens.shape)
    qkv_flat = qkv_part.reshape(-1)
    out_flat = out_part.reshape(-1)
    down_flat = down_part.reshape(-1)
    late = (
        lax.psum_scatter(qkv_flat, ("dp", "ctx"), scatter_dimension=0, tiled=True),
        lax.psum_scatter(out_flat, ("dp", "ctx"), scatter_dimension=0, tiled=True),
        lax.psum_scatter(down_flat, ("dp", "ctx"), scatter_dimension=0, tiled=True),
        lax.psum_scatter(first_gain_part, ("dp", "ctx"), scatter_dimension=0, tiled=True),
        lax.psum_scatter(first_bias_part, ("dp", "ctx"), scatter_dimension=0, tiled=True),
    )
    qkv_share, out_share, down_share, gain_one_share, bias_one_share = late
    return (
        output,
        input_grad,
        qkv_share,
        out_share,
        gate_up_share,
        down_share,
        gain_one_share,
        bias_one_share,
        gain_two_share,
        bias_two_share,
    )


PAIR = 2 * HEAD_DIM
HALF_D = D // 2
LOG2E = 1.4426950408889634
BF = jnp.bfloat16
F32 = jnp.float32
AXES = ("dp", "ctx")
LIGHT = pl.CostEstimate(flops=1024, bytes_accessed=1024, transcendentals=0)
SIDE, DEPTH = 2, 4
OWNERS = 2 * SIDE * SIDE * DEPTH
D_ROWS, FF_ROWS = D // OWNERS, FF // OWNERS
FF_HALF = FF // 2
FF_COLS = FF_HALF // (SIDE * SIDE)
NORM_COLS = 128
OUT_COLS = HALF_D + NORM_COLS
Q_COLS = 3 * HALF_D
NEAR_COLS = Q_COLS + OUT_COLS


def dot_nn(left, right):
    return lax.dot_general(left, right, (((1,), (0,)), ((), ())), preferred_element_type=F32)


def dot_nt(left, right):
    return lax.dot_general(left, right, (((1,), (1,)), ((), ())), preferred_element_type=F32)


def dot_tn(left, right):
    return lax.dot_general(left, right, (((0,), (0,)), ((), ())), preferred_element_type=F32)


def swap_halves(tile):
    lane = lax.broadcasted_iota(jnp.int32, tile.shape, 1)
    low_half = lax.rem(lane, HEAD_DIM) < HEAD_DIM // 2
    ahead = pltpu.roll(tile, PAIR - HEAD_DIM // 2, 1)
    behind = pltpu.roll(tile, HEAD_DIM // 2, 1)
    return jnp.where(low_half, ahead, behind)


def qkv_body(x_ref, w_ref, cos_ref, sin_ref, o_ref):
    product = dot_nn(x_ref[...], w_ref[...])
    part = pl.program_id(0)

    @pl.when(part < 2)
    def _():
        for c in range(HALF_D // PAIR):
            tile = product[:, c * PAIR : (c + 1) * PAIR]
            turned = tile * cos_ref[...] + swap_halves(tile) * sin_ref[...]
            o_ref[:, c * PAIR : (c + 1) * PAIR] = turned.astype(BF)

    @pl.when(part == 2)
    def _():
        o_ref[...] = product.astype(BF)


def project_qkv(tokens, weight, cosine, sine):
    rows = tokens.shape[0]
    tile = rows
    return pl.pallas_call(
        qkv_body,
        out_shape=jax.ShapeDtypeStruct((rows, 3 * HALF_D), BF),
        grid=(3, rows // tile),
        in_specs=[
            pl.BlockSpec((tile, D), lambda i, r: (r, 0)),
            pl.BlockSpec((D, HALF_D), lambda i, r: (0, i)),
            pl.BlockSpec((tile, PAIR), lambda i, r: (r, 0)),
            pl.BlockSpec((tile, PAIR), lambda i, r: (r, 0)),
        ],
        out_specs=pl.BlockSpec((tile, HALF_D), lambda i, r: (r, i)),
        cost_estimate=LIGHT,
        compiler_params=pltpu.CompilerParams(vmem_limit_bytes=32 * 2**20),
        name="project_qkv",
    )(tokens, weight, cosine, sine)


Q_TILE = 1024


def lane_head(shape):
    return lax.broadcasted_iota(jnp.int32, shape, 1) // HEAD_DIM


def row_head(shape):
    return lax.broadcasted_iota(jnp.int32, shape, 0) // HEAD_DIM


def attend_body(q_ref, k_ref, v_ref, segc_ref, segr_ref, o_ref, l_ref):
    keys = k_ref[...]
    values_t = v_ref[...].astype(F32).T.astype(BF)
    heads_down = row_head(values_t.shape)
    masked_values = [jnp.where(heads_down == h, values_t, jnp.zeros_like(values_t)) for h in range(2)]
    rows = q_ref.shape[0]
    scale = 0.125 * LOG2E
    for t in range(rows // Q_TILE):
        span = pl.ds(t * Q_TILE, Q_TILE)
        queries = q_ref[span, :]
        heads_across = lane_head(queries.shape)
        same = segc_ref[...] == segr_ref[:, span]
        total = jnp.zeros((PAIR, Q_TILE), F32)
        for h in range(2):
            scores = dot_nt(keys, jnp.where(heads_across == h, queries, jnp.zeros_like(queries)))
            scores = jnp.where(same, scores * scale, masked_score)
            highest = jnp.max(scores, axis=0, keepdims=True)
            weights = jnp.exp2(scores - highest)
            norm = jnp.sum(weights, axis=0, keepdims=True)
            l_ref[h : h + 1, span] = highest + jnp.log2(norm)
            total = total + dot_nn(masked_values[h], weights.astype(BF)) * (1.0 / norm)
        o_ref[span, :] = total.T.astype(BF)


def attend_pair(pair, qkv, seg_col, seg_row):
    rows = qkv.shape[0]
    pairs = HALF_D // PAIR
    return pl.pallas_call(
        attend_body,
        out_shape=(
            jax.ShapeDtypeStruct((rows, PAIR), BF),
            jax.ShapeDtypeStruct((8, rows), F32),
        ),
        grid=(1,),
        in_specs=[
            pl.BlockSpec((rows, PAIR), lambda i: (0, pair)),
            pl.BlockSpec((rows, PAIR), lambda i: (0, pairs + pair)),
            pl.BlockSpec((rows, PAIR), lambda i: (0, 2 * pairs + pair)),
            pl.BlockSpec((rows, 1), lambda i: (0, 0)),
            pl.BlockSpec((1, rows), lambda i: (0, 0)),
        ],
        out_specs=(
            pl.BlockSpec((rows, PAIR), lambda i: (0, 0)),
            pl.BlockSpec((8, rows), lambda i: (0, 0)),
        ),
        compiler_params=pltpu.CompilerParams(vmem_limit_bytes=40 * 2**20),
        cost_estimate=LIGHT,
        name="attend_pair",
    )(qkv, qkv, qkv, seg_col, seg_row)


def attend_back_body(
    q_ref, k_ref, v_ref, g_ref, l_ref, segc_ref, segr_ref, cos_ref, sin_ref, *others
):
    d_ref, dk_sum, dv_sum = others[-3:]
    keys = k_ref[...]
    values = v_ref[...]
    keys_t = keys.astype(F32).T.astype(BF)
    heads_down = row_head(keys_t.shape)
    masked_keys = [jnp.where(heads_down == h, keys_t, jnp.zeros_like(keys_t)) for h in range(2)]
    rows = q_ref.shape[0]
    scale = 0.125 * LOG2E
    for t in range(rows // Q_TILE):
        span = pl.ds(t * Q_TILE, Q_TILE)
        queries = q_ref[span, :]
        grads = g_ref[span, :]
        heads_across = lane_head(queries.shape)
        same = segc_ref[...] == segr_ref[:, span]
        dq_t = jnp.zeros((PAIR, Q_TILE), F32)
        dk_part = None
        dv_part = None
        for h in range(2):
            own_q = jnp.where(heads_across == h, queries, jnp.zeros_like(queries))
            own_g = jnp.where(heads_across == h, grads, jnp.zeros_like(grads))
            scores = dot_nt(keys, own_q)
            logits = jnp.where(same, scores * scale, masked_score)
            probs = jnp.exp2(logits - l_ref[h : h + 1, span])
            prob_grad = dot_nt(values, own_g)
            mixed = probs * prob_grad
            mean = jnp.sum(mixed, axis=0, keepdims=True)
            score_grad = (mixed - probs * mean).astype(BF)
            dv_new = dot_nn(probs.astype(BF), own_g)
            dk_new = dot_nn(score_grad, own_q)
            dv_part = dv_new if dv_part is None else dv_part + dv_new
            dk_part = dk_new if dk_part is None else dk_part + dk_new
            dq_t = dq_t + dot_nn(masked_keys[h], score_grad)
        if t == 0:
            dk_sum[...] = dk_part
            dv_sum[...] = dv_part
        else:
            dk_sum[...] += dk_part
            dv_sum[...] += dv_part
        dq = dq_t.T * 0.125
        d_ref[0, span, :] = (dq * cos_ref[span, :] - swap_halves(dq) * sin_ref[span, :]).astype(BF)
    dk = dk_sum[...] * 0.125
    d_ref[1] = (dk * cos_ref[...] - swap_halves(dk) * sin_ref[...]).astype(BF)
    d_ref[2] = dv_sum[...].astype(BF)


def attend_back_pair(pair, earlier, qkv, grads, totals, seg_col, seg_row, cosine, sine):
    rows = qkv.shape[0]
    pairs = HALF_D // PAIR
    column = pl.BlockSpec((rows, PAIR), lambda i: (0, pair))
    whole = pl.BlockSpec((rows, PAIR), lambda i: (0, 0))
    carried = [] if earlier is None else [earlier]
    return pl.pallas_call(
        attend_back_body,
        out_shape=jax.ShapeDtypeStruct((3, rows, HALF_D), BF),
        grid=(1,),
        in_specs=[
            column,
            pl.BlockSpec((rows, PAIR), lambda i: (0, pairs + pair)),
            pl.BlockSpec((rows, PAIR), lambda i: (0, 2 * pairs + pair)),
            column,
            pl.BlockSpec((8, rows), lambda i: (0, 0)),
            pl.BlockSpec((rows, 1), lambda i: (0, 0)),
            pl.BlockSpec((1, rows), lambda i: (0, 0)),
            whole,
            whole,
        ] + [pl.BlockSpec(memory_space=pl.ANY)] * len(carried),
        out_specs=pl.BlockSpec((3, rows, PAIR), lambda i: (0, 0, pair)),
        scratch_shapes=[pltpu.VMEM((rows, PAIR), F32), pltpu.VMEM((rows, PAIR), F32)],
        input_output_aliases={9: 0} if carried else {},
        compiler_params=pltpu.CompilerParams(vmem_limit_bytes=44 * 2**20),
        cost_estimate=LIGHT,
        name="attend_back_pair",
    )(qkv, qkv, qkv, grads, totals, seg_col, seg_row, cosine, sine, *carried)


def coordinates():
    place = lax.axis_index("dp")
    return place // (2 * SIDE), (place // 2) & 1, place & 1, lax.axis_index("ctx")


def whole(*shape):
    return pl.BlockSpec(shape, lambda *_: (0,) * len(shape))


def kernel(body, name, mebibytes, **arguments):
    return pl.pallas_call(
        body,
        compiler_params=pltpu.CompilerParams(vmem_limit_bytes=mebibytes * 2**20),
        cost_estimate=LIGHT,
        name=name,
        **arguments,
    )


def normalize(hidden_sum):
    centered = hidden_sum - jnp.mean(hidden_sum, axis=-1, keepdims=True)
    reciprocal = lax.rsqrt(jnp.mean(centered * centered, axis=-1, keepdims=True) + norm_epsilon)
    return centered * reciprocal, reciprocal


def norm_grad(upstream, normed, reciprocal, gain):
    grad = upstream * gain
    return reciprocal * (
        grad
        - jnp.mean(grad, axis=-1, keepdims=True)
        - normed * jnp.mean(grad * normed, axis=-1, keepdims=True)
    )


def add_sums(sums_ref, start, upstream, normed):
    first, second = pl.ds(start, 1), pl.ds(start + 1, 1)
    sums_ref[first, :] += jnp.sum(upstream * normed, axis=0, keepdims=True)
    sums_ref[second, :] += jnp.sum(upstream, axis=0, keepdims=True)


ROW_TILE = 256


def first_norm_body(a_ref, b_ref, w_ref, t_ref, p_ref, sum_ref, low_ref):
    total = t_ref[...].astype(F32)
    total = total + dot_nn(a_ref[...], w_ref[:HALF_D, :]) + dot_nn(b_ref[...], w_ref[HALF_D:, :])
    sum_ref[...] = total
    hat, _ = normalize(total)
    low_ref[...] = (hat * p_ref[0:1, :] + p_ref[1:2, :]).astype(BF)


def first_norm(attended_own, attended_got, out_mat, tokens, norms):
    rows = attended_own.shape[0]
    part = pl.BlockSpec((ROW_TILE, HALF_D), lambda i: (i, 0))
    full = pl.BlockSpec((ROW_TILE, D), lambda i: (i, 0))
    return kernel(
        first_norm_body,
        "first_norm",
        24,
        out_shape=(jax.ShapeDtypeStruct((rows, D), F32), jax.ShapeDtypeStruct((rows, D), BF)),
        grid=(rows // ROW_TILE,),
        in_specs=[part, part, whole(D, D), full, whole(8, D)],
        out_specs=(full, full),
    )(attended_own, attended_got, out_mat, tokens, norms)


FF_TILE = 256


def gate_up_body(x_ref, wg_ref, wu_ref, gate_ref, up_ref, h_ref):
    gate = dot_nn(x_ref[...], wg_ref[...])
    up_part = dot_nn(x_ref[...], wu_ref[...])
    gate_ref[...] = gate.astype(BF)
    up_ref[...] = up_part.astype(BF)
    h_ref[...] = (gate * lax.logistic(gate) * up_part).astype(BF)


def gate_up_forward(normed, weight):
    rows = normed.shape[0]
    tiles = FF_HALF // FF_TILE
    part = jax.ShapeDtypeStruct((rows, FF_HALF), BF)
    column = pl.BlockSpec((rows, FF_TILE), lambda i: (0, i))
    return kernel(
        gate_up_body,
        "gate_up_forward",
        24,
        out_shape=(part, part, part),
        grid=(tiles,),
        in_specs=[
            whole(rows, D),
            pl.BlockSpec((D, FF_TILE), lambda i: (0, i)),
            pl.BlockSpec((D, FF_TILE), lambda i: (0, tiles + i)),
        ],
        out_specs=(column, column, column),
    )(normed, weight, weight)


def second_norm_body(
    h_ref, w_ref, got_ref, sum_ref, p_ref, g_ref, result_ref, grad_ref, low_ref, sums_ref
):
    @pl.when(pl.program_id(0) == 0)
    def _():
        sums_ref[...] = jnp.zeros_like(sums_ref)

    hat, _ = normalize(sum_ref[...])
    total = hat * p_ref[0:1, :] + p_ref[1:2, :]
    total = total + dot_nn(h_ref[...], w_ref[...]) + got_ref[...].astype(F32)
    hat, reciprocal = normalize(total)
    gain = p_ref[2:3, :]
    result_ref[...] = (hat * gain + p_ref[3:4, :]).astype(BF)
    upstream = g_ref[...].astype(F32)
    add_sums(sums_ref, 2, upstream, hat)
    grad = norm_grad(upstream, hat, reciprocal, gain)
    grad_ref[...] = grad
    low_ref[...] = grad.astype(BF)


def second_norm(hidden, down_mat, got, first_sum, norms, output_grad):
    rows = hidden.shape[0]
    full = pl.BlockSpec((ROW_TILE, D), lambda i: (i, 0))
    return kernel(
        second_norm_body,
        "second_norm",
        32,
        out_shape=(
            jax.ShapeDtypeStruct((rows, D), BF),
            jax.ShapeDtypeStruct((rows, D), F32),
            jax.ShapeDtypeStruct((rows, D), BF),
            jax.ShapeDtypeStruct((8, D), F32),
        ),
        grid=(rows // ROW_TILE,),
        in_specs=[
            pl.BlockSpec((ROW_TILE, FF_HALF), lambda i: (i, 0)),
            whole(FF_HALF, D),
            full,
            full,
            whole(8, D),
            full,
        ],
        out_specs=(full, full, full, whole(8, D)),
    )(hidden, down_mat, got, first_sum, norms, output_grad)


def hidden_back_body(m_ref, w_ref, gate_ref, up_ref, o_ref):
    hidden_grad = dot_nt(m_ref[...], w_ref[...])
    gate, up_part = gate_ref[...].astype(F32), up_ref[...].astype(F32)
    sigmoid = lax.logistic(gate)
    o_ref[0] = (hidden_grad * up_part * (sigmoid * (1.0 + gate * (1.0 - sigmoid)))).astype(BF)
    o_ref[1] = (hidden_grad * (gate * sigmoid)).astype(BF)


def hidden_back(mlp_grad, down_mat, gate, up_part):
    rows = mlp_grad.shape[0]
    column = pl.BlockSpec((rows, FF_TILE), lambda i: (0, i))
    return kernel(
        hidden_back_body,
        "hidden_back",
        24,
        out_shape=jax.ShapeDtypeStruct((2, rows, FF_HALF), BF),
        grid=(FF_HALF // FF_TILE,),
        in_specs=[whole(rows, D), pl.BlockSpec((FF_TILE, D), lambda i: (i, 0)), column, column],
        out_specs=pl.BlockSpec((2, rows, FF_TILE), lambda i: (0, 0, i)),
    )(mlp_grad, down_mat, gate, up_part)


def normed_part_body(g_ref, w_ref, o_ref, acc_ref):
    product = dot_nt(g_ref[0], w_ref[...])
    step = pl.program_id(0)

    @pl.when(step == 0)
    def _():
        acc_ref[...] = product

    @pl.when(step > 0)
    def _():
        acc_ref[...] += product

    @pl.when(step == pl.num_programs(0) - 1)
    def _():
        o_ref[...] = acc_ref[...].astype(BF)


BACK_TILE = 768


def normed_part(grads, weight):
    rows = grads.shape[1]
    tiles = FF_HALF // BACK_TILE
    return kernel(
        normed_part_body,
        "normed_part",
        24,
        out_shape=jax.ShapeDtypeStruct((rows, D), BF),
        grid=(2 * tiles,),
        in_specs=[
            pl.BlockSpec((1, rows, BACK_TILE), lambda i: (i // tiles, 0, i % tiles)),
            pl.BlockSpec((D, BACK_TILE), lambda i: (0, i)),
        ],
        out_specs=whole(rows, D),
        scratch_shapes=[pltpu.VMEM((rows, D), F32)],
    )(grads, weight)


def first_back_body(
    g_ref, w_ref, got_ref, upper_ref, sum_ref, p_ref, out_ref, s_ref, grad_ref, own_ref, give_ref, sums_ref, acc_ref
):
    product = dot_nt(g_ref[0], w_ref[...])
    step = pl.program_id(0)

    @pl.when(step == 0)
    def _():
        acc_ref[...] = product

    @pl.when(step > 0)
    def _():
        acc_ref[...] += product

    @pl.when(step == pl.num_programs(0) - 1)
    def _():
        sums_ref[...] = s_ref[...]
        for n in range(acc_ref.shape[0] // ROW_TILE):
            span = pl.ds(n * ROW_TILE, ROW_TILE)
            upstream = acc_ref[span, :] + got_ref[span, :].astype(F32) + upper_ref[span, :]
            hat, reciprocal = normalize(sum_ref[span, :])
            add_sums(sums_ref, 0, upstream, hat)
            grad = norm_grad(upstream, hat, reciprocal, p_ref[0:1, :])
            grad_ref[span, :] = grad
            low = grad.astype(BF)
            own_ref[span, :] = dot_nt(low, out_ref[:HALF_D, :]).astype(BF)
            give_ref[span, :] = dot_nt(low, out_ref[HALF_D:, :]).astype(BF)


def first_back(grads, weight, got, second_grad, first_sum, norms, out_mat, sums):
    rows = grads.shape[1]
    tiles = FF_HALF // BACK_TILE
    part = jax.ShapeDtypeStruct((rows, HALF_D), BF)
    return kernel(
        first_back_body,
        "first_back",
        40,
        out_shape=(
            jax.ShapeDtypeStruct((rows, D), F32),
            part,
            part,
            jax.ShapeDtypeStruct((8, D), F32),
        ),
        grid=(2 * tiles,),
        in_specs=[
            pl.BlockSpec((1, rows, BACK_TILE), lambda i: (i // tiles, 0, i % tiles)),
            pl.BlockSpec((D, BACK_TILE), lambda i: (0, i)),
            whole(rows, D),
            whole(rows, D),
            whole(rows, D),
            whole(8, D),
            whole(D, D),
            whole(8, D),
        ],
        out_specs=(whole(rows, D), whole(rows, HALF_D), whole(rows, HALF_D), whole(8, D)),
        scratch_shapes=[pltpu.VMEM((rows, D), F32)],
    )(grads, weight, got, second_grad, first_sum, norms, out_mat, sums)


def out_part_body(a_ref, b_ref, g_ref, s_ref, keep_ref, give_ref):
    _, _, k, _ = coordinates()
    low = g_ref[...].astype(BF)
    parts = [dot_tn(a_ref[...], low), dot_tn(b_ref[...], low)]
    pad = jnp.zeros((NORM_COLS - 8, D), F32)
    sums = jnp.concatenate([s_ref[...], pad], axis=0).T
    for n in range(2):
        rows = jnp.where(k == n, parts[0], parts[1])
        left, right = rows[:, :HALF_D], rows[:, HALF_D:]
        span = slice(n * HALF_D, (n + 1) * HALF_D)
        keep_ref[span, :HALF_D] = jnp.where(k == 0, left, right)
        give_ref[span, :HALF_D] = jnp.where(k == 0, right, left).astype(BF)
    keep_ref[:, HALF_D:] = sums
    give_ref[:, HALF_D:] = sums.astype(BF)


def out_weight_part(attended_own, attended_got, first_grad, sums):
    rows = attended_own.shape[0]
    return kernel(
        out_part_body,
        "out_weight_part",
        32,
        out_shape=(
            jax.ShapeDtypeStruct((D, OUT_COLS), F32),
            jax.ShapeDtypeStruct((D, OUT_COLS), BF),
        ),
    )(attended_own, attended_got, first_grad, sums)


CHUNK = DEPTH * D_ROWS


def store_split(product, x, y, a_keep, a_send, b_keep, b_send, span=slice(None)):
    def block(yy, xx, kk):
        start = ((yy * SIDE + xx) * 2 + kk) * CHUNK
        return product[start : start + CHUNK]

    for n in range(2):
        a_keep[n, :, span] = jnp.where(x == 0, block(n, 0, 0), block(n, 1, 0))
        a_send[n, :, span] = jnp.where(x == 0, block(n, 1, 0), block(n, 0, 0))
        b_keep[n, :, span] = jnp.where(y == 0, block(0, n, 1), block(1, n, 1))
        b_send[n, :, span] = jnp.where(y == 0, block(1, n, 1), block(0, n, 1))


def second_split_body(a_ref, a_got, b_ref, b_got, a_keep, a_send, b_keep, b_send):
    y, x, _, _ = coordinates()
    for own, got, keep, send, index in (
        (a_ref, a_got, a_keep, a_send, y),
        (b_ref, b_got, b_keep, b_send, x),
    ):
        keep[...] = own[index].astype(F32) + got[index].astype(F32)
        send[...] = (own[1 - index].astype(F32) + got[1 - index].astype(F32)).astype(BF)


def second_split(a_keep, a_got, b_keep, b_got):
    cols = a_keep.shape[-1]
    keep, send = (jax.ShapeDtypeStruct((CHUNK, cols), kind) for kind in (F32, BF))
    return kernel(second_split_body, "second_split", 32, out_shape=(keep, send, keep, send))(
        a_keep, a_got, b_keep, b_got
    )


def far_split_body(a_ref, a_got, b_ref, b_got, sum_ref, up_ref, down_ref):
    _, _, _, z = coordinates()
    for n, (own, got) in enumerate(((a_ref, a_got), (b_ref, b_got))):
        total = own[...] + got[...].astype(F32)
        for m in range(DEPTH):
            sum_ref[m, n] = total[m * D_ROWS : (m + 1) * D_ROWS]
    far = (z + 2) & 3
    up_ref[...] = sum_ref[far, 0].astype(BF)
    down_ref[...] = sum_ref[far, 1].astype(BF)


def far_split(a_keep, a_got, b_keep, b_got):
    cols = a_keep.shape[-1]
    send = jax.ShapeDtypeStruct((D_ROWS, cols), BF)
    return kernel(
        far_split_body,
        "far_split",
        32,
        out_shape=(jax.ShapeDtypeStruct((DEPTH, 2, D_ROWS, cols), F32), send, send),
    )(a_keep, a_got, b_keep, b_got)


def close_split_body(sum_ref, first_ref, second_ref, up_ref, down_ref):
    _, _, _, z = coordinates()
    above, below = (z + 1) & 3, (z + 3) & 3
    up_ref[0] = (sum_ref[above, 0] + first_ref[...].astype(F32)).astype(BF)
    up_ref[1] = sum_ref[above, 1].astype(BF)
    down_ref[0] = sum_ref[below, 0].astype(BF)
    down_ref[1] = (sum_ref[below, 1] + second_ref[...].astype(F32)).astype(BF)


def close_split(sums, first, second):
    send = jax.ShapeDtypeStruct(sums.shape[1:], BF)
    return kernel(close_split_body, "close_split", 24, out_shape=(send, send))(sums, first, second)


def core_split_body(sum_ref, up_ref, down_ref, keep_ref, send_ref):
    _, _, k, z = coordinates()

    def total(index):
        return sum_ref[z, index] + up_ref[index].astype(F32) + down_ref[index].astype(F32)

    keep_ref[...] = total(k)
    send_ref[...] = total(1 - k)[:, : send_ref.shape[1]].astype(BF)


def core_split(sums, from_below, from_above, give_cols):
    return kernel(
        core_split_body,
        "core_split",
        24,
        out_shape=(
            jax.ShapeDtypeStruct(sums.shape[2:], F32),
            jax.ShapeDtypeStruct((D_ROWS, give_cols), BF),
        ),
    )(sums, from_below, from_above)


def near_part_body(x_ref, g_ref, out_ref, got_ref, a_keep, a_send, b_keep, b_send):
    y, x, _, _ = coordinates()
    outs = (a_keep, a_send, b_keep, b_send)
    for n in range(3):
        product = dot_tn(x_ref[...], g_ref[n]).astype(BF)
        store_split(product, x, y, *outs, span=slice(n * HALF_D, (n + 1) * HALF_D))
    rest = (out_ref[...] + got_ref[...].astype(F32)).astype(BF)
    store_split(rest, x, y, *outs, span=slice(Q_COLS, NEAR_COLS))


def near_weight_part(tokens, grads, out_keep, out_got):
    part = jax.ShapeDtypeStruct((SIDE, CHUNK, NEAR_COLS), BF)
    return kernel(near_part_body, "near_weight_part", 40, out_shape=(part,) * 4)(
        tokens, grads, out_keep, out_got
    )


def gate_up_part_body(x_ref, y_ref, g_ref, h_ref, *outs):
    y, x, _, _ = coordinates()
    product = (dot_tn(x_ref[...], g_ref[0]) + dot_tn(y_ref[...], h_ref[0])).astype(BF)
    store_split(product, x, y, *outs)


def row_sum_body(x_ref, y_ref, g_ref, h_ref, o_ref):
    o_ref[...] = (dot_tn(x_ref[...], g_ref[...]) + dot_tn(y_ref[...], h_ref[...])).astype(BF)


def gate_up_weight_part(normed, grads):
    rows, tile = normed[0].shape[0], 512
    tiles = FF_HALF // tile
    column = pl.BlockSpec((1, rows, tile), lambda i: (i // tiles, 0, i % tiles))
    return kernel(
        gate_up_part_body,
        "gate_up_weight_part",
        24,
        out_shape=(jax.ShapeDtypeStruct((SIDE, CHUNK, FF), BF),) * 4,
        grid=(FF // tile,),
        in_specs=[whole(rows, D), whole(rows, D), column, column],
        out_specs=(pl.BlockSpec((SIDE, CHUNK, tile), lambda i: (0, 0, i)),) * 4,
    )(*normed, *grads)


def down_weight_part(hidden, grads):
    rows, tile = hidden[0].shape[0], 512
    column = pl.BlockSpec((rows, tile), lambda i: (0, i))
    return kernel(
        row_sum_body,
        "down_weight_part",
        24,
        out_shape=jax.ShapeDtypeStruct((FF_HALF, D), BF),
        grid=(FF_HALF // tile,),
        in_specs=[column, column, whole(rows, D), whole(rows, D)],
        out_specs=pl.BlockSpec((tile, D), lambda i: (i, 0)),
    )(*hidden, *grads)


def input_part_body(g_ref, w_ref, o_ref):
    total = dot_nt(g_ref[0], w_ref[:, :HALF_D])
    for n in range(1, 3):
        total = total + dot_nt(g_ref[n], w_ref[:, n * HALF_D : (n + 1) * HALF_D])
    o_ref[...] = total.astype(o_ref.dtype)


def input_part(grads, weight, block, dtype):
    rows = grads.shape[1] // 2
    return pl.pallas_call(
        input_part_body,
        out_shape=jax.ShapeDtypeStruct((rows, D), dtype),
        grid=(1,),
        in_specs=[
            pl.BlockSpec((3, rows, HALF_D), lambda i: (0, block, 0)),
            pl.BlockSpec((D, 3 * HALF_D), lambda i: (0, 0)),
        ],
        out_specs=pl.BlockSpec((rows, D), lambda i: (0, 0)),
        compiler_params=pltpu.CompilerParams(vmem_limit_bytes=24 * 2**20),
        cost_estimate=LIGHT,
        name="input_part",
    )(grads, weight)


def at(array, index, axis=0):
    return lax.dynamic_index_in_dim(array, index, axis, keepdims=False)


def after(value, earlier):
    return lax.optimization_barrier((value, earlier))[0]


def place(pieces, shapes, moves):
    dtype = pieces[0].dtype
    count = len(moves(0, 0, 0, 0))
    inputs = len(pieces)

    def body(*refs):
        sources, results, sems = refs[:inputs], refs[inputs:-1], refs[-1]
        copies = []
        for n, (piece, part, result, spot) in enumerate(moves(*coordinates())):
            source = sources[piece] if part is None else sources[piece].at[part]
            copies.append(pltpu.make_async_copy(source, results[result].at[spot], sems.at[n]))
        for copy in copies:
            copy.start()
        for copy in copies:
            copy.wait()

    anywhere = pl.BlockSpec(memory_space=pl.ANY)
    size = sum(math.prod(shape) for shape in shapes) * 2 * jnp.dtype(dtype).itemsize
    return pl.pallas_call(
        body,
        out_shape=tuple(jax.ShapeDtypeStruct(shape, dtype) for shape in shapes),
        in_specs=[anywhere] * inputs,
        out_specs=tuple(pl.BlockSpec(memory_space=pltpu.VMEM) for _ in shapes),
        scratch_shapes=[pltpu.SemaphoreType.DMA((count,))],
        compiler_params=pltpu.CompilerParams(vmem_limit_bytes=max(8 * 2**20, 2 * size)),
        cost_estimate=LIGHT,
        name="place",
    )(*pieces)


def move(array, target):
    pairs = []
    for y in range(SIDE):
        for x in range(SIDE):
            for k in range(2):
                for z in range(DEPTH):
                    ty, tx, tk, tz = target(y, x, k, z)
                    source = ((y * SIDE + x) * 2 + k) * DEPTH + z
                    goal = ((ty * SIDE + tx) * 2 + tk) * DEPTH + tz % DEPTH
                    pairs.append((source, goal))
    return lax.ppermute(array, AXES, pairs)


def core(array):
    return move(array, lambda y, x, k, z: (y, x, 1 - k, z))


def across_x(array):
    return move(array, lambda y, x, k, z: (y, 1 - x, k, z))


def across_y(array):
    return move(array, lambda y, x, k, z: (1 - y, x, k, z))


def up(array):
    return move(array, lambda y, x, k, z: (y, x, k, z + 1))


def down(array):
    return move(array, lambda y, x, k, z: (y, x, k, z - 1))


def order(index, own, other, axis=0):
    first = jnp.where(index == 0, own, other)
    second = jnp.where(index == 0, other, own)
    return jnp.stack([first, second], axis)


def ring_near(array):
    return down(array), up(array)


def ring_far(above, below):
    half = above.shape[0] // 2
    return up(below[:half]), down(above[half:])


def pair_x(array, got):
    return place(
        (array, got), [(SIDE, *array.shape)], lambda y, x, k, z: [(n, None, 0, (x ^ n,)) for n in range(2)]
    )[0]


def pair_y(array, got):
    return place(
        (array, got), [(SIDE, *array.shape)], lambda y, x, k, z: [(n, None, 0, (y ^ n,)) for n in range(2)]
    )[0]


def spread_z(block, pieces):
    both = range(2)
    return place(
        (block, *pieces),
        [(DEPTH, *block.shape[1:])] * 2,
        lambda y, x, k, z: [
            (n, (m,), m, ((z + step) & 3,)) for n, step in ((0, 0), (1, 1), (2, 3)) for m in both
        ] + [(3 + m, (0,), m, ((z + 2) & 3,)) for m in both],
    )


def scatter(array, index, across, axis=0, gate=None):
    got = across(at(array, 1 - index, axis).astype(BF))
    if gate is not None:
        got = after(got, gate)
    return at(array, index, axis).astype(F32) + got.astype(F32)


def scatter_far(array, z, axis):
    far = at(array, (z + 2) & 3, axis).astype(BF)
    half = far.shape[0] // 2
    return up(far[:half]), down(far[half:])


def scatter_near(array, z, axis, first, second):
    above, below = at(array, (z + 1) & 3, axis), at(array, (z + 3) & 3, axis)
    half = above.shape[0] // 2
    sum_above = (above[:half].astype(F32) + first.astype(F32)).astype(BF)
    sum_below = (below[half:].astype(F32) + second.astype(F32)).astype(BF)
    got_a = up(jnp.concatenate([sum_above, above[half:].astype(BF)], 0))
    got_b = down(jnp.concatenate([below[:half].astype(BF), sum_below], 0))
    return got_a, got_b


def scatter_own(array, z, axis, got_a, got_b):
    return at(array, z, axis).astype(F32) + got_a.astype(F32) + got_b.astype(F32)


def sequence_step(r):
    return lambda y, x, k, z: (y, x, z // 2, 2 * k + ((r + z) & 1))


def to_sequence(blocks, z):
    return [move(at(blocks, (z + r) & 1), sequence_step(r)) for r in range(2)]


def from_sequence(quarters):
    return [move(quarters[r], sequence_step(r)) for r in range(2)]


def chip_local(
    tokens,
    segments,
    positions,
    qkv_weight,
    out_weight,
    gate_up_weight,
    down_weight,
    first_gain,
    first_bias,
    second_gain,
    second_bias,
    output_grad,
):
    y, x, k, z = coordinates()
    quarter = tokens.shape[1]
    rows = DEPTH * quarter
    half = rows // 2
    planes = SIDE * SIDE

    norms = jnp.stack([first_gain, first_bias, second_gain, second_bias], axis=1)
    norms = jnp.pad(norms, ((0, 0), (0, NORM_COLS - 4)))
    qkv_own = qkv_weight.reshape(D_ROWS, 3 * D)
    gate_up_own = gate_up_weight.reshape(D_ROWS, 2 * FF)
    out_own = out_weight.reshape(D_ROWS, D)

    def column_half(index):
        def part(matrix, start, width):
            left, right = matrix[:, start : start + width], matrix[:, start + width : start + 2 * width]
            return jnp.where(index == 0, left, right)

        pieces = [part(qkv_own, n * D, HALF_D) for n in range(3)]
        pieces += [part(out_own, 0, HALF_D), norms]
        pieces += [part(gate_up_own, n * 2 * FF_COLS, FF_COLS) for n in range(2 * planes)]
        return jnp.concatenate(pieces, axis=1)

    mine, theirs = column_half(k), core(column_half(1 - k))
    both, every = range(2), slice(None)
    near_span, gate_up_span = pl.ds(0, NEAR_COLS), pl.ds(NEAR_COLS, FF)
    near_block, gate_up_block = place(
        (mine, theirs),
        [(2, D_ROWS, NEAR_COLS), (2, D_ROWS, FF)],
        lambda y, x, k, z: [
            (n, (every, span), r, (k ^ n,)) for n in both for r, span in enumerate((near_span, gate_up_span))
        ],
    )

    near_close = ring_near(near_block)
    near_ring = (*near_close, *ring_far(*near_close))
    near_a, near_b = spread_z(near_block, near_ring)
    down_x = down_weight.reshape(FF_ROWS, D)
    down_x = pair_x(down_x, across_x(down_x))
    near_a, near_b, down_x = lax.optimization_barrier((near_a, near_b, down_x))
    near_ax = pair_x(near_a, across_x(near_a))
    near_by = pair_y(near_b, across_y(near_b))
    down_x = (down_x, across_y(down_x))
    gate_up_close = ring_near(after(gate_up_block, near_ring))
    gate_up_far = ring_far(*gate_up_close)

    extra = jnp.stack([segments, positions >> 5, positions & 31], axis=1).astype(BF)
    extra = jnp.pad(extra, ((0, 0), (0, 13), (0, D - quarter)))
    packed = after(jnp.concatenate([tokens, extra], axis=1), gate_up_far[0])
    own_tokens = jnp.concatenate(to_sequence(packed, z), axis=0)
    other_tokens = core(own_tokens)
    blocks = jnp.concatenate([own_tokens, other_tokens], 0).reshape(DEPTH, quarter + 16, D)
    all_tokens = blocks[:, :quarter].reshape(rows, D)
    all_extra = blocks[:, quarter:, :quarter].astype(F32)
    seg_all = all_extra[:, 0].reshape(rows)
    pos_all = (all_extra[:, 1] * 32.0 + all_extra[:, 2]).reshape(rows)
    lane = jnp.arange(PAIR)
    counter = (lane & (HEAD_DIM // 2 - 1)).astype(F32)
    inverse = jnp.exp(counter * (-2.0 * math.log(rotary_base) / HEAD_DIM))
    angles = pos_all[:, None] * inverse
    cosine = jnp.cos(angles)
    sine = jnp.where((lane & (HEAD_DIM - 1)) < HEAD_DIM // 2, -1.0, 1.0) * jnp.sin(angles)
    seg_col, seg_row = seg_all[:, None], seg_all[None, :]

    qkv_mat, out_half = place(
        (near_ax, across_y(near_ax), near_by, across_x(near_by)),
        [(SIDE, SIDE, 2, DEPTH, D_ROWS, Q_COLS), (SIDE, SIDE, 2, DEPTH, D_ROWS, OUT_COLS)],
        lambda y, x, k, z: [
            (n, (row, every, every, cols), r, ((y ^ n) ^ (k * r), row, 0))
            for n in both for row in both for r, cols in ((0, pl.ds(0, Q_COLS)), (1, pl.ds(Q_COLS, OUT_COLS)))
        ] + [
            (2 + n, (row, every, every, cols), r, (row ^ (k * r), x ^ n, 1))
            for n in both for row in both for r, cols in ((0, pl.ds(0, Q_COLS)), (1, pl.ds(Q_COLS, OUT_COLS)))
        ],
    )
    qkv_mat, out_half = qkv_mat.reshape(D, Q_COLS), out_half.reshape(D, OUT_COLS)

    out_other = core(out_half)
    swapped = jnp.concatenate([out_other[HALF_D:, :HALF_D], out_other[:HALF_D, :HALF_D]], axis=0)
    own_cols = out_half[:, :HALF_D]
    out_mat = jnp.concatenate(
        [jnp.where(k == 0, own_cols, swapped), jnp.where(k == 0, swapped, own_cols)], axis=1
    )
    norms_all = out_half[:, HALF_D : HALF_D + 8].astype(F32)
    norms_all = jnp.where(k == 0, norms_all, jnp.roll(norms_all, HALF_D, axis=0)).T

    gate_up_a, gate_up_b = spread_z(gate_up_block, (*gate_up_close, *gate_up_far))
    gate_up_ax = pair_x(gate_up_a, across_x(gate_up_a))
    gate_up_by = pair_y(gate_up_b, across_y(gate_up_b))

    token_half = all_tokens[:half]
    all_tokens, gate_up_ax, gate_up_by = lax.optimization_barrier((all_tokens, gate_up_ax, gate_up_by))
    qkv = project_qkv(all_tokens, qkv_mat, cosine, sine)
    down_y = pair_y(*after(down_x, other_tokens)).reshape(planes, FF_ROWS, D)
    down_close = ring_near(down_y)
    pairs = range(HALF_D // PAIR)
    attended, totals = [], []
    for pair in pairs:
        if pair:
            qkv, attended[-1] = lax.optimization_barrier((qkv, attended[-1]))
        one, total = attend_pair(pair, qkv, seg_col, seg_row)
        attended.append(one)
        if pair == 1:
            grad_quarters = to_sequence(after(output_grad, one), z)
        totals.append(total)
    gate_up_mat = place(
        (gate_up_ax, across_y(gate_up_ax), gate_up_by, across_x(gate_up_by)),
        [(SIDE, SIDE, 2, DEPTH, D_ROWS, FF)],
        lambda y, x, k, z: [
            (n, (row,), 0, (y ^ n, row, 0)) for n in both for row in both
        ] + [(2 + n, (row,), 0, (row, x ^ n, 1)) for n in both for row in both],
    )[0].reshape(D, FF)
    attended = jnp.concatenate(attended, axis=1)
    attended_own, attended_got = attended[:half], core(attended[half:])
    down_ring = (*down_close, *ring_far(*after(down_close, attended_got)))
    first, second = pl.ds(0, planes // 2), pl.ds(planes // 2, planes // 2)
    first_sum, normed_own = first_norm(attended_own, attended_got, out_mat, token_half, norms_all)
    normed_got = core(normed_own)
    normed_own, grad_quarters = lax.optimization_barrier((normed_own, grad_quarters))
    gate_own, up_own, hidden_own = gate_up_forward(normed_own, gate_up_mat)
    gate_got, up_got, hidden_got = gate_up_forward(after(normed_got, hidden_own), gate_up_mat)
    down_ring = after(down_ring, hidden_got)
    down_mat = place(
        (down_y, *down_ring),
        [(planes, DEPTH, FF_ROWS, D)],
        lambda y, x, k, z: [
            (0, None, 0, (every, z)),
            (1, None, 0, (every, (z + 1) & 3)),
            (2, None, 0, (every, (z + 3) & 3)),
            (3, None, 0, (first, (z + 2) & 3)),
            (4, None, 0, (second, (z + 2) & 3)),
        ],
    )[0].reshape(FF_HALF, D)
    mlp_got = core(dot_nn(hidden_got, down_mat).astype(BF))
    grad_half = jnp.concatenate(grad_quarters, axis=0)
    result, second_grad, mlp_own, sums = second_norm(
        hidden_own, down_mat, mlp_got, first_sum, norms_all, grad_half
    )

    other_grad = core(mlp_own)
    output_got = from_sequence([result[:quarter], result[quarter:]])
    gate_up_own = hidden_back(mlp_own, down_mat, gate_own, up_own)
    gate_up_other = hidden_back(after(other_grad, gate_up_own), down_mat, gate_got, up_got)
    normed_back = normed_part(gate_up_other, gate_up_mat)
    normed_got_back = core(normed_back)
    down_part = down_weight_part((hidden_own, hidden_got), (mlp_own, after(other_grad, normed_back)))
    gate_up_part = gate_up_weight_part(
        (normed_own, normed_got), (gate_up_own, after(gate_up_other, down_part))
    )
    first_grad, attended_mine, attended_give, sums = first_back(
        gate_up_own,
        gate_up_mat,
        after(normed_got_back, (gate_up_part, output_got)),
        second_grad,
        first_sum,
        norms_all,
        out_mat,
        sums,
    )
    attended_grad = jnp.concatenate([attended_mine, core(attended_give)], axis=0)

    output = order(z & 1, output_got[0], output_got[1])
    down_part = down_part.reshape(planes, DEPTH, FF_ROWS, D)
    down_far = scatter_far(down_part, z, 1)
    down_near = scatter_near(down_part, z, 1, *after(down_far, first_grad))
    far_ak, far_as, far_bk, far_bs = gate_up_part
    far_as, far_bs = across_x(far_as), across_y(far_bs)

    out_keep, out_give = out_weight_part(attended_own, attended_got, first_grad, sums)
    out_got = core(out_give)

    projected_grad = None
    for pair in pairs:
        if pair == 1:
            far_as, far_bs = after((far_as, far_bs), projected_grad)
            far_ak, far_as, far_bk, far_bs = second_split(far_ak, far_as, far_bk, far_bs)
            attended_grad, far_ak, projected_grad = lax.optimization_barrier(
                (attended_grad, far_ak, projected_grad)
            )
            far_as, far_bs = across_y(far_as), across_x(far_bs)
        if pair == 2:
            far_as, far_bs, down_near = after((far_as, far_bs, down_near), projected_grad)
            down_z = scatter_own(down_part, z, 1, *down_near)
            far_sum, far_up, far_down = far_split(far_ak, far_as, far_bk, far_bs)
            attended_grad, far_sum, down_z, projected_grad = lax.optimization_barrier(
                (attended_grad, far_sum, down_z, projected_grad)
            )
            far_up, far_down = up(far_up), down(far_down)
            down_y = across_y(at(down_z.reshape(SIDE, SIDE, FF_ROWS, D), 1 - y).astype(BF))
        projected_grad = attend_back_pair(
            pair, projected_grad, qkv, attended_grad, totals[pair], seg_col, seg_row, cosine, sine
        )
    far_up, far_down, down_y = after((far_up, far_down, down_y), projected_grad)
    down_y = at(down_z.reshape(SIDE, SIDE, FF_ROWS, D), y) + down_y.astype(F32)
    far_up, far_down = close_split(far_sum, far_up, far_down)
    input_give = input_part(projected_grad, qkv_mat, 1, BF)
    projected_grad, far_up, far_down, input_give = lax.optimization_barrier(
        (projected_grad, far_up, far_down, input_give)
    )
    far_up, far_down = up(far_up), down(far_down)
    input_got = core(input_give)
    near_ak, near_as, near_bk, near_bs = near_weight_part(
        all_tokens, projected_grad, out_keep, out_got
    )
    near_as, near_bs = across_x(near_as), across_y(near_bs)
    input_own = input_part(after(projected_grad, near_ak), qkv_mat, 0, F32)
    input_half = (first_grad + input_own + input_got.astype(F32)).astype(BF)
    near_as, near_bs = after((near_as, near_bs), input_half)
    near_ak, near_as, near_bk, near_bs = second_split(near_ak, near_as, near_bk, near_bs)
    near_as, near_bs = across_y(near_as), across_x(near_bs)
    down_x = after(across_x(at(down_y, 1 - x).astype(BF)), near_ak)
    down_share = (at(down_y, x) + down_x.astype(F32)).reshape(-1)
    far_up, far_down = after((far_up, far_down), near_ak)
    far_own, far_give = core_split(far_sum, far_up, far_down, FF)
    far_got = core(far_give).astype(F32)
    near_sum, near_up, near_down = far_split(near_ak, near_as, near_bk, near_bs)
    near_up, near_down = close_split(near_sum, up(near_up), down(near_down))
    gate_up_share = order(
        k,
        far_own.reshape(D_ROWS, 2 * planes, FF_COLS),
        after(far_got, near_up).reshape(D_ROWS, 2 * planes, FF_COLS),
        2,
    ).reshape(-1)
    near_own, near_give = core_split(near_sum, up(near_up), down(near_down), Q_COLS + HALF_D)
    near_got = core(near_give).astype(F32)
    qkv_share = order(
        k,
        near_own[:, :Q_COLS].reshape(D_ROWS, 3, HALF_D),
        near_got[:, :Q_COLS].reshape(D_ROWS, 3, HALF_D),
        2,
    ).reshape(-1)
    out_share = order(k, near_own[:, Q_COLS : Q_COLS + HALF_D], near_got[:, Q_COLS:], 1).reshape(-1)
    norm_share = near_own[:, Q_COLS + HALF_D : Q_COLS + HALF_D + 4].T
    input_grad = from_sequence([input_half[:quarter], input_half[quarter:]])
    input_grad = order(z & 1, input_grad[0], input_grad[1]).astype(F32)
    return (
        output,
        input_grad,
        qkv_share,
        out_share,
        gate_up_share,
        down_share,
        norm_share[0],
        norm_share[1],
        norm_share[2],
        norm_share[3],
    )


def solution(mesh):
    in_specs = (
        P("dp", "ctx", None),
        P("dp", "ctx"),
        P("dp", "ctx"),
        P(("dp", "ctx")),
        P(("dp", "ctx")),
        P(("dp", "ctx")),
        P(("dp", "ctx")),
        P(("dp", "ctx")),
        P(("dp", "ctx")),
        P(("dp", "ctx")),
        P(("dp", "ctx")),
        P("dp", "ctx", None),
    )
    out_specs = (
        P("dp", "ctx", None),
        P("dp", "ctx", None),
        P(("dp", "ctx")),
        P(("dp", "ctx")),
        P(("dp", "ctx")),
        P(("dp", "ctx")),
        P(("dp", "ctx")),
        P(("dp", "ctx")),
        P(("dp", "ctx")),
        P(("dp", "ctx")),
    )
    fits = mesh.shape["dp"] == 8 and mesh.shape["ctx"] == 4
    body = chip_local if fits else local
    return jax.shard_map(body, mesh=mesh, in_specs=in_specs, out_specs=out_specs, check_vma=False)
```

```python
import math

import jax
import jax.numpy as jnp
from jax import lax
from jax.experimental import pallas as pl
from jax.experimental.pallas import tpu as pltpu
from jax.sharding import PartitionSpec as P

D = 768
HEADS = 12
HEAD_DIM = 64
FF = 3072


norm_epsilon = 1e-05
rotary_base = 1000.0
masked_score = -1000000000.0


def rotary_tables(positions, head_size):
    half_dim = head_size // 2
    counter = jnp.arange(half_dim, dtype=jnp.float32)
    inverse = jnp.exp(counter * (-2.0 * math.log(rotary_base) / head_size))
    angles = positions.astype(jnp.float32)[..., None] * inverse
    return (jnp.cos(angles)[..., None, :], jnp.sin(angles)[..., None, :])


def rotate(values, cosine_table, sine_table):
    half_dim = values.shape[-1] // 2
    first_half = values[..., :half_dim]
    second_half = values[..., half_dim:]
    return jnp.concatenate(
        [
            first_half * cosine_table - second_half * sine_table,
            second_half * cosine_table + first_half * sine_table,
        ],
        axis=-1,
    )


def rotate_back(grads, cosine_table, sine_table):
    half_dim = grads.shape[-1] // 2
    first_half = grads[..., :half_dim]
    second_half = grads[..., half_dim:]
    return jnp.concatenate(
        [
            first_half * cosine_table + second_half * sine_table,
            second_half * cosine_table - first_half * sine_table,
        ],
        axis=-1,
    )


def layer_norm(hidden_sum, gain, bias):
    average = jnp.mean(hidden_sum, axis=-1, keepdims=True)
    centered = hidden_sum - average
    variance = jnp.mean(centered * centered, axis=-1, keepdims=True)
    reciprocal = lax.rsqrt(variance + norm_epsilon)
    normed = centered * reciprocal
    return (normed * gain + bias, normed, reciprocal)


def norm_back(upstream, normed, reciprocal, gain):
    gain_grad = jnp.sum(upstream * normed, axis=0)
    bias_grad = jnp.sum(upstream, axis=0)
    normed_grad = upstream * gain
    input_part = reciprocal * (
        normed_grad
        - jnp.mean(normed_grad, axis=-1, keepdims=True)
        - normed * jnp.mean(normed_grad * normed, axis=-1, keepdims=True)
    )
    return (input_part, gain_grad, bias_grad)


def contract_rows(left, right):
    return lax.dot_general(
        left, right, (((0,), (0,)), ((), ())), preferred_element_type=jnp.float32
    )


def back_dot(left, right):
    return lax.dot_general(
        left, right, (((1,), (1,)), ((), ())), preferred_element_type=jnp.float32
    )


def unpack(gathered):
    qkv_flat, out_flat, gate_up_flat, down_flat, gain_one, bias_one, gain_two, bias_two = gathered
    return (
        qkv_flat.reshape(D, 3 * D),
        out_flat.reshape(D, D),
        gate_up_flat.reshape(D, 2 * FF),
        down_flat.reshape(FF, D),
        gain_one.astype(jnp.float32),
        bias_one.astype(jnp.float32),
        gain_two.astype(jnp.float32),
        bias_two.astype(jnp.float32),
    )


def head_slice(array, offset, lanes):
    piece = lax.dynamic_slice_in_dim(array, offset, lanes, 2)
    return piece.reshape(array.shape[0], array.shape[1], 2, HEAD_DIM)


def pair_logits(query_pair, key_pair, same_doc):
    scores = jnp.einsum("sqhd,skhd->shqk", query_pair, key_pair, preferred_element_type=jnp.float32)
    return jnp.where(same_doc, scores * 0.125, masked_score)


def attend(queries, keys_all, values_all, same_doc):
    seq_count, row_count, feature_count = queries.shape
    lanes = 2 * HEAD_DIM

    def pair_step(head_pair, buffers):
        out_buffer, total_buffer = buffers
        offset = head_pair * lanes
        logits = pair_logits(
            head_slice(queries, offset, lanes), head_slice(keys_all, offset, lanes), same_doc
        )
        highest = jnp.max(logits, axis=-1, keepdims=True)
        log_total = highest + jnp.log(jnp.sum(jnp.exp(logits - highest), axis=-1, keepdims=True))
        probs_low = jnp.exp(logits - log_total).astype(jnp.bfloat16)
        attended = jnp.einsum(
            "shqk,skhd->sqhd",
            probs_low,
            head_slice(values_all, offset, lanes),
            preferred_element_type=jnp.float32,
        ).astype(jnp.bfloat16)
        out_buffer = lax.dynamic_update_slice_in_dim(
            out_buffer, attended.reshape(seq_count, row_count, lanes), offset, 2
        )
        total_buffer = lax.dynamic_update_slice_in_dim(
            total_buffer, log_total[..., 0], 2 * head_pair, 1
        )
        return (out_buffer, total_buffer)

    initial = (
        jnp.zeros((seq_count, row_count, feature_count), jnp.bfloat16),
        jnp.zeros((seq_count, HEADS, row_count), jnp.float32),
    )
    return lax.fori_loop(0, HEADS // 2, pair_step, initial)


def attend_back(queries, keys_all, values_all, same_doc, total_buffer, attended_grad):
    seq_count, row_count, feature_count = queries.shape
    key_count = keys_all.shape[1]
    lanes = 2 * HEAD_DIM

    def pair_step(head_pair, buffers):
        query_buffer, key_buffer, value_buffer = buffers
        offset = head_pair * lanes
        query_pair = head_slice(queries, offset, lanes)
        key_pair = head_slice(keys_all, offset, lanes)
        value_pair = head_slice(values_all, offset, lanes)
        grad_pair = head_slice(attended_grad, offset, lanes)
        logits = pair_logits(query_pair, key_pair, same_doc)
        log_total = lax.dynamic_slice_in_dim(total_buffer, 2 * head_pair, 2, 1)
        probs = jnp.exp(logits - log_total[..., None])
        prob_grad = jnp.einsum(
            "sqhd,skhd->shqk", grad_pair, value_pair, preferred_element_type=jnp.float32
        )
        logit_grad = probs * (prob_grad - jnp.sum(probs * prob_grad, axis=-1, keepdims=True))
        score_grad = (logit_grad * 0.125).astype(jnp.bfloat16)
        query_part = jnp.einsum(
            "shqk,skhd->sqhd", score_grad, key_pair, preferred_element_type=jnp.float32
        )
        key_part = jnp.einsum(
            "shqk,sqhd->skhd", score_grad, query_pair, preferred_element_type=jnp.float32
        )
        value_part = jnp.einsum(
            "shqk,sqhd->skhd",
            probs.astype(jnp.bfloat16),
            grad_pair,
            preferred_element_type=jnp.float32,
        )
        query_buffer = lax.dynamic_update_slice_in_dim(
            query_buffer, query_part.reshape(seq_count, row_count, lanes), offset, 2
        )
        key_buffer = lax.dynamic_update_slice_in_dim(
            key_buffer, key_part.reshape(seq_count, key_count, lanes), offset, 2
        )
        value_buffer = lax.dynamic_update_slice_in_dim(
            value_buffer, value_part.reshape(seq_count, key_count, lanes), offset, 2
        )
        return (query_buffer, key_buffer, value_buffer)

    initial = (
        jnp.zeros((seq_count, row_count, feature_count), jnp.float32),
        jnp.zeros((seq_count, key_count, feature_count), jnp.float32),
        jnp.zeros((seq_count, key_count, feature_count), jnp.float32),
    )
    return lax.fori_loop(0, HEADS // 2, pair_step, initial)


def local(
    tokens,
    segments,
    positions,
    qkv_weight,
    out_weight,
    gate_up_weight,
    down_weight,
    first_gain,
    first_bias,
    second_gain,
    second_bias,
    output_grad,
):
    seq_count = tokens.shape[0]
    row_count = tokens.shape[1]
    gathered = (
        lax.all_gather(qkv_weight, ("dp", "ctx"), axis=0, tiled=True),
        lax.all_gather(out_weight, ("dp", "ctx"), axis=0, tiled=True),
        lax.all_gather(gate_up_weight, ("dp", "ctx"), axis=0, tiled=True),
        lax.all_gather(down_weight, ("dp", "ctx"), axis=0, tiled=True),
        lax.all_gather(first_gain, ("dp", "ctx"), axis=0, tiled=True),
        lax.all_gather(first_bias, ("dp", "ctx"), axis=0, tiled=True),
        lax.all_gather(second_gain, ("dp", "ctx"), axis=0, tiled=True),
        lax.all_gather(second_bias, ("dp", "ctx"), axis=0, tiled=True),
    )
    qkv_mat, out_mat, gate_up_mat, down_mat, gain_one, bias_one, gain_two, bias_two = unpack(
        gathered
    )
    token_rows = tokens.reshape(seq_count * row_count, D)
    cosine_table, sine_table = rotary_tables(positions, HEAD_DIM)
    projected = jnp.dot(token_rows, qkv_mat, preferred_element_type=jnp.float32)
    projected = projected.reshape(seq_count, row_count, 3, HEADS, HEAD_DIM)
    queries = (
        rotate(projected[:, :, 0], cosine_table, sine_table)
        .astype(jnp.bfloat16)
        .reshape(seq_count, row_count, D)
    )
    keys_low = (
        rotate(projected[:, :, 1], cosine_table, sine_table)
        .astype(jnp.bfloat16)
        .reshape(seq_count, row_count, D)
    )
    values_low = projected[:, :, 2].astype(jnp.bfloat16).reshape(seq_count, row_count, D)
    key_ids = segments.astype(jnp.bfloat16)
    keys_all, values_all, ids_all = (
        lax.all_gather(keys_low, "ctx", axis=1, tiled=True),
        lax.all_gather(values_low, "ctx", axis=1, tiled=True),
        lax.all_gather(key_ids, "ctx", axis=1, tiled=True),
    )
    same_doc = (
        segments.astype(jnp.float32)[:, None, :, None]
        == ids_all.astype(jnp.float32)[:, None, None, :]
    )
    attended, total_buffer = attend(queries, keys_all, values_all, same_doc)
    attended_rows = attended.reshape(seq_count * row_count, D)
    branch = jnp.dot(attended_rows, out_mat, preferred_element_type=jnp.float32)
    normed_one, hat_one, recip_one = layer_norm(
        token_rows.astype(jnp.float32) + branch, gain_one, bias_one
    )
    normed_low = normed_one.astype(jnp.bfloat16)
    gate_up = jnp.dot(normed_low, gate_up_mat, preferred_element_type=jnp.float32)
    gate_part = gate_up[:, :FF]
    up_part = gate_up[:, FF:]
    sigmoid_gate = jax.nn.sigmoid(gate_part)
    silu_gate = gate_part * sigmoid_gate
    hidden = (silu_gate * up_part).astype(jnp.bfloat16)
    mlp_out = jnp.dot(hidden, down_mat, preferred_element_type=jnp.float32)
    result, hat_two, recip_two = layer_norm(normed_one + mlp_out, gain_two, bias_two)
    output = result.astype(jnp.bfloat16).reshape(tokens.shape)
    again = (
        lax.all_gather(qkv_weight, ("dp", "ctx"), axis=0, tiled=True),
        lax.all_gather(out_weight, ("dp", "ctx"), axis=0, tiled=True),
        lax.all_gather(gate_up_weight, ("dp", "ctx"), axis=0, tiled=True),
        lax.all_gather(down_weight, ("dp", "ctx"), axis=0, tiled=True),
        lax.all_gather(first_gain, ("dp", "ctx"), axis=0, tiled=True),
        lax.all_gather(first_bias, ("dp", "ctx"), axis=0, tiled=True),
        lax.all_gather(second_gain, ("dp", "ctx"), axis=0, tiled=True),
        lax.all_gather(second_bias, ("dp", "ctx"), axis=0, tiled=True),
    )
    qkv_mat, out_mat, gate_up_mat, down_mat, gain_one, bias_one, gain_two, bias_two = unpack(again)
    keys_all, values_all, ids_all = (
        lax.all_gather(keys_low, "ctx", axis=1, tiled=True),
        lax.all_gather(values_low, "ctx", axis=1, tiled=True),
        lax.all_gather(key_ids, "ctx", axis=1, tiled=True),
    )
    upstream = output_grad.reshape(seq_count * row_count, D).astype(jnp.float32)
    second_grad, second_gain_part, second_bias_part = norm_back(
        upstream, hat_two, recip_two, gain_two
    )
    mlp_grad = second_grad.astype(jnp.bfloat16)
    down_part = contract_rows(hidden, mlp_grad)
    hidden_grad = back_dot(mlp_grad, down_mat)
    gate_grad = hidden_grad * up_part * (sigmoid_gate * (1.0 + gate_part * (1.0 - sigmoid_gate)))
    up_grad = hidden_grad * silu_gate
    gate_up_grad = jnp.concatenate([gate_grad, up_grad], axis=1).astype(jnp.bfloat16)
    gate_up_part = contract_rows(normed_low, gate_up_grad)
    gate_up_flat = gate_up_part.reshape(-1)
    early = (
        lax.psum_scatter(gate_up_flat, ("dp", "ctx"), scatter_dimension=0, tiled=True),
        lax.psum_scatter(second_gain_part, ("dp", "ctx"), scatter_dimension=0, tiled=True),
        lax.psum_scatter(second_bias_part, ("dp", "ctx"), scatter_dimension=0, tiled=True),
    )
    gate_up_share, gain_two_share, bias_two_share = early
    normed_grad = second_grad + back_dot(gate_up_grad, gate_up_mat)
    first_grad, first_gain_part, first_bias_part = norm_back(
        normed_grad, hat_one, recip_one, gain_one
    )
    branch_grad = first_grad.astype(jnp.bfloat16)
    out_part = contract_rows(attended_rows, branch_grad)
    attended_grad = (
        back_dot(branch_grad, out_mat).astype(jnp.bfloat16).reshape(seq_count, row_count, D)
    )
    query_grad, key_partial, value_partial = attend_back(
        queries, keys_all, values_all, same_doc, total_buffer, attended_grad
    )
    key_grad, value_grad = (
        lax.psum_scatter(
            key_partial.astype(jnp.bfloat16), "ctx", scatter_dimension=1, tiled=True
        ).astype(jnp.float32),
        lax.psum_scatter(
            value_partial.astype(jnp.bfloat16), "ctx", scatter_dimension=1, tiled=True
        ).astype(jnp.float32),
    )
    head_shape = (seq_count, row_count, HEADS, HEAD_DIM)
    query_raw = rotate_back(query_grad.reshape(head_shape), cosine_table, sine_table).reshape(-1, D)
    key_raw = rotate_back(key_grad.reshape(head_shape), cosine_table, sine_table).reshape(-1, D)
    projected_grad = jnp.concatenate(
        [query_raw, key_raw, value_grad.reshape(-1, D)], axis=1
    ).astype(jnp.bfloat16)
    qkv_part = contract_rows(token_rows, projected_grad)
    input_grad = (back_dot(projected_grad, qkv_mat) + first_grad).reshape(tokens.shape)
    qkv_flat = qkv_part.reshape(-1)
    out_flat = out_part.reshape(-1)
    down_flat = down_part.reshape(-1)
    late = (
        lax.psum_scatter(qkv_flat, ("dp", "ctx"), scatter_dimension=0, tiled=True),
        lax.psum_scatter(out_flat, ("dp", "ctx"), scatter_dimension=0, tiled=True),
        lax.psum_scatter(down_flat, ("dp", "ctx"), scatter_dimension=0, tiled=True),
        lax.psum_scatter(first_gain_part, ("dp", "ctx"), scatter_dimension=0, tiled=True),
        lax.psum_scatter(first_bias_part, ("dp", "ctx"), scatter_dimension=0, tiled=True),
    )
    qkv_share, out_share, down_share, gain_one_share, bias_one_share = late
    return (
        output,
        input_grad,
        qkv_share,
        out_share,
        gate_up_share,
        down_share,
        gain_one_share,
        bias_one_share,
        gain_two_share,
        bias_two_share,
    )


PAIR = 2 * HEAD_DIM
HALF_D = D // 2
LOG2E = 1.4426950408889634
BF = jnp.bfloat16
F32 = jnp.float32
AXES = ("dp", "ctx")
LIGHT = pl.CostEstimate(flops=1024, bytes_accessed=1024, transcendentals=0)
SIDE, DEPTH = 2, 4
OWNERS = 2 * SIDE * SIDE * DEPTH
D_ROWS, FF_ROWS = D // OWNERS, FF // OWNERS
FF_HALF = FF // 2
FF_COLS = FF_HALF // (SIDE * SIDE)
NORM_COLS = 128
OUT_COLS = HALF_D + NORM_COLS
Q_COLS = 3 * HALF_D
NEAR_COLS = Q_COLS + OUT_COLS


def dot_nn(left, right):
    return lax.dot_general(left, right, (((1,), (0,)), ((), ())), preferred_element_type=F32)


def dot_nt(left, right):
    return lax.dot_general(left, right, (((1,), (1,)), ((), ())), preferred_element_type=F32)


def dot_tn(left, right):
    return lax.dot_general(left, right, (((0,), (0,)), ((), ())), preferred_element_type=F32)


def swap_halves(tile):
    lane = lax.broadcasted_iota(jnp.int32, tile.shape, 1)
    low_half = lax.rem(lane, HEAD_DIM) < HEAD_DIM // 2
    ahead = pltpu.roll(tile, PAIR - HEAD_DIM // 2, 1)
    behind = pltpu.roll(tile, HEAD_DIM // 2, 1)
    return jnp.where(low_half, ahead, behind)


def qkv_body(x_ref, w_ref, cos_ref, sin_ref, o_ref):
    product = dot_nn(x_ref[...], w_ref[...])
    part = pl.program_id(0)

    @pl.when(part < 2)
    def _():
        for c in range(HALF_D // PAIR):
            tile = product[:, c * PAIR : (c + 1) * PAIR]
            turned = tile * cos_ref[...] + swap_halves(tile) * sin_ref[...]
            o_ref[:, c * PAIR : (c + 1) * PAIR] = turned.astype(BF)

    @pl.when(part == 2)
    def _():
        o_ref[...] = product.astype(BF)


def project_qkv(tokens, weight, cosine, sine):
    rows = tokens.shape[0]
    tile = rows
    return pl.pallas_call(
        qkv_body,
        out_shape=jax.ShapeDtypeStruct((rows, 3 * HALF_D), BF),
        grid=(3, rows // tile),
        in_specs=[
            pl.BlockSpec((tile, D), lambda i, r: (r, 0)),
            pl.BlockSpec((D, HALF_D), lambda i, r: (0, i)),
            pl.BlockSpec((tile, PAIR), lambda i, r: (r, 0)),
            pl.BlockSpec((tile, PAIR), lambda i, r: (r, 0)),
        ],
        out_specs=pl.BlockSpec((tile, HALF_D), lambda i, r: (r, i)),
        cost_estimate=LIGHT,
        compiler_params=pltpu.CompilerParams(vmem_limit_bytes=32 * 2**20),
        name="project_qkv",
    )(tokens, weight, cosine, sine)


Q_TILE = 1024


def lane_head(shape):
    return lax.broadcasted_iota(jnp.int32, shape, 1) // HEAD_DIM


def row_head(shape):
    return lax.broadcasted_iota(jnp.int32, shape, 0) // HEAD_DIM


def attend_body(q_ref, k_ref, v_ref, segc_ref, segr_ref, o_ref, l_ref):
    keys = k_ref[...]
    values_t = v_ref[...].astype(F32).T.astype(BF)
    heads_down = row_head(values_t.shape)
    masked_values = [jnp.where(heads_down == h, values_t, jnp.zeros_like(values_t)) for h in range(2)]
    rows = q_ref.shape[0]
    scale = 0.125 * LOG2E
    for t in range(rows // Q_TILE):
        span = pl.ds(t * Q_TILE, Q_TILE)
        queries = q_ref[span, :]
        heads_across = lane_head(queries.shape)
        same = segc_ref[...] == segr_ref[:, span]
        total = jnp.zeros((PAIR, Q_TILE), F32)
        for h in range(2):
            scores = dot_nt(keys, jnp.where(heads_across == h, queries, jnp.zeros_like(queries)))
            scores = jnp.where(same, scores * scale, masked_score)
            highest = jnp.max(scores, axis=0, keepdims=True)
            weights = jnp.exp2(scores - highest)
            norm = jnp.sum(weights, axis=0, keepdims=True)
            l_ref[h : h + 1, span] = highest + jnp.log2(norm)
            total = total + dot_nn(masked_values[h], weights.astype(BF)) * (1.0 / norm)
        o_ref[span, :] = total.T.astype(BF)


def attend_pair(pair, qkv, seg_col, seg_row):
    rows = qkv.shape[0]
    pairs = HALF_D // PAIR
    return pl.pallas_call(
        attend_body,
        out_shape=(
            jax.ShapeDtypeStruct((rows, PAIR), BF),
            jax.ShapeDtypeStruct((8, rows), F32),
        ),
        grid=(1,),
        in_specs=[
            pl.BlockSpec((rows, PAIR), lambda i: (0, pair)),
            pl.BlockSpec((rows, PAIR), lambda i: (0, pairs + pair)),
            pl.BlockSpec((rows, PAIR), lambda i: (0, 2 * pairs + pair)),
            pl.BlockSpec((rows, 1), lambda i: (0, 0)),
            pl.BlockSpec((1, rows), lambda i: (0, 0)),
        ],
        out_specs=(
            pl.BlockSpec((rows, PAIR), lambda i: (0, 0)),
            pl.BlockSpec((8, rows), lambda i: (0, 0)),
        ),
        compiler_params=pltpu.CompilerParams(vmem_limit_bytes=40 * 2**20),
        cost_estimate=LIGHT,
        name="attend_pair",
    )(qkv, qkv, qkv, seg_col, seg_row)


def attend_back_body(
    q_ref, k_ref, v_ref, g_ref, l_ref, segc_ref, segr_ref, cos_ref, sin_ref, *others
):
    d_ref, dk_sum, dv_sum = others[-3:]
    keys = k_ref[...]
    values = v_ref[...]
    keys_t = keys.astype(F32).T.astype(BF)
    heads_down = row_head(keys_t.shape)
    masked_keys = [jnp.where(heads_down == h, keys_t, jnp.zeros_like(keys_t)) for h in range(2)]
    rows = q_ref.shape[0]
    scale = 0.125 * LOG2E
    for t in range(rows // Q_TILE):
        span = pl.ds(t * Q_TILE, Q_TILE)
        queries = q_ref[span, :]
        grads = g_ref[span, :]
        heads_across = lane_head(queries.shape)
        same = segc_ref[...] == segr_ref[:, span]
        dq_t = jnp.zeros((PAIR, Q_TILE), F32)
        dk_part = None
        dv_part = None
        for h in range(2):
            own_q = jnp.where(heads_across == h, queries, jnp.zeros_like(queries))
            own_g = jnp.where(heads_across == h, grads, jnp.zeros_like(grads))
            scores = dot_nt(keys, own_q)
            logits = jnp.where(same, scores * scale, masked_score)
            probs = jnp.exp2(logits - l_ref[h : h + 1, span])
            prob_grad = dot_nt(values, own_g)
            mixed = probs * prob_grad
            mean = jnp.sum(mixed, axis=0, keepdims=True)
            score_grad = (mixed - probs * mean).astype(BF)
            dv_new = dot_nn(probs.astype(BF), own_g)
            dk_new = dot_nn(score_grad, own_q)
            dv_part = dv_new if dv_part is None else dv_part + dv_new
            dk_part = dk_new if dk_part is None else dk_part + dk_new
            dq_t = dq_t + dot_nn(masked_keys[h], score_grad)
        if t == 0:
            dk_sum[...] = dk_part
            dv_sum[...] = dv_part
        else:
            dk_sum[...] += dk_part
            dv_sum[...] += dv_part
        dq = dq_t.T * 0.125
        d_ref[0, span, :] = (dq * cos_ref[span, :] - swap_halves(dq) * sin_ref[span, :]).astype(BF)
    dk = dk_sum[...] * 0.125
    d_ref[1] = (dk * cos_ref[...] - swap_halves(dk) * sin_ref[...]).astype(BF)
    d_ref[2] = dv_sum[...].astype(BF)


def attend_back_pair(pair, earlier, qkv, grads, totals, seg_col, seg_row, cosine, sine):
    rows = qkv.shape[0]
    pairs = HALF_D // PAIR
    column = pl.BlockSpec((rows, PAIR), lambda i: (0, pair))
    whole = pl.BlockSpec((rows, PAIR), lambda i: (0, 0))
    carried = [] if earlier is None else [earlier]
    return pl.pallas_call(
        attend_back_body,
        out_shape=jax.ShapeDtypeStruct((3, rows, HALF_D), BF),
        grid=(1,),
        in_specs=[
            column,
            pl.BlockSpec((rows, PAIR), lambda i: (0, pairs + pair)),
            pl.BlockSpec((rows, PAIR), lambda i: (0, 2 * pairs + pair)),
            column,
            pl.BlockSpec((8, rows), lambda i: (0, 0)),
            pl.BlockSpec((rows, 1), lambda i: (0, 0)),
            pl.BlockSpec((1, rows), lambda i: (0, 0)),
            whole,
            whole,
        ] + [pl.BlockSpec(memory_space=pl.ANY)] * len(carried),
        out_specs=pl.BlockSpec((3, rows, PAIR), lambda i: (0, 0, pair)),
        scratch_shapes=[pltpu.VMEM((rows, PAIR), F32), pltpu.VMEM((rows, PAIR), F32)],
        input_output_aliases={9: 0} if carried else {},
        compiler_params=pltpu.CompilerParams(vmem_limit_bytes=44 * 2**20),
        cost_estimate=LIGHT,
        name="attend_back_pair",
    )(qkv, qkv, qkv, grads, totals, seg_col, seg_row, cosine, sine, *carried)


def coordinates():
    place = lax.axis_index("dp")
    return place // (2 * SIDE), (place // 2) & 1, place & 1, lax.axis_index("ctx")


def whole(*shape):
    return pl.BlockSpec(shape, lambda *_: (0,) * len(shape))


def kernel(body, name, mebibytes, **arguments):
    return pl.pallas_call(
        body,
        compiler_params=pltpu.CompilerParams(vmem_limit_bytes=mebibytes * 2**20),
        cost_estimate=LIGHT,
        name=name,
        **arguments,
    )


def normalize(hidden_sum):
    centered = hidden_sum - jnp.mean(hidden_sum, axis=-1, keepdims=True)
    reciprocal = lax.rsqrt(jnp.mean(centered * centered, axis=-1, keepdims=True) + norm_epsilon)
    return centered * reciprocal, reciprocal


def norm_grad(upstream, normed, reciprocal, gain):
    grad = upstream * gain
    return reciprocal * (
        grad
        - jnp.mean(grad, axis=-1, keepdims=True)
        - normed * jnp.mean(grad * normed, axis=-1, keepdims=True)
    )


def add_sums(sums_ref, start, upstream, normed):
    first, second = pl.ds(start, 1), pl.ds(start + 1, 1)
    sums_ref[first, :] += jnp.sum(upstream * normed, axis=0, keepdims=True)
    sums_ref[second, :] += jnp.sum(upstream, axis=0, keepdims=True)


ROW_TILE = 256


def first_norm_body(a_ref, b_ref, w_ref, t_ref, p_ref, sum_ref, low_ref):
    total = t_ref[...].astype(F32)
    total = total + dot_nn(a_ref[...], w_ref[:HALF_D, :]) + dot_nn(b_ref[...], w_ref[HALF_D:, :])
    sum_ref[...] = total
    hat, _ = normalize(total)
    low_ref[...] = (hat * p_ref[0:1, :] + p_ref[1:2, :]).astype(BF)


def first_norm(attended_own, attended_got, out_mat, tokens, norms):
    rows = attended_own.shape[0]
    part = pl.BlockSpec((ROW_TILE, HALF_D), lambda i: (i, 0))
    full = pl.BlockSpec((ROW_TILE, D), lambda i: (i, 0))
    return kernel(
        first_norm_body,
        "first_norm",
        24,
        out_shape=(jax.ShapeDtypeStruct((rows, D), F32), jax.ShapeDtypeStruct((rows, D), BF)),
        grid=(rows // ROW_TILE,),
        in_specs=[part, part, whole(D, D), full, whole(8, D)],
        out_specs=(full, full),
    )(attended_own, attended_got, out_mat, tokens, norms)


FF_TILE = 256


def gate_up_body(x_ref, wg_ref, wu_ref, gate_ref, up_ref, h_ref):
    gate = dot_nn(x_ref[...], wg_ref[...])
    up_part = dot_nn(x_ref[...], wu_ref[...])
    gate_ref[...] = gate.astype(BF)
    up_ref[...] = up_part.astype(BF)
    h_ref[...] = (gate * lax.logistic(gate) * up_part).astype(BF)


def gate_up_forward(normed, weight):
    rows = normed.shape[0]
    tiles = FF_HALF // FF_TILE
    part = jax.ShapeDtypeStruct((rows, FF_HALF), BF)
    column = pl.BlockSpec((rows, FF_TILE), lambda i: (0, i))
    return kernel(
        gate_up_body,
        "gate_up_forward",
        24,
        out_shape=(part, part, part),
        grid=(tiles,),
        in_specs=[
            whole(rows, D),
            pl.BlockSpec((D, FF_TILE), lambda i: (0, i)),
            pl.BlockSpec((D, FF_TILE), lambda i: (0, tiles + i)),
        ],
        out_specs=(column, column, column),
    )(normed, weight, weight)


def second_norm_body(
    h_ref, w_ref, got_ref, sum_ref, p_ref, g_ref, result_ref, grad_ref, low_ref, sums_ref
):
    @pl.when(pl.program_id(0) == 0)
    def _():
        sums_ref[...] = jnp.zeros_like(sums_ref)

    hat, _ = normalize(sum_ref[...])
    total = hat * p_ref[0:1, :] + p_ref[1:2, :]
    total = total + dot_nn(h_ref[...], w_ref[...]) + got_ref[...].astype(F32)
    hat, reciprocal = normalize(total)
    gain = p_ref[2:3, :]
    result_ref[...] = (hat * gain + p_ref[3:4, :]).astype(BF)
    upstream = g_ref[...].astype(F32)
    add_sums(sums_ref, 2, upstream, hat)
    grad = norm_grad(upstream, hat, reciprocal, gain)
    grad_ref[...] = grad
    low_ref[...] = grad.astype(BF)


def second_norm(hidden, down_mat, got, first_sum, norms, output_grad):
    rows = hidden.shape[0]
    full = pl.BlockSpec((ROW_TILE, D), lambda i: (i, 0))
    return kernel(
        second_norm_body,
        "second_norm",
        32,
        out_shape=(
            jax.ShapeDtypeStruct((rows, D), BF),
            jax.ShapeDtypeStruct((rows, D), F32),
            jax.ShapeDtypeStruct((rows, D), BF),
            jax.ShapeDtypeStruct((8, D), F32),
        ),
        grid=(rows // ROW_TILE,),
        in_specs=[
            pl.BlockSpec((ROW_TILE, FF_HALF), lambda i: (i, 0)),
            whole(FF_HALF, D),
            full,
            full,
            whole(8, D),
            full,
        ],
        out_specs=(full, full, full, whole(8, D)),
    )(hidden, down_mat, got, first_sum, norms, output_grad)


def hidden_back_body(m_ref, w_ref, gate_ref, up_ref, o_ref):
    hidden_grad = dot_nt(m_ref[...], w_ref[...])
    gate, up_part = gate_ref[...].astype(F32), up_ref[...].astype(F32)
    sigmoid = lax.logistic(gate)
    o_ref[0] = (hidden_grad * up_part * (sigmoid * (1.0 + gate * (1.0 - sigmoid)))).astype(BF)
    o_ref[1] = (hidden_grad * (gate * sigmoid)).astype(BF)


def hidden_back(mlp_grad, down_mat, gate, up_part):
    rows = mlp_grad.shape[0]
    column = pl.BlockSpec((rows, FF_TILE), lambda i: (0, i))
    return kernel(
        hidden_back_body,
        "hidden_back",
        24,
        out_shape=jax.ShapeDtypeStruct((2, rows, FF_HALF), BF),
        grid=(FF_HALF // FF_TILE,),
        in_specs=[whole(rows, D), pl.BlockSpec((FF_TILE, D), lambda i: (i, 0)), column, column],
        out_specs=pl.BlockSpec((2, rows, FF_TILE), lambda i: (0, 0, i)),
    )(mlp_grad, down_mat, gate, up_part)


def normed_part_body(g_ref, w_ref, o_ref, acc_ref):
    product = dot_nt(g_ref[0], w_ref[...])
    step = pl.program_id(0)

    @pl.when(step == 0)
    def _():
        acc_ref[...] = product

    @pl.when(step > 0)
    def _():
        acc_ref[...] += product

    @pl.when(step == pl.num_programs(0) - 1)
    def _():
        o_ref[...] = acc_ref[...].astype(BF)


BACK_TILE = 768


def normed_part(grads, weight):
    rows = grads.shape[1]
    tiles = FF_HALF // BACK_TILE
    return kernel(
        normed_part_body,
        "normed_part",
        24,
        out_shape=jax.ShapeDtypeStruct((rows, D), BF),
        grid=(2 * tiles,),
        in_specs=[
            pl.BlockSpec((1, rows, BACK_TILE), lambda i: (i // tiles, 0, i % tiles)),
            pl.BlockSpec((D, BACK_TILE), lambda i: (0, i)),
        ],
        out_specs=whole(rows, D),
        scratch_shapes=[pltpu.VMEM((rows, D), F32)],
    )(grads, weight)


def first_back_body(
    g_ref, w_ref, got_ref, upper_ref, sum_ref, p_ref, out_ref, s_ref, grad_ref, own_ref, give_ref, sums_ref, acc_ref
):
    product = dot_nt(g_ref[0], w_ref[...])
    step = pl.program_id(0)

    @pl.when(step == 0)
    def _():
        acc_ref[...] = product

    @pl.when(step > 0)
    def _():
        acc_ref[...] += product

    @pl.when(step == pl.num_programs(0) - 1)
    def _():
        sums_ref[...] = s_ref[...]
        for n in range(acc_ref.shape[0] // ROW_TILE):
            span = pl.ds(n * ROW_TILE, ROW_TILE)
            upstream = acc_ref[span, :] + got_ref[span, :].astype(F32) + upper_ref[span, :]
            hat, reciprocal = normalize(sum_ref[span, :])
            add_sums(sums_ref, 0, upstream, hat)
            grad = norm_grad(upstream, hat, reciprocal, p_ref[0:1, :])
            grad_ref[span, :] = grad
            low = grad.astype(BF)
            own_ref[span, :] = dot_nt(low, out_ref[:HALF_D, :]).astype(BF)
            give_ref[span, :] = dot_nt(low, out_ref[HALF_D:, :]).astype(BF)


def first_back(grads, weight, got, second_grad, first_sum, norms, out_mat, sums):
    rows = grads.shape[1]
    tiles = FF_HALF // BACK_TILE
    part = jax.ShapeDtypeStruct((rows, HALF_D), BF)
    return kernel(
        first_back_body,
        "first_back",
        40,
        out_shape=(
            jax.ShapeDtypeStruct((rows, D), F32),
            part,
            part,
            jax.ShapeDtypeStruct((8, D), F32),
        ),
        grid=(2 * tiles,),
        in_specs=[
            pl.BlockSpec((1, rows, BACK_TILE), lambda i: (i // tiles, 0, i % tiles)),
            pl.BlockSpec((D, BACK_TILE), lambda i: (0, i)),
            whole(rows, D),
            whole(rows, D),
            whole(rows, D),
            whole(8, D),
            whole(D, D),
            whole(8, D),
        ],
        out_specs=(whole(rows, D), whole(rows, HALF_D), whole(rows, HALF_D), whole(8, D)),
        scratch_shapes=[pltpu.VMEM((rows, D), F32)],
    )(grads, weight, got, second_grad, first_sum, norms, out_mat, sums)


def out_part_body(a_ref, b_ref, g_ref, s_ref, keep_ref, give_ref):
    _, _, k, _ = coordinates()
    low = g_ref[...].astype(BF)
    parts = [dot_tn(a_ref[...], low), dot_tn(b_ref[...], low)]
    pad = jnp.zeros((NORM_COLS - 8, D), F32)
    sums = jnp.concatenate([s_ref[...], pad], axis=0).T
    for n in range(2):
        rows = jnp.where(k == n, parts[0], parts[1])
        left, right = rows[:, :HALF_D], rows[:, HALF_D:]
        span = slice(n * HALF_D, (n + 1) * HALF_D)
        keep_ref[span, :HALF_D] = jnp.where(k == 0, left, right)
        give_ref[span, :HALF_D] = jnp.where(k == 0, right, left).astype(BF)
    keep_ref[:, HALF_D:] = sums
    give_ref[:, HALF_D:] = sums.astype(BF)


def out_weight_part(attended_own, attended_got, first_grad, sums):
    rows = attended_own.shape[0]
    return kernel(
        out_part_body,
        "out_weight_part",
        32,
        out_shape=(
            jax.ShapeDtypeStruct((D, OUT_COLS), F32),
            jax.ShapeDtypeStruct((D, OUT_COLS), BF),
        ),
    )(attended_own, attended_got, first_grad, sums)


CHUNK = DEPTH * D_ROWS


def store_split(product, x, y, a_keep, a_send, b_keep, b_send, span=slice(None)):
    def block(yy, xx, kk):
        start = ((yy * SIDE + xx) * 2 + kk) * CHUNK
        return product[start : start + CHUNK]

    for n in range(2):
        a_keep[n, :, span] = jnp.where(x == 0, block(n, 0, 0), block(n, 1, 0))
        a_send[n, :, span] = jnp.where(x == 0, block(n, 1, 0), block(n, 0, 0))
        b_keep[n, :, span] = jnp.where(y == 0, block(0, n, 1), block(1, n, 1))
        b_send[n, :, span] = jnp.where(y == 0, block(1, n, 1), block(0, n, 1))


def second_split_body(a_ref, a_got, b_ref, b_got, a_keep, a_send, b_keep, b_send):
    y, x, _, _ = coordinates()
    for own, got, keep, send, index in (
        (a_ref, a_got, a_keep, a_send, y),
        (b_ref, b_got, b_keep, b_send, x),
    ):
        keep[...] = own[index].astype(F32) + got[index].astype(F32)
        send[...] = (own[1 - index].astype(F32) + got[1 - index].astype(F32)).astype(BF)


def second_split(a_keep, a_got, b_keep, b_got):
    cols = a_keep.shape[-1]
    keep, send = (jax.ShapeDtypeStruct((CHUNK, cols), kind) for kind in (F32, BF))
    return kernel(second_split_body, "second_split", 32, out_shape=(keep, send, keep, send))(
        a_keep, a_got, b_keep, b_got
    )


def far_split_body(a_ref, a_got, b_ref, b_got, sum_ref, up_ref, down_ref):
    _, _, _, z = coordinates()
    for n, (own, got) in enumerate(((a_ref, a_got), (b_ref, b_got))):
        total = own[...] + got[...].astype(F32)
        for m in range(DEPTH):
            sum_ref[m, n] = total[m * D_ROWS : (m + 1) * D_ROWS]
    far = (z + 2) & 3
    up_ref[...] = sum_ref[far, 0].astype(BF)
    down_ref[...] = sum_ref[far, 1].astype(BF)


def far_split(a_keep, a_got, b_keep, b_got):
    cols = a_keep.shape[-1]
    send = jax.ShapeDtypeStruct((D_ROWS, cols), BF)
    return kernel(
        far_split_body,
        "far_split",
        32,
        out_shape=(jax.ShapeDtypeStruct((DEPTH, 2, D_ROWS, cols), F32), send, send),
    )(a_keep, a_got, b_keep, b_got)


def close_split_body(sum_ref, first_ref, second_ref, up_ref, down_ref):
    _, _, _, z = coordinates()
    above, below = (z + 1) & 3, (z + 3) & 3
    up_ref[0] = (sum_ref[above, 0] + first_ref[...].astype(F32)).astype(BF)
    up_ref[1] = sum_ref[above, 1].astype(BF)
    down_ref[0] = sum_ref[below, 0].astype(BF)
    down_ref[1] = (sum_ref[below, 1] + second_ref[...].astype(F32)).astype(BF)


def close_split(sums, first, second):
    send = jax.ShapeDtypeStruct(sums.shape[1:], BF)
    return kernel(close_split_body, "close_split", 24, out_shape=(send, send))(sums, first, second)


def core_split_body(sum_ref, up_ref, down_ref, keep_ref, send_ref):
    _, _, k, z = coordinates()

    def total(index):
        return sum_ref[z, index] + up_ref[index].astype(F32) + down_ref[index].astype(F32)

    keep_ref[...] = total(k)
    send_ref[...] = total(1 - k)[:, : send_ref.shape[1]].astype(BF)


def core_split(sums, from_below, from_above, give_cols):
    return kernel(
        core_split_body,
        "core_split",
        24,
        out_shape=(
            jax.ShapeDtypeStruct(sums.shape[2:], F32),
            jax.ShapeDtypeStruct((D_ROWS, give_cols), BF),
        ),
    )(sums, from_below, from_above)


def near_part_body(x_ref, g_ref, out_ref, got_ref, a_keep, a_send, b_keep, b_send):
    y, x, _, _ = coordinates()
    outs = (a_keep, a_send, b_keep, b_send)
    for n in range(3):
        product = dot_tn(x_ref[...], g_ref[n]).astype(BF)
        store_split(product, x, y, *outs, span=slice(n * HALF_D, (n + 1) * HALF_D))
    rest = (out_ref[...] + got_ref[...].astype(F32)).astype(BF)
    store_split(rest, x, y, *outs, span=slice(Q_COLS, NEAR_COLS))


def near_weight_part(tokens, grads, out_keep, out_got):
    part = jax.ShapeDtypeStruct((SIDE, CHUNK, NEAR_COLS), BF)
    return kernel(near_part_body, "near_weight_part", 40, out_shape=(part,) * 4)(
        tokens, grads, out_keep, out_got
    )


def gate_up_part_body(x_ref, y_ref, g_ref, h_ref, *outs):
    y, x, _, _ = coordinates()
    product = (dot_tn(x_ref[...], g_ref[0]) + dot_tn(y_ref[...], h_ref[0])).astype(BF)
    store_split(product, x, y, *outs)


def row_sum_body(x_ref, y_ref, g_ref, h_ref, o_ref):
    o_ref[...] = (dot_tn(x_ref[...], g_ref[...]) + dot_tn(y_ref[...], h_ref[...])).astype(BF)


def gate_up_weight_part(normed, grads):
    rows, tile = normed[0].shape[0], 512
    tiles = FF_HALF // tile
    column = pl.BlockSpec((1, rows, tile), lambda i: (i // tiles, 0, i % tiles))
    return kernel(
        gate_up_part_body,
        "gate_up_weight_part",
        24,
        out_shape=(jax.ShapeDtypeStruct((SIDE, CHUNK, FF), BF),) * 4,
        grid=(FF // tile,),
        in_specs=[whole(rows, D), whole(rows, D), column, column],
        out_specs=(pl.BlockSpec((SIDE, CHUNK, tile), lambda i: (0, 0, i)),) * 4,
    )(*normed, *grads)


def down_weight_part(hidden, grads):
    rows, tile = hidden[0].shape[0], 512
    column = pl.BlockSpec((rows, tile), lambda i: (0, i))
    return kernel(
        row_sum_body,
        "down_weight_part",
        24,
        out_shape=jax.ShapeDtypeStruct((FF_HALF, D), BF),
        grid=(FF_HALF // tile,),
        in_specs=[column, column, whole(rows, D), whole(rows, D)],
        out_specs=pl.BlockSpec((tile, D), lambda i: (i, 0)),
    )(*hidden, *grads)


def input_part_body(g_ref, w_ref, o_ref):
    total = dot_nt(g_ref[0], w_ref[:, :HALF_D])
    for n in range(1, 3):
        total = total + dot_nt(g_ref[n], w_ref[:, n * HALF_D : (n + 1) * HALF_D])
    o_ref[...] = total.astype(o_ref.dtype)


def input_part(grads, weight, block, dtype):
    rows = grads.shape[1] // 2
    return pl.pallas_call(
        input_part_body,
        out_shape=jax.ShapeDtypeStruct((rows, D), dtype),
        grid=(1,),
        in_specs=[
            pl.BlockSpec((3, rows, HALF_D), lambda i: (0, block, 0)),
            pl.BlockSpec((D, 3 * HALF_D), lambda i: (0, 0)),
        ],
        out_specs=pl.BlockSpec((rows, D), lambda i: (0, 0)),
        compiler_params=pltpu.CompilerParams(vmem_limit_bytes=24 * 2**20),
        cost_estimate=LIGHT,
        name="input_part",
    )(grads, weight)


def at(array, index, axis=0):
    return lax.dynamic_index_in_dim(array, index, axis, keepdims=False)


def after(value, earlier):
    return lax.optimization_barrier((value, earlier))[0]


def place(pieces, shapes, moves):
    dtype = pieces[0].dtype
    count = len(moves(0, 0, 0, 0))
    inputs = len(pieces)

    def body(*refs):
        sources, results, sems = refs[:inputs], refs[inputs:-1], refs[-1]
        copies = []
        for n, (piece, part, result, spot) in enumerate(moves(*coordinates())):
            source = sources[piece] if part is None else sources[piece].at[part]
            copies.append(pltpu.make_async_copy(source, results[result].at[spot], sems.at[n]))
        for copy in copies:
            copy.start()
        for copy in copies:
            copy.wait()

    anywhere = pl.BlockSpec(memory_space=pl.ANY)
    size = sum(math.prod(shape) for shape in shapes) * 2 * jnp.dtype(dtype).itemsize
    return pl.pallas_call(
        body,
        out_shape=tuple(jax.ShapeDtypeStruct(shape, dtype) for shape in shapes),
        in_specs=[anywhere] * inputs,
        out_specs=tuple(pl.BlockSpec(memory_space=pltpu.VMEM) for _ in shapes),
        scratch_shapes=[pltpu.SemaphoreType.DMA((count,))],
        compiler_params=pltpu.CompilerParams(vmem_limit_bytes=max(8 * 2**20, 2 * size)),
        cost_estimate=LIGHT,
        name="place",
    )(*pieces)


def move(array, target):
    pairs = []
    for y in range(SIDE):
        for x in range(SIDE):
            for k in range(2):
                for z in range(DEPTH):
                    ty, tx, tk, tz = target(y, x, k, z)
                    source = ((y * SIDE + x) * 2 + k) * DEPTH + z
                    goal = ((ty * SIDE + tx) * 2 + tk) * DEPTH + tz % DEPTH
                    pairs.append((source, goal))
    return lax.ppermute(array, AXES, pairs)


def core(array):
    return move(array, lambda y, x, k, z: (y, x, 1 - k, z))


def across_x(array):
    return move(array, lambda y, x, k, z: (y, 1 - x, k, z))


def across_y(array):
    return move(array, lambda y, x, k, z: (1 - y, x, k, z))


def up(array):
    return move(array, lambda y, x, k, z: (y, x, k, z + 1))


def down(array):
    return move(array, lambda y, x, k, z: (y, x, k, z - 1))


def order(index, own, other, axis=0):
    first = jnp.where(index == 0, own, other)
    second = jnp.where(index == 0, other, own)
    return jnp.stack([first, second], axis)


def ring_near(array):
    return down(array), up(array)


def ring_far(above, below):
    half = above.shape[0] // 2
    return up(below[:half]), down(above[half:])


def pair_x(array, got):
    return place(
        (array, got), [(SIDE, *array.shape)], lambda y, x, k, z: [(n, None, 0, (x ^ n,)) for n in range(2)]
    )[0]


def pair_y(array, got):
    return place(
        (array, got), [(SIDE, *array.shape)], lambda y, x, k, z: [(n, None, 0, (y ^ n,)) for n in range(2)]
    )[0]


def spread_z(block, pieces):
    both = range(2)
    return place(
        (block, *pieces),
        [(DEPTH, *block.shape[1:])] * 2,
        lambda y, x, k, z: [
            (n, (m,), m, ((z + step) & 3,)) for n, step in ((0, 0), (1, 1), (2, 3)) for m in both
        ] + [(3 + m, (0,), m, ((z + 2) & 3,)) for m in both],
    )


def scatter(array, index, across, axis=0, gate=None):
    got = across(at(array, 1 - index, axis).astype(BF))
    if gate is not None:
        got = after(got, gate)
    return at(array, index, axis).astype(F32) + got.astype(F32)


def scatter_far(array, z, axis):
    far = at(array, (z + 2) & 3, axis).astype(BF)
    half = far.shape[0] // 2
    return up(far[:half]), down(far[half:])


def scatter_near(array, z, axis, first, second):
    above, below = at(array, (z + 1) & 3, axis), at(array, (z + 3) & 3, axis)
    half = above.shape[0] // 2
    sum_above = (above[:half].astype(F32) + first.astype(F32)).astype(BF)
    sum_below = (below[half:].astype(F32) + second.astype(F32)).astype(BF)
    got_a = up(jnp.concatenate([sum_above, above[half:].astype(BF)], 0))
    got_b = down(jnp.concatenate([below[:half].astype(BF), sum_below], 0))
    return got_a, got_b


def scatter_own(array, z, axis, got_a, got_b):
    return at(array, z, axis).astype(F32) + got_a.astype(F32) + got_b.astype(F32)


def sequence_step(r):
    return lambda y, x, k, z: (y, x, z // 2, 2 * k + ((r + z) & 1))


def to_sequence(blocks, z):
    return [move(at(blocks, (z + r) & 1), sequence_step(r)) for r in range(2)]


def from_sequence(quarters):
    return [move(quarters[r], sequence_step(r)) for r in range(2)]


def chip_local(
    tokens,
    segments,
    positions,
    qkv_weight,
    out_weight,
    gate_up_weight,
    down_weight,
    first_gain,
    first_bias,
    second_gain,
    second_bias,
    output_grad,
):
    y, x, k, z = coordinates()
    quarter = tokens.shape[1]
    rows = DEPTH * quarter
    half = rows // 2
    planes = SIDE * SIDE

    norms = jnp.stack([first_gain, first_bias, second_gain, second_bias], axis=1)
    norms = jnp.pad(norms, ((0, 0), (0, NORM_COLS - 4)))
    qkv_own = qkv_weight.reshape(D_ROWS, 3 * D)
    gate_up_own = gate_up_weight.reshape(D_ROWS, 2 * FF)
    out_own = out_weight.reshape(D_ROWS, D)

    def column_half(index):
        def part(matrix, start, width):
            left, right = matrix[:, start : start + width], matrix[:, start + width : start + 2 * width]
            return jnp.where(index == 0, left, right)

        pieces = [part(qkv_own, n * D, HALF_D) for n in range(3)]
        pieces += [part(out_own, 0, HALF_D), norms]
        pieces += [part(gate_up_own, n * 2 * FF_COLS, FF_COLS) for n in range(2 * planes)]
        return jnp.concatenate(pieces, axis=1)

    mine, theirs = column_half(k), core(column_half(1 - k))
    both, every = range(2), slice(None)
    near_span, gate_up_span = pl.ds(0, NEAR_COLS), pl.ds(NEAR_COLS, FF)
    near_block, gate_up_block = place(
        (mine, theirs),
        [(2, D_ROWS, NEAR_COLS), (2, D_ROWS, FF)],
        lambda y, x, k, z: [
            (n, (every, span), r, (k ^ n,)) for n in both for r, span in enumerate((near_span, gate_up_span))
        ],
    )

    near_close = ring_near(near_block)
    near_ring = (*near_close, *ring_far(*near_close))
    near_a, near_b = spread_z(near_block, near_ring)
    down_x = down_weight.reshape(FF_ROWS, D)
    down_x = pair_x(down_x, across_x(down_x))
    near_a, near_b, down_x = lax.optimization_barrier((near_a, near_b, down_x))
    near_ax = pair_x(near_a, across_x(near_a))
    near_by = pair_y(near_b, across_y(near_b))
    down_x = (down_x, across_y(down_x))
    gate_up_close = ring_near(after(gate_up_block, near_ring))
    gate_up_far = ring_far(*gate_up_close)

    extra = jnp.stack([segments, positions >> 5, positions & 31], axis=1).astype(BF)
    extra = jnp.pad(extra, ((0, 0), (0, 13), (0, D - quarter)))
    packed = after(jnp.concatenate([tokens, extra], axis=1), gate_up_far[0])
    own_tokens = jnp.concatenate(to_sequence(packed, z), axis=0)
    other_tokens = core(own_tokens)
    blocks = jnp.concatenate([own_tokens, other_tokens], 0).reshape(DEPTH, quarter + 16, D)
    all_tokens = blocks[:, :quarter].reshape(rows, D)
    all_extra = blocks[:, quarter:, :quarter].astype(F32)
    seg_all = all_extra[:, 0].reshape(rows)
    pos_all = (all_extra[:, 1] * 32.0 + all_extra[:, 2]).reshape(rows)
    lane = jnp.arange(PAIR)
    counter = (lane & (HEAD_DIM // 2 - 1)).astype(F32)
    inverse = jnp.exp(counter * (-2.0 * math.log(rotary_base) / HEAD_DIM))
    angles = pos_all[:, None] * inverse
    cosine = jnp.cos(angles)
    sine = jnp.where((lane & (HEAD_DIM - 1)) < HEAD_DIM // 2, -1.0, 1.0) * jnp.sin(angles)
    seg_col, seg_row = seg_all[:, None], seg_all[None, :]

    qkv_mat, out_half = place(
        (near_ax, across_y(near_ax), near_by, across_x(near_by)),
        [(SIDE, SIDE, 2, DEPTH, D_ROWS, Q_COLS), (SIDE, SIDE, 2, DEPTH, D_ROWS, OUT_COLS)],
        lambda y, x, k, z: [
            (n, (row, every, every, cols), r, ((y ^ n) ^ (k * r), row, 0))
            for n in both for row in both for r, cols in ((0, pl.ds(0, Q_COLS)), (1, pl.ds(Q_COLS, OUT_COLS)))
        ] + [
            (2 + n, (row, every, every, cols), r, (row ^ (k * r), x ^ n, 1))
            for n in both for row in both for r, cols in ((0, pl.ds(0, Q_COLS)), (1, pl.ds(Q_COLS, OUT_COLS)))
        ],
    )
    qkv_mat, out_half = qkv_mat.reshape(D, Q_COLS), out_half.reshape(D, OUT_COLS)

    out_other = core(out_half)
    swapped = jnp.concatenate([out_other[HALF_D:, :HALF_D], out_other[:HALF_D, :HALF_D]], axis=0)
    own_cols = out_half[:, :HALF_D]
    out_mat = jnp.concatenate(
        [jnp.where(k == 0, own_cols, swapped), jnp.where(k == 0, swapped, own_cols)], axis=1
    )
    norms_all = out_half[:, HALF_D : HALF_D + 8].astype(F32)
    norms_all = jnp.where(k == 0, norms_all, jnp.roll(norms_all, HALF_D, axis=0)).T

    gate_up_a, gate_up_b = spread_z(gate_up_block, (*gate_up_close, *gate_up_far))
    gate_up_ax = pair_x(gate_up_a, across_x(gate_up_a))
    gate_up_by = pair_y(gate_up_b, across_y(gate_up_b))

    token_half = all_tokens[:half]
    all_tokens, gate_up_ax, gate_up_by = lax.optimization_barrier((all_tokens, gate_up_ax, gate_up_by))
    qkv = project_qkv(all_tokens, qkv_mat, cosine, sine)
    down_y = pair_y(*after(down_x, other_tokens)).reshape(planes, FF_ROWS, D)
    down_close = ring_near(down_y)
    pairs = range(HALF_D // PAIR)
    attended, totals = [], []
    for pair in pairs:
        if pair:
            qkv, attended[-1] = lax.optimization_barrier((qkv, attended[-1]))
        one, total = attend_pair(pair, qkv, seg_col, seg_row)
        attended.append(one)
        totals.append(total)
    gate_up_mat = place(
        (gate_up_ax, across_y(gate_up_ax), gate_up_by, across_x(gate_up_by)),
        [(SIDE, SIDE, 2, DEPTH, D_ROWS, FF)],
        lambda y, x, k, z: [
            (n, (row,), 0, (y ^ n, row, 0)) for n in both for row in both
        ] + [(2 + n, (row,), 0, (row, x ^ n, 1)) for n in both for row in both],
    )[0].reshape(D, FF)
    attended = jnp.concatenate(attended, axis=1)
    attended_own, attended_got = attended[:half], core(attended[half:])
    down_ring = (*down_close, *ring_far(*after(down_close, attended_got)))
    first, second = pl.ds(0, planes // 2), pl.ds(planes // 2, planes // 2)
    first_sum, normed_own = first_norm(attended_own, attended_got, out_mat, token_half, norms_all)
    normed_got = core(normed_own)
    grad_quarters = to_sequence(after(output_grad, down_ring[-2:]), z)
    gate_own, up_own, hidden_own = gate_up_forward(normed_own, gate_up_mat)
    gate_got, up_got, hidden_got = gate_up_forward(after(normed_got, hidden_own), gate_up_mat)
    down_ring = after(down_ring, hidden_got)
    down_mat = place(
        (down_y, *down_ring),
        [(planes, DEPTH, FF_ROWS, D)],
        lambda y, x, k, z: [
            (0, None, 0, (every, z)),
            (1, None, 0, (every, (z + 1) & 3)),
            (2, None, 0, (every, (z + 3) & 3)),
            (3, None, 0, (first, (z + 2) & 3)),
            (4, None, 0, (second, (z + 2) & 3)),
        ],
    )[0].reshape(FF_HALF, D)
    down_mat, grad_quarters = lax.optimization_barrier((down_mat, grad_quarters))
    mlp_got = core(dot_nn(hidden_got, down_mat).astype(BF))
    grad_half = jnp.concatenate(grad_quarters, axis=0)
    result, second_grad, mlp_own, sums = second_norm(
        hidden_own, down_mat, mlp_got, first_sum, norms_all, grad_half
    )

    other_grad = core(mlp_own)
    output_got = from_sequence([result[:quarter], result[quarter:]])
    gate_up_own = hidden_back(mlp_own, down_mat, gate_own, up_own)
    gate_up_other = hidden_back(after(other_grad, gate_up_own), down_mat, gate_got, up_got)
    normed_back = normed_part(gate_up_other, gate_up_mat)
    normed_got_back = core(normed_back)
    down_part = down_weight_part((hidden_own, hidden_got), (mlp_own, after(other_grad, normed_back)))
    gate_up_part = gate_up_weight_part(
        (normed_own, normed_got), (gate_up_own, after(gate_up_other, down_part))
    )
    first_grad, attended_mine, attended_give, sums = first_back(
        gate_up_own,
        gate_up_mat,
        after(normed_got_back, (gate_up_part, output_got)),
        second_grad,
        first_sum,
        norms_all,
        out_mat,
        sums,
    )
    attended_grad = jnp.concatenate([attended_mine, core(attended_give)], axis=0)

    output = order(z & 1, output_got[0], output_got[1])
    down_part = down_part.reshape(planes, DEPTH, FF_ROWS, D)
    down_far = scatter_far(down_part, z, 1)
    down_near = scatter_near(down_part, z, 1, *after(down_far, first_grad))
    far_ak, far_as, far_bk, far_bs = gate_up_part
    far_as, far_bs = across_x(far_as), across_y(far_bs)

    out_keep, out_give = out_weight_part(attended_own, attended_got, first_grad, sums)
    out_got = core(out_give)

    projected_grad = None
    for pair in pairs:
        if pair == 1:
            far_as, far_bs = after((far_as, far_bs), projected_grad)
            far_ak, far_as, far_bk, far_bs = second_split(far_ak, far_as, far_bk, far_bs)
            attended_grad, far_ak, projected_grad = lax.optimization_barrier(
                (attended_grad, far_ak, projected_grad)
            )
            far_as, far_bs = across_y(far_as), across_x(far_bs)
        if pair == 2:
            far_as, far_bs, down_near = after((far_as, far_bs, down_near), projected_grad)
            down_z = scatter_own(down_part, z, 1, *down_near)
            far_sum, far_up, far_down = far_split(far_ak, far_as, far_bk, far_bs)
            attended_grad, far_sum, down_z, projected_grad = lax.optimization_barrier(
                (attended_grad, far_sum, down_z, projected_grad)
            )
            far_up, far_down = up(far_up), down(far_down)
            down_y = across_y(at(down_z.reshape(SIDE, SIDE, FF_ROWS, D), 1 - y).astype(BF))
        projected_grad = attend_back_pair(
            pair, projected_grad, qkv, attended_grad, totals[pair], seg_col, seg_row, cosine, sine
        )
    far_up, far_down, down_y = after((far_up, far_down, down_y), projected_grad)
    down_y = at(down_z.reshape(SIDE, SIDE, FF_ROWS, D), y) + down_y.astype(F32)
    far_up, far_down = close_split(far_sum, far_up, far_down)
    input_give = input_part(projected_grad, qkv_mat, 1, BF)
    projected_grad, far_up, far_down, input_give = lax.optimization_barrier(
        (projected_grad, far_up, far_down, input_give)
    )
    far_up, far_down = up(far_up), down(far_down)
    input_got = core(input_give)
    near_ak, near_as, near_bk, near_bs = near_weight_part(
        all_tokens, projected_grad, out_keep, out_got
    )
    near_as, near_bs = across_x(near_as), across_y(near_bs)
    input_own = input_part(after(projected_grad, near_ak), qkv_mat, 0, F32)
    input_half = (first_grad + input_own + input_got.astype(F32)).astype(BF)
    near_as, near_bs = after((near_as, near_bs), input_half)
    near_ak, near_as, near_bk, near_bs = second_split(near_ak, near_as, near_bk, near_bs)
    near_as, near_bs = across_y(near_as), across_x(near_bs)
    down_x = after(across_x(at(down_y, 1 - x).astype(BF)), near_ak)
    down_share = (at(down_y, x) + down_x.astype(F32)).reshape(-1)
    far_up, far_down = after((far_up, far_down), near_ak)
    far_own, far_give = core_split(far_sum, far_up, far_down, FF)
    far_got = core(far_give).astype(F32)
    near_sum, near_up, near_down = far_split(near_ak, near_as, near_bk, near_bs)
    near_up, near_down = close_split(near_sum, up(near_up), down(near_down))
    gate_up_share = order(
        k,
        far_own.reshape(D_ROWS, 2 * planes, FF_COLS),
        after(far_got, near_up).reshape(D_ROWS, 2 * planes, FF_COLS),
        2,
    ).reshape(-1)
    near_own, near_give = core_split(near_sum, up(near_up), down(near_down), Q_COLS + HALF_D)
    near_got = core(near_give).astype(F32)
    qkv_share = order(
        k,
        near_own[:, :Q_COLS].reshape(D_ROWS, 3, HALF_D),
        near_got[:, :Q_COLS].reshape(D_ROWS, 3, HALF_D),
        2,
    ).reshape(-1)
    out_share = order(k, near_own[:, Q_COLS : Q_COLS + HALF_D], near_got[:, Q_COLS:], 1).reshape(-1)
    norm_share = near_own[:, Q_COLS + HALF_D : Q_COLS + HALF_D + 4].T
    input_grad = from_sequence([input_half[:quarter], input_half[quarter:]])
    input_grad = order(z & 1, input_grad[0], input_grad[1]).astype(F32)
    return (
        output,
        input_grad,
        qkv_share,
        out_share,
        gate_up_share,
        down_share,
        norm_share[0],
        norm_share[1],
        norm_share[2],
        norm_share[3],
    )


def solution(mesh):
    in_specs = (
        P("dp", "ctx", None),
        P("dp", "ctx"),
        P("dp", "ctx"),
        P(("dp", "ctx")),
        P(("dp", "ctx")),
        P(("dp", "ctx")),
        P(("dp", "ctx")),
        P(("dp", "ctx")),
        P(("dp", "ctx")),
        P(("dp", "ctx")),
        P(("dp", "ctx")),
        P("dp", "ctx", None),
    )
    out_specs = (
        P("dp", "ctx", None),
        P("dp", "ctx", None),
        P(("dp", "ctx")),
        P(("dp", "ctx")),
        P(("dp", "ctx")),
        P(("dp", "ctx")),
        P(("dp", "ctx")),
        P(("dp", "ctx")),
        P(("dp", "ctx")),
        P(("dp", "ctx")),
    )
    fits = mesh.shape["dp"] == 8 and mesh.shape["ctx"] == 4
    body = chip_local if fits else local
    return jax.shard_map(body, mesh=mesh, in_specs=in_specs, out_specs=out_specs, check_vma=False)
```
